32 devices in a mesh: pb: 8 (over y, x, core), ka: 4 (over z).
Axes of the slice: x: 2, y: 2, z: 4, core: 2. Of those that a mesh axis runs over, the one named last changes fastest.
Arguments:
- layer_input: bfloat16 [16384, 768], P(('pb', 'ka')), may hold values from -24 to 24, as said below
- second_start: int32 [8], P('pb'), may hold values from 1024 to 2048, as said below
- gain_attn: float32 [768], replicated, may hold values from 0.5 to 1.5
- w_qkv: bfloat16 [768, 2304], P('ka'), may hold values from -0.21875 to 0.21875
- w_out: bfloat16 [768, 768], P('ka'), may hold values from -3.5 to 3.5
- gain_mlp: float32 [768], replicated, may hold values from 0.5 to 1.5
- w_up: bfloat16 [768, 3072], P('ka'), may hold values from -0.21875 to 0.21875
- w_down: bfloat16 [3072, 768], P('ka'), may hold values from -0.109375 to 0.109375
- d_output: bfloat16 [16384, 768], P(('pb', 'ka')), may hold values from -6 to 6
Outputs:
- output: bfloat16 [16384, 768], P(('pb', 'ka'))
- d_input: float32 [16384, 768], P(('pb', 'ka'))
- d_gain_attn: float32 [768], P('ka')
- d_w_qkv: float32 [768, 2304], P('ka')
- d_w_out: float32 [768, 768], P('ka')
- d_gain_mlp: float32 [768], P('ka')
- d_w_up: float32 [768, 3072], P('ka')
- d_w_down: float32 [3072, 768], P('ka')
- rms: float32 [4], P('ka')
The draws below stay inside these ranges and needn't reach their ends.
Inputs may be any that keep to these rules, and one draw needn't show every extreme that they name: `layer_input`: every value is finite. `second_start`: exactly half of the 8 groups, drawn from the seed, hold two sequences of 1024 tokens, the second starting at 1024; the others hold one sequence of 2048 tokens and have the value 2048.
All inputs are finite; a program needn't handle non-finite values.
Results may differ from the reference program's by a relative error of at most 0.019.
Values may be sent and summed in bfloat16 or wider, within the bound.
A program may use at most 192 MiB of HBM per device.

```python
import math
from functools import partial
import jax
import jax.numpy as jnp
from jax import lax

D = 768
HEADS = 12
HEAD = 64
FF = 3072
GROUP = 2048
GROUPS = 8
TOKENS = 16384


def draw_layer_input(key, part):
    key_base = jax.random.fold_in(key, 11)
    key_cols = jax.random.fold_in(key, 12)
    position = jnp.arange(TOKENS).astype(jnp.float32)[:, None] / TOKENS
    col_scale = 10.0 ** jax.random.uniform(key_cols, (1, D), jnp.float32, -0.5, 0.5)
    draw_base = jnp.clip(jax.random.normal(key_base, (TOKENS, D), jnp.float32), -5.0, 5.0)
    row_scale = 0.5 + position
    return (draw_base * row_scale * col_scale).astype(jnp.bfloat16)


def draw_second_start(key, part):
    shuffled = jax.random.permutation(jax.random.fold_in(key, 21), GROUPS)
    return jnp.where(shuffled < GROUPS // 2, GROUP // 2, GROUP).astype(jnp.int32)


def steps_of(stream_key, dims, cuts, smallest, high):
    def one(dim, parts):
        steps = jax.random.uniform(jax.random.fold_in(jax.random.fold_in(stream_key, 6), dim), (parts,), jnp.float32, smallest / len(cuts), high / len(cuts))
        return jnp.repeat(jnp.exp(steps), dims[dim] // parts).reshape((-1,) + (1,) * (len(dims) - dim - 1))

    loudness = one(*cuts[0])
    for cut in cuts[1:]:
        loudness = loudness * one(*cut)
    return loudness


def centred(key, shape, scale, limit, shards=(), kind=jnp.bfloat16):
    array = scale * jax.random.normal(key, shape, jnp.float32)
    if shards:
        array = array * steps_of(key, shape, shards, -0.22, 0.18)
    return jnp.clip(array, -limit, limit).astype(kind)


def setup_inputs(seed: int = 0) -> dict:
    arg_keys = jax.random.split(jax.random.key(seed), 10)
    return {
        "layer_input": draw_layer_input(jax.random.fold_in(arg_keys[9], 71), 0),
        "second_start": draw_second_start(jax.random.fold_in(arg_keys[9], 71), 0),
        "gain_attn": jnp.clip(1.0 + 0.1 * jax.random.normal(arg_keys[2], (D,), jnp.float32), 0.5, 1.5),
        "w_qkv": centred(arg_keys[3], (D, 3 * D), D ** -0.5, 0.21875, ((0, 4),)),
        "w_out": centred(arg_keys[4], (D, D), (max(8 * D // GROUP, 1)) ** -0.5, 3.5, ((0, 4),)),
        "gain_mlp": jnp.clip(1.0 + 0.1 * jax.random.normal(arg_keys[5], (D,), jnp.float32), 0.5, 1.5),
        "w_up": centred(arg_keys[6], (D, FF), D ** -0.5, 0.21875, ((0, 4),)),
        "w_down": centred(arg_keys[7], (FF, D), FF ** -0.5, 0.109375, ((0, 4),)),
        "d_output": centred(arg_keys[8], (TOKENS, D), 1.0, 6.0, ((0, 32),)),
    }


@jax.custom_vjp
def low(v):
    return lax.optimization_barrier(v.astype(jnp.bfloat16)).astype(jnp.float32)

@jax.custom_vjp
def low_back(v):
    return v

def low_keep(v):
    return (low(v), None)

def low_pass(kept, grad):
    return (grad,)

def back_keep(v):
    return (v, None)

def back_low(kept, grad):
    return (low(grad),)
low.defvjp(low_keep, low_pass)
low_back.defvjp(back_keep, back_low)
highest = lax.Precision.HIGHEST

def normalize(values):
    center = values - lax.optimization_barrier(jnp.mean(values, axis=1, keepdims=True))
    spread = lax.optimization_barrier(jnp.mean(center * center, axis=1, keepdims=True))
    return center * lax.rsqrt(spread + 1e-05)

def head_attend(allowed, score_scale, pieces):
    queries, keys_head, values_head = pieces
    scores = low_back(jnp.dot(queries, keys_head.T, precision=highest) * score_scale)
    expo = jnp.where(allowed, jnp.cosh(scores), 0.0)
    totals = lax.optimization_barrier(jnp.sum(expo, axis=1, keepdims=True))
    signed = low(jnp.where(allowed, jnp.sinh(scores), 0.0))
    mixed = low_back(jnp.dot(signed, values_head, precision=highest))
    return mixed / totals

def group_layer(weights, pieces):
    inputs, split_at = pieces
    gain_attn, w_qkv, w_out, gain_mlp, w_up, w_down = weights
    group_rows = inputs.shape[0]
    attn_in = low(normalize(inputs) * gain_attn)
    projected = low(low_back(jnp.dot(attn_in, w_qkv, precision=highest)))

    def heads_first(columns):
        return columns.reshape(group_rows, HEADS, HEAD).transpose(1, 0, 2)
    position = jnp.arange(group_rows).astype(jnp.int32)
    seq_side = position >= split_at
    allowed = (position[None, :] <= position[:, None]) & (seq_side[None, :] == seq_side[:, None])
    score_scale = 1.0 / math.sqrt(HEAD)
    mixed = lax.map(jax.checkpoint(partial(head_attend, allowed, score_scale)), (heads_first(projected[:, :D]), heads_first(projected[:, D:2 * D]), heads_first(projected[:, 2 * D:])))
    attn_heads = mixed.transpose(1, 0, 2).reshape(group_rows, D)
    attn_low = low(low_back(attn_heads))
    attn_branch = low_back(jnp.dot(attn_low, w_out, precision=highest))
    middle = inputs + attn_branch
    mlp_in = low(normalize(middle) * gain_mlp)
    up_proj = low_back(jnp.dot(mlp_in, w_up, precision=highest))
    activated = low(jax.nn.gelu(up_proj, approximate=True))
    mlp_branch = jnp.dot(activated, w_down, precision=highest)
    squares = jnp.stack([jnp.sum(inputs * inputs), jnp.sum(attn_branch * attn_branch), jnp.sum(middle * middle), jnp.sum(mlp_branch * mlp_branch)])
    return (middle + mlp_branch, squares)

def reference(layer_input, second_start, gain_attn, w_qkv, w_out, gain_mlp, w_up, w_down, d_output):

    def forward(inputs, gain_one, qkv_weight, out_weight, gain_two, up_weight, down_weight):
        weights = (gain_one, qkv_weight, out_weight, gain_two, up_weight, down_weight)
        results, squares = lax.map(jax.checkpoint(partial(group_layer, weights)), (inputs.reshape(GROUPS, GROUP, D), second_start))
        return (results.reshape(TOKENS, D), lax.optimization_barrier(jnp.sum(squares, axis=0)))
    result, pullback, squares = jax.vjp(forward, layer_input.astype(jnp.float32), gain_attn.astype(jnp.float32), w_qkv.astype(jnp.float32), w_out.astype(jnp.float32), gain_mlp.astype(jnp.float32), w_up.astype(jnp.float32), w_down.astype(jnp.float32), has_aux=True)
    grads = pullback(d_output.astype(jnp.float32))
    rms = jnp.sqrt(squares / (TOKENS * D))
    return (result.astype(jnp.bfloat16), grads[0], grads[1], grads[2], grads[3], grads[4], grads[5], grads[6], rms)
```

```python
import functools
import math

import jax
import jax.numpy as jnp
from jax import lax
from jax.experimental import pallas as pl
from jax.experimental.pallas import tpu as pltpu
from jax.sharding import PartitionSpec as P

D = 768
HEADS = 12
HEAD = 64
SPAN = 4
LOCAL = HEADS // SPAN
WIDE = LOCAL * HEAD
LOG2E = 1.4426950408889634
MESH = pl.DeviceIdType.MESH
BF = jnp.bfloat16
F32 = jnp.float32


def mirror(depth, side):
    return depth + side * (SPAN - 1 - 2 * depth)


def neighbours(pb):
    across_x = pb + 2 - 4 * ((pb // 2) % 2)
    across_y = pb + 4 - 8 * ((pb // 4) % 2)
    across_both = across_x + 4 - 8 * ((across_x // 4) % 2)
    return across_x, across_y, across_both


def sibling_of(pb):
    return pb + 1 - 2 * (pb % 2)


def far(src, dst, send_sem, recv_sem, pb, ka):
    return pltpu.make_async_remote_copy(
        src, dst, send_sem, recv_sem, device_id=(pb, ka), device_id_type=MESH
    )


def greet(peers):
    barrier = pltpu.get_barrier_semaphore()
    for peer in peers:
        pl.semaphore_signal(barrier, 1, device_id=peer, device_id_type=MESH)
    pl.semaphore_wait(barrier, len(peers))


def dot_nt(left, right):
    return lax.dot_general(left, right, (((1,), (1,)), ((), ())), preferred_element_type=F32)


def dot_tn(left, right):
    return lax.dot_general(left, right, (((0,), (0,)), ((), ())), preferred_element_type=F32)


def dot_nn(left, right):
    return jnp.dot(left, right, preferred_element_type=F32)


def fold_lanes(tile):
    out = tile[:, :128]
    for at in range(128, tile.shape[1], 128):
        out = out + tile[:, at : at + 128]
    return out


def forward_kernel(
    xa, wq4, start, wo, wu, wd,
    ohome, xg_out, wq_out, q_out, k_out, v_out, ah_out, tot_out, start_out, wog, wug, wdg,
    xg, wqs, qs, ks, vs, ahs, tots, ob, starts,
    send_x, recv_x, send_q, recv_q, send_s, recv_s, send_o, recv_o,
    send_z, recv_z, send_p, recv_p, send_c, recv_c, own_sem, out_sem,
):
    pb = lax.axis_index("pb")
    ka = lax.axis_index("ka")
    core = pb % 2
    base = pb - core
    side = ka // 2
    depth = mirror(ka, side)
    home_u = mirror(ka, core)
    quarter = 2 * depth + core
    sibling = sibling_of(pb)
    plane = neighbours(pb)
    rows = xa.shape[0]
    half = rows // 2
    rank = (pb // 2) % 4

    column = [((base + k), (ka + i) % SPAN) for i in range(SPAN) for k in range(2)]
    greet(
        [(pb, (ka + i) % SPAN) for i in range(1, SPAN)]
        + [(sibling, (ka + i) % SPAN) for i in range(SPAN)]
        + [(p, ka) for p in plane]
    )

    odd = (((home_u + 1) // 2) % 2) * (1 - home_u // 2)
    goal = mirror(1 - odd, core)
    out_x = [
        far(xa.at[pl.ds(h * half, half)], xg.at[ka, h], send_x.at[h], recv_x.at[ka, h], base + h, goal)
        for h in range(2)
    ]
    for copy in out_x:
        copy.start()

    at_home = core == side

    def near_copies():
        remote = [
            far(xa.at[pl.ds(h * half, half)], xg.at[ka, h], send_x.at[2 + h], recv_x.at[ka, h], sibling, ka)
            for h in range(2)
        ]
        local = [
            pltpu.make_async_copy(xa.at[pl.ds(h * half, half)], xg.at[ka, h], recv_x.at[ka, h])
            for h in range(2)
        ]
        return remote, local

    @pl.when(at_home)
    def _():
        remote, local = near_copies()
        for copy in remote + local:
            copy.start()

    def start_copies():
        out = []
        for n, (d, k) in enumerate(((0, 1), (1, 0), (1, 1))):
            target = base + (core + k) % 2
            out.append(far(start, starts, send_s.at[n], recv_s, target, mirror(d, core)))
        return out

    @pl.when(home_u == 0)
    def _():
        for copy in start_copies():
            copy.start()
        pltpu.make_async_copy(start, starts, recv_s).start()

    out_q = []
    for i in range(1, SPAN):
        z = (ka + i) % SPAN
        zd = mirror(z, z // 2)
        out_q.append(
            far(wq4.at[2 * zd + core], wqs.at[ka], send_q.at[i - 1], recv_q.at[i - 1], pb, z)
        )
    for copy in out_q:
        copy.start()
    own_q = pltpu.make_async_copy(wq4.at[quarter], wqs.at[ka], own_sem.at[0])
    own_q.start()
    own_w = [
        pltpu.make_async_copy(src, dst.at[ka], own_sem.at[1 + n])
        for n, (src, dst) in enumerate(((wo, wog), (wu, wug), (wd, wdg)))
    ]
    for copy in own_w:
        copy.start()

    spread = []
    for i in range(3):
        u = (1 - depth) if i == 0 else i + 1
        b = mirror(u, side)
        far(xg.at[b, core], xg.at[b, core], send_x.at[4], recv_x.at[b, core], pb, ka).wait_recv()
        copy = far(xg.at[b, core], xg.at[b, core], send_x.at[4 + i], recv_x.at[b, core], sibling, ka)
        copy.start()
        spread.append(copy)
        if i >= 1:
            onward = far(
                xg.at[b, core], xg.at[b, core], send_x.at[6 + i], recv_x.at[b, core], pb, mirror(0, side)
            )

            @pl.when(depth == 1)
            def _():
                onward.start()

            spread.append(onward)
    b_near = ka
    for h in range(2):
        far(xg.at[b_near, h], xg.at[b_near, h], send_x.at[4], recv_x.at[b_near, h], pb, ka).wait_recv()
    for i in range(3):
        u = (1 - depth) if i == 0 else i + 1
        b = mirror(u, side)
        far(xg.at[b, 1 - core], xg.at[b, 1 - core], send_x.at[4], recv_x.at[b, 1 - core], pb, ka).wait_recv()

    parts = (
        (wo, wog, wo.shape[0] // 4, wo.shape[1] // 2),
        (wu, wug, wu.shape[0] // 4, wu.shape[1] // 2),
        (wd, wdg, wd.shape[0] // 4, wd.shape[1] // 2),
    )

    def piece(ref, n):
        _, _, r, c = parts[n]
        return ref.at[pl.ds(pl.multiple_of(rank * r, 16), r), pl.ds(pl.multiple_of(core * c, 128), c)]

    def strip(ref, n):
        _, _, _, c = parts[n]
        return ref.at[:, pl.ds(pl.multiple_of(core * c, 128), c)]

    def strip_other(ref, n):
        _, _, _, c = parts[n]
        return ref.at[:, pl.ds(pl.multiple_of((1 - core) * c, 128), c)]

    along_z = []
    for i in range(1, SPAN):
        z = (ka + i) % SPAN
        for n, (src, dst, _, _) in enumerate(parts):
            along_z.append(
                far(piece(src, n), piece(dst.at[ka], n), send_z.at[n, i - 1], recv_z.at[n, i - 1], pb, z)
            )
    for copy in along_z:
        copy.start()

    for i in range(1, SPAN):
        far(wq4.at[quarter], wqs.at[(ka - i) % SPAN], send_q.at[0], recv_q.at[i - 1], pb, ka).wait_recv()
    own_q.wait()
    pltpu.make_async_copy(start, starts, recv_s).wait()

    def project(b, carry):
        xb = xg[b].reshape(rows, D)
        at = pl.multiple_of(b * rows, rows)
        for dst, col in ((qs, 0), (ks, WIDE), (vs, 2 * WIDE)):
            w = wqs[:, :, col : col + WIDE].reshape(D, WIDE)
            out = dot_nn(xb, w).astype(BF)
            for h in range(LOCAL):
                dst[h, pl.ds(at, rows), :] = out[:, h * HEAD : (h + 1) * HEAD]
        return carry

    lax.fori_loop(0, SPAN, project, 0)

    in_plane = []

    def begin_plane():
        for i in range(1, SPAN):
            z = (ka - i) % SPAN
            for n, (src, dst, _, _) in enumerate(parts):
                far(piece(src, n), piece(dst.at[z], n), send_z.at[n, 0], recv_z.at[n, i - 1], pb, ka).wait_recv()
                for m, p in enumerate(plane):
                    copy = far(
                        piece(dst.at[z], n), piece(dst.at[z], n),
                        send_p.at[n, i - 1, m], recv_p.at[n, i - 1, m], p, ka,
                    )
                    copy.start()
                    in_plane.append(copy)

    across = []

    def begin_across():
        for i in range(1, SPAN):
            z = (ka - i) % SPAN
            for n, (src, dst, _, _) in enumerate(parts):
                for m in range(3):
                    far(
                        piece(dst.at[z], n), piece(dst.at[z], n),
                        send_p.at[n, i - 1, m], recv_p.at[n, i - 1, m], pb, ka,
                    ).wait_recv()
                copy = far(
                    strip(dst.at[z], n), strip(dst.at[z], n), send_c.at[n, i - 1], recv_c.at[n, i - 1], sibling, ka
                )
                copy.start()
                across.append(copy)

    scale = LOG2E / math.sqrt(HEAD)
    one = starts[0:1, 0:1] > (SPAN // 2) * rows + 0.5
    sub = 256

    def tile_terms(q, at, width):
        s = dot_nt(q, ks_at(at, width)) * scale
        return jnp.exp2(s - 1.0), jnp.exp2(-s - 1.0)

    def attend(h, carry):
        def ks_at(at, width):
            return ks[h, pl.ds(at, width), :]

        def full(q, at, acc, tot):
            s = dot_nt(q, ks[h, pl.ds(at, rows), :]) * scale
            up, down = jnp.exp2(s - 1.0), jnp.exp2(-s - 1.0)
            tot = tot + fold_lanes(up + down)
            acc = acc + dot_nn((up - down).astype(BF), vs[h, pl.ds(at, rows), :])
            return acc, tot

        return carry

    def attend_block(b):
        for h in range(LOCAL):
            for part in range(rows // sub):
                row0 = b * rows + part * sub
                q = qs[h, row0 : row0 + sub, :]

                def full(kb, state, q=q, h=h):
                    acc, tot = state
                    at = pl.multiple_of(kb * rows, rows)
                    s = dot_nt(q, ks[h, pl.ds(at, rows), :]) * scale
                    up, down = jnp.exp2(s - 1.0), jnp.exp2(-s - 1.0)
                    tot = tot + fold_lanes(up + down)
                    acc = acc + dot_nn((up - down).astype(BF), vs[h, pl.ds(at, rows), :])
                    return acc, tot

                state = (jnp.zeros((sub, HEAD), F32), jnp.zeros((sub, 128), F32))
                if b >= SPAN // 2:
                    acc, tot = lax.fori_loop(0, SPAN // 2, full, state)
                    state = (jnp.where(one, acc, 0.0), jnp.where(one, tot, 0.0))
                    state = lax.fori_loop(SPAN // 2, b, full, state)
                else:
                    state = lax.fori_loop(0, b, full, state)
                acc, tot = state
                width = (part + 1) * sub
                s = dot_nt(q, ks[h, b * rows : b * rows + width, :]) * scale
                seen = (
                    lax.broadcasted_iota(jnp.int32, (sub, width), 0) + part * sub
                    >= lax.broadcasted_iota(jnp.int32, (sub, width), 1)
                )
                up = jnp.where(seen, jnp.exp2(s - 1.0), 0.0)
                down = jnp.where(seen, jnp.exp2(-s - 1.0), 0.0)
                tot = tot + fold_lanes(up + down)
                acc = acc + dot_nn((up - down).astype(BF), vs[h, b * rows : b * rows + width, :])
                total = jnp.sum(tot, axis=1, keepdims=True)
                heads = acc / total
                ahs[h, row0 : row0 + sub, :] = heads
                tots[h, row0 : row0 + sub, :] = jnp.broadcast_to(total, (sub, HEAD))

    send_back = []
    for b in range(SPAN):
        attend_block(b)
        joined = jnp.concatenate(
            [ahs[h, b * rows : (b + 1) * rows, :] for h in range(LOCAL)], axis=1
        )
        ob[b] = joined.astype(BF)
        if b == 0:
            begin_plane()
        if b == 2:
            begin_across()
        remote = far(ob.at[b], ohome.at[quarter], send_o.at[b], recv_o.at[quarter], base + side, b)
        mine = (core == side) & (ka == b)

        @pl.when(jnp.logical_not(mine))
        def _():
            remote.start()

        @pl.when(mine)
        def _():
            pltpu.make_async_copy(ob.at[b], ohome.at[quarter], recv_o.at[quarter]).start()

        send_back.append((mine, remote))

    saves = [
        pltpu.make_async_copy(src, dst, out_sem.at[n])
        for n, (src, dst) in enumerate(
            (
                (xg, xg_out), (wqs, wq_out), (qs, q_out), (ks, k_out), (vs, v_out),
                (ahs, ah_out), (tots, tot_out), (starts, start_out),
            )
        )
    ]
    for copy in saves:
        copy.start()

    for i in range(1, SPAN):
        z = (ka - i) % SPAN
        for n, (src, dst, _, _) in enumerate(parts):
            far(
                strip_other(dst.at[z], n), strip_other(dst.at[z], n),
                send_c.at[n, 0], recv_c.at[n, i - 1], pb, ka,
            ).wait_recv()
    for n in range(SPAN):
        far(ob.at[0], ohome.at[n], send_o.at[0], recv_o.at[n], pb, ka).wait_recv()
    for copy in saves + own_w:
        copy.wait()
    for copy in out_x + out_q + along_z + in_plane + across:
        copy.wait_send()
    for n in range(3):
        spread[(0, 1, 3)[n]].wait_send()

    @pl.when(depth == 1)
    def _():
        spread[2].wait_send()
        spread[4].wait_send()

    @pl.when(at_home)
    def _():
        remote, _ = near_copies()
        for copy in remote:
            copy.wait_send()

    @pl.when(home_u == 0)
    def _():
        for copy in start_copies():
            copy.wait_send()

    for mine, remote in send_back:

        @pl.when(jnp.logical_not(mine))
        def _():
            remote.wait_send()


def forward_call(xa, wq4, start, wo, wu, wd):
    rows = xa.shape[0]
    group = rows * SPAN
    anyspace = pl.BlockSpec(memory_space=pl.ANY)
    vmem = pl.BlockSpec(memory_space=pltpu.VMEM)
    shape = jax.ShapeDtypeStruct
    dma = pltpu.SemaphoreType.DMA
    outs = (
        shape((SPAN, rows, WIDE), BF),
        shape((SPAN, 2, rows // 2, D), BF),
        shape((SPAN, D // SPAN, 3 * WIDE), BF),
        shape((LOCAL, group, HEAD), BF),
        shape((LOCAL, group, HEAD), BF),
        shape((LOCAL, group, HEAD), BF),
        shape((LOCAL, group, HEAD), F32),
        shape((LOCAL, group, HEAD), F32),
        shape((8, 128), F32),
        shape((SPAN,) + wo.shape, BF),
        shape((SPAN,) + wu.shape, BF),
        shape((SPAN,) + wd.shape, BF),
    )
    vm = pltpu.VMEM
    scratch = [
        vm((SPAN, 2, rows // 2, D), BF),
        vm((SPAN, D // SPAN, 3 * WIDE), BF),
        vm((LOCAL, group, HEAD), BF),
        vm((LOCAL, group, HEAD), BF),
        vm((LOCAL, group, HEAD), BF),
        vm((LOCAL, group, HEAD), F32),
        vm((LOCAL, group, HEAD), F32),
        vm((SPAN, rows, WIDE), BF),
        vm((8, 128), F32),
        dma((9,)), dma((SPAN, 2)), dma((3,)), dma((3,)), dma((3,)), dma, dma((SPAN,)), dma((SPAN,)),
        dma((3, 3)), dma((3, 3)), dma((3, 3, 3)), dma((3, 3, 3)), dma((3, 3)), dma((3, 3)), dma((4,)), dma((8,)),
    ]
    return pl.pallas_call(
        forward_kernel,
        out_shape=outs,
        in_specs=[vmem, anyspace, vmem, anyspace, anyspace, anyspace],
        out_specs=(anyspace,) * len(outs),
        scratch_shapes=scratch,
        compiler_params=pltpu.CompilerParams(
            collective_id=0, has_side_effects=True, vmem_limit_bytes=56 << 20
        ),
        name="forward_attention",
    )(xa, wq4, start, wo, wu, wd)


def normalize(values):
    center = values - jnp.mean(values, axis=1, keepdims=True)
    spread = jnp.mean(center * center, axis=1, keepdims=True)
    return center * lax.rsqrt(spread + 1e-05)


def norm_gain(values, gain_vec):
    return normalize(values) * gain_vec


def gelu_tanh(values):
    return jax.nn.gelu(values, approximate=True)


def contract_rows(left, right):
    return lax.dot_general(
        left, right, (((0,), (0,)), ((), ())), preferred_element_type=jnp.float32
    )


def contract_cols(left, right):
    return lax.dot_general(
        left, right, (((1,), (1,)), ((), ())), preferred_element_type=jnp.float32
    )


def body(layer_input, second_start, gain_attn, w_qkv, w_out, gain_mlp, w_up, w_down, d_output):
    row_count = layer_input.shape[0]
    kv_index = lax.axis_index("ka")
    kv_count = lax.axis_size("ka")
    group_rows = row_count * kv_count
    block_rows = min(512, group_rows)
    block_count = group_rows // block_rows
    score_scale = 1.0 / math.sqrt(HEAD)
    split_at = second_start[0]
    full_qkv = lax.all_gather(w_qkv, "ka", axis=0, tiled=True)
    inputs32 = layer_input.astype(jnp.float32)
    attn_in = (normalize(inputs32) * gain_attn).astype(jnp.bfloat16)
    wq4 = w_qkv.reshape(D // SPAN, 3, SPAN, WIDE).transpose(2, 0, 1, 3).reshape(SPAN, D // SPAN, 3 * WIDE)
    start = jnp.full((8, 128), split_at, F32)
    got = forward_call(attn_in, wq4, start, w_out, w_up, w_down)
    full_out = got[9].reshape(D, D)
    full_up = got[10].reshape(D, -1)
    full_down = got[11].reshape(-1, D)
    projected = jnp.dot(attn_in, full_qkv, preferred_element_type=jnp.float32).astype(jnp.bfloat16)
    keys_own = projected[:, D : 2 * D].reshape(row_count, HEADS, HEAD)
    values_own = projected[:, 2 * D :].reshape(row_count, HEADS, HEAD)
    block_ids = jnp.arange(block_count)
    own_pos = kv_index * row_count + jnp.arange(row_count)

    def pair_scores(query_blk, query_pos, key_blk, key_pos):
        query_side = query_pos >= split_at
        key_side = key_pos >= split_at
        allowed = (key_pos[None, :] <= query_pos[:, None]) & (
            key_side[None, :] == query_side[:, None]
        )
        scores = (
            jnp.einsum("qhd,khd->hqk", query_blk, key_blk, preferred_element_type=jnp.float32)
            * score_scale
        )
        expo = jnp.where(allowed[None], jnp.cosh(scores), 0.0)
        sine = jnp.where(allowed[None], jnp.sinh(scores), 0.0)
        signed = sine.astype(jnp.bfloat16)
        return (sine, expo, signed)

    def block_scores(query_blk, block_idx):
        query_pos = block_idx * block_rows + jnp.arange(block_rows)
        return pair_scores(query_blk, query_pos, keys_own, own_pos)

    queries_all = lax.all_gather(projected[:, :D], "ka", axis=0, tiled=True)
    query_blocks = queries_all.reshape(block_count, block_rows, HEADS, HEAD)

    def forward_block(pieces):
        query_blk, block_idx = pieces
        sine, expo, signed = block_scores(query_blk, block_idx)
        partial_blk = jnp.einsum(
            "hqk,khd->qhd", signed, values_own, preferred_element_type=jnp.float32
        )
        return (partial_blk.reshape(block_rows, D), jnp.sum(expo, axis=2))

    partial_out, partial_sums = lax.map(forward_block, (query_blocks, block_ids))
    partial_out = partial_out.reshape(group_rows, D)
    partial_sums = jnp.transpose(partial_sums, (1, 0, 2)).reshape(HEADS, group_rows)
    sums_all = lax.psum(partial_sums.astype(jnp.bfloat16), "ka").astype(jnp.float32)
    own_out = lax.psum_scatter(
        partial_out.astype(jnp.bfloat16), "ka", scatter_dimension=0, tiled=True
    ).astype(jnp.float32)
    own_sums = lax.dynamic_slice_in_dim(sums_all, kv_index * row_count, row_count, 1)
    row_totals = own_sums.T[:, :, None]
    attn_heads = own_out.reshape(row_count, HEADS, HEAD) / row_totals
    attn_low = got[0].transpose(1, 0, 2).reshape(row_count, D)
    attn_branch = jnp.dot(attn_low, full_out, preferred_element_type=jnp.float32)
    middle = inputs32 + attn_branch
    mlp_in = (normalize(middle) * gain_mlp).astype(jnp.bfloat16)
    up_proj = jnp.dot(mlp_in, full_up, preferred_element_type=jnp.float32)
    activated = gelu_tanh(up_proj).astype(jnp.bfloat16)
    mlp_branch = jnp.dot(activated, full_down, preferred_element_type=jnp.float32)
    output = (middle + mlp_branch).astype(jnp.bfloat16)
    squares = jnp.stack(
        [
            jnp.sum(inputs32 * inputs32),
            jnp.sum(attn_branch * attn_branch),
            jnp.sum(middle * middle),
            jnp.sum(mlp_branch * mlp_branch),
        ]
    )
    d_act = contract_cols(d_output, full_down)
    d_w_down = contract_rows(activated, d_output)
    gelu_back = jax.vjp(gelu_tanh, up_proj)[1]
    d_up = gelu_back(d_act)[0].astype(jnp.bfloat16)
    d_w_up = contract_rows(mlp_in, d_up)
    d_mlp_in = contract_cols(d_up, full_up)
    norm_back_two = jax.vjp(norm_gain, middle, gain_mlp)[1]
    d_middle_norm, d_gain_mlp = norm_back_two(d_mlp_in)
    d_middle = d_output.astype(jnp.float32) + d_middle_norm
    g_middle = d_middle.astype(jnp.bfloat16)
    d_w_out = contract_rows(attn_low, g_middle)
    d_attn = contract_cols(g_middle, full_out).astype(jnp.bfloat16)
    d_attn_heads = d_attn.astype(jnp.float32).reshape(row_count, HEADS, HEAD)
    d_mixed = (d_attn_heads / row_totals).reshape(row_count, D).astype(jnp.bfloat16)
    row_terms = (jnp.sum(d_attn_heads * attn_heads, axis=2) / own_sums.T).T
    mixed_all, terms_all = (
        lax.all_gather(d_mixed, "ka", axis=0, tiled=True),
        lax.all_gather(row_terms.astype(jnp.bfloat16), "ka", axis=1, tiled=True).astype(
            row_terms.dtype
        ),
    )
    grad_blocks = mixed_all.reshape(block_count, block_rows, HEADS, HEAD)
    term_blocks = jnp.transpose(terms_all.reshape(HEADS, block_count, block_rows), (1, 0, 2))

    def backward_block(carry, pieces):
        key_acc, value_acc = carry
        query_blk, grad_blk, term_blk, block_idx = pieces
        sine, expo, signed = block_scores(query_blk, block_idx)
        d_signed = jnp.einsum(
            "qhd,khd->hqk", grad_blk, values_own, preferred_element_type=jnp.float32
        )
        d_scores = (expo * d_signed - sine * term_blk[:, :, None]).astype(jnp.bfloat16)
        d_query = (
            jnp.einsum("hqk,khd->qhd", d_scores, keys_own, preferred_element_type=jnp.float32)
            * score_scale
        )
        key_acc = (
            key_acc
            + jnp.einsum("hqk,qhd->khd", d_scores, query_blk, preferred_element_type=jnp.float32)
            * score_scale
        )
        value_acc = value_acc + jnp.einsum(
            "hqk,qhd->khd", signed, grad_blk, preferred_element_type=jnp.float32
        )
        return ((key_acc, value_acc), d_query.reshape(block_rows, D))

    zero_acc = jnp.zeros((row_count, HEADS, HEAD), jnp.float32)
    (d_keys, d_values), query_parts = lax.scan(
        backward_block, (zero_acc, zero_acc), (query_blocks, grad_blocks, term_blocks, block_ids)
    )
    d_queries = lax.psum_scatter(
        query_parts.reshape(group_rows, D).astype(jnp.bfloat16),
        "ka",
        scatter_dimension=0,
        tiled=True,
    ).astype(jnp.float32)
    d_projected = jnp.concatenate(
        [d_queries, d_keys.reshape(row_count, D), d_values.reshape(row_count, D)], axis=1
    ).astype(jnp.bfloat16)
    d_w_qkv = contract_rows(attn_in, d_projected)
    d_attn_in = contract_cols(d_projected, full_qkv)
    norm_back_one = jax.vjp(norm_gain, inputs32, gain_attn)[1]
    d_input_norm, d_gain_attn = norm_back_one(d_attn_in)
    d_input = d_middle + d_input_norm
    all_totals = lax.psum(
        (
            lax.psum_scatter(
                d_gain_attn.astype(jnp.bfloat16), "ka", scatter_dimension=0, tiled=True
            ).astype(jnp.float32),
            lax.psum_scatter(
                d_w_qkv.astype(jnp.bfloat16), "ka", scatter_dimension=0, tiled=True
            ).astype(jnp.float32),
            lax.psum_scatter(
                d_w_out.astype(jnp.bfloat16), "ka", scatter_dimension=0, tiled=True
            ).astype(jnp.float32),
            lax.psum_scatter(
                d_gain_mlp.astype(jnp.bfloat16), "ka", scatter_dimension=0, tiled=True
            ).astype(jnp.float32),
            lax.psum_scatter(
                d_w_up.astype(jnp.bfloat16), "ka", scatter_dimension=0, tiled=True
            ).astype(jnp.float32),
            lax.psum_scatter(
                d_w_down.astype(jnp.bfloat16), "ka", scatter_dimension=0, tiled=True
            ).astype(jnp.float32),
            lax.psum_scatter(
                squares.astype(jnp.bfloat16), "ka", scatter_dimension=0, tiled=True
            ).astype(jnp.float32),
        ),
        "pb",
    )
    total_gain_attn, total_qkv, total_out, total_gain_mlp, total_up, total_down, total_squares = (
        all_totals
    )
    entry_count = row_count * kv_count * lax.axis_size("pb") * D
    rms = jnp.sqrt(total_squares / entry_count)
    return (
        output,
        d_input,
        total_gain_attn,
        total_qkv,
        total_out,
        total_gain_mlp,
        total_up,
        total_down,
        rms,
    )


def solution(mesh):
    placed = (
        P(("pb", "ka"), None),
        P("pb"),
        P(),
        P("ka", None),
        P("ka", None),
        P(),
        P("ka", None),
        P("ka", None),
        P(("pb", "ka"), None),
    )
    return jax.shard_map(
        body,
        mesh=mesh,
        in_specs=placed,
        out_specs=(
            P(("pb", "ka"), None),
            P(("pb", "ka"), None),
            P("ka"),
            P("ka", None),
            P("ka", None),
            P("ka"),
            P("ka", None),
            P("ka", None),
            P("ka"),
        ),
        check_vma=False,
    )
```

```python
import functools
import math

import jax
import jax.numpy as jnp
from jax import lax
from jax.experimental import pallas as pl
from jax.experimental.pallas import tpu as pltpu
from jax.sharding import PartitionSpec as P

D = 768
HEADS = 12
HEAD = 64
SPAN = 4
LOCAL = HEADS // SPAN
WIDE = LOCAL * HEAD
LOG2E = 1.4426950408889634
MESH = pl.DeviceIdType.MESH
BF = jnp.bfloat16
F32 = jnp.float32


def mirror(depth, side):
    return depth + side * (SPAN - 1 - 2 * depth)


def neighbours(pb):
    across_x = pb + 2 - 4 * ((pb // 2) % 2)
    across_y = pb + 4 - 8 * ((pb // 4) % 2)
    across_both = across_x + 4 - 8 * ((across_x // 4) % 2)
    return across_x, across_y, across_both


def sibling_of(pb):
    return pb + 1 - 2 * (pb % 2)


def far(src, dst, send_sem, recv_sem, pb, ka):
    return pltpu.make_async_remote_copy(
        src, dst, send_sem, recv_sem, device_id=(pb, ka), device_id_type=MESH
    )


def greet(peers):
    barrier = pltpu.get_barrier_semaphore()
    for peer in peers:
        pl.semaphore_signal(barrier, 1, device_id=peer, device_id_type=MESH)
    pl.semaphore_wait(barrier, len(peers))


def dot_nt(left, right):
    return lax.dot_general(left, right, (((1,), (1,)), ((), ())), preferred_element_type=F32)


def dot_tn(left, right):
    return lax.dot_general(left, right, (((0,), (0,)), ((), ())), preferred_element_type=F32)


def dot_nn(left, right):
    return jnp.dot(left, right, preferred_element_type=F32)


def fold_lanes(tile):
    out = tile[:, :128]
    for at in range(128, tile.shape[1], 128):
        out = out + tile[:, at : at + 128]
    return out


def forward_kernel(
    xa, wq4, start, wo, wu, wd,
    ohome, xg_out, wq_out, q_out, k_out, v_out, ah_out, tot_out, start_out, wog, wug, wdg,
    xg, wqs, qs, ks, vs, ahs, tots, ob, starts,
    send_x, recv_x, send_q, recv_q, send_s, recv_s, send_o, recv_o,
    send_z, recv_z, send_p, recv_p, send_c, recv_c, own_sem, out_sem,
):
    pb = lax.axis_index("pb")
    ka = lax.axis_index("ka")
    core = pb % 2
    base = pb - core
    side = ka // 2
    depth = mirror(ka, side)
    home_u = mirror(ka, core)
    quarter = 2 * depth + core
    sibling = sibling_of(pb)
    plane = neighbours(pb)
    rows = xa.shape[0]
    half = rows // 2
    rank = (pb // 2) % 4

    greet(
        [(pb, (ka + i) % SPAN) for i in range(1, SPAN)]
        + [(sibling, (ka + i) % SPAN) for i in range(SPAN)]
        + [(p, ka) for p in plane]
    )

    odd = (((home_u + 1) // 2) % 2) * (1 - home_u // 2)
    goal = mirror(1 - odd, core)
    out_x = [
        far(xa.at[pl.ds(h * half, half)], xg.at[ka, h], send_x.at[h], recv_x.at[ka, h], base + h, goal)
        for h in range(2)
    ]
    for copy in out_x:
        copy.start()

    at_home = core == side

    def near_copies():
        remote = [
            far(xa.at[pl.ds(h * half, half)], xg.at[ka, h], send_x.at[2 + h], recv_x.at[ka, h], sibling, ka)
            for h in range(2)
        ]
        local = [
            pltpu.make_async_copy(xa.at[pl.ds(h * half, half)], xg.at[ka, h], recv_x.at[ka, h])
            for h in range(2)
        ]
        return remote, local

    @pl.when(at_home)
    def _():
        remote, local = near_copies()
        for copy in remote + local:
            copy.start()

    def start_copies():
        out = []
        for n, (d, k) in enumerate(((0, 1), (1, 0), (1, 1))):
            target = base + (core + k) % 2
            out.append(far(start, starts, send_s.at[n], recv_s, target, mirror(d, core)))
        return out

    @pl.when(home_u == 0)
    def _():
        for copy in start_copies():
            copy.start()
        pltpu.make_async_copy(start, starts, recv_s).start()

    out_q = []
    for i in range(1, SPAN):
        z = (ka + i) % SPAN
        zd = mirror(z, z // 2)
        out_q.append(
            far(wq4.at[2 * zd + core], wqs.at[ka], send_q.at[i - 1], recv_q.at[i - 1], pb, z)
        )
    for copy in out_q:
        copy.start()
    own_q = pltpu.make_async_copy(wq4.at[quarter], wqs.at[ka], own_sem.at[0])
    own_q.start()
    own_w = [
        pltpu.make_async_copy(src, dst.at[ka], own_sem.at[1 + n])
        for n, (src, dst) in enumerate(((wo, wog), (wu, wug), (wd, wdg)))
    ]
    for copy in own_w:
        copy.start()

    spread = []
    for i in range(3):
        u = (1 - depth) if i == 0 else i + 1
        b = mirror(u, side)
        far(xg.at[b, core], xg.at[b, core], send_x.at[4], recv_x.at[b, core], pb, ka).wait_recv()
        copy = far(xg.at[b, core], xg.at[b, core], send_x.at[4 + i], recv_x.at[b, core], sibling, ka)
        copy.start()
        spread.append(copy)
        if i >= 1:
            onward = far(
                xg.at[b, core], xg.at[b, core], send_x.at[6 + i], recv_x.at[b, core], pb, mirror(0, side)
            )

            @pl.when(depth == 1)
            def _():
                onward.start()

            spread.append(onward)
    b_near = ka
    for h in range(2):
        far(xg.at[b_near, h], xg.at[b_near, h], send_x.at[4], recv_x.at[b_near, h], pb, ka).wait_recv()
    for i in range(3):
        u = (1 - depth) if i == 0 else i + 1
        b = mirror(u, side)
        far(xg.at[b, 1 - core], xg.at[b, 1 - core], send_x.at[4], recv_x.at[b, 1 - core], pb, ka).wait_recv()

    parts = (
        (wo, wog, wo.shape[0] // 4, wo.shape[1] // 2),
        (wu, wug, wu.shape[0] // 4, wu.shape[1] // 2),
        (wd, wdg, wd.shape[0] // 4, wd.shape[1] // 2),
    )

    def piece(ref, n):
        _, _, r, c = parts[n]
        return ref.at[pl.ds(pl.multiple_of(rank * r, 16), r), pl.ds(pl.multiple_of(core * c, 128), c)]

    def strip(ref, n):
        _, _, _, c = parts[n]
        return ref.at[:, pl.ds(pl.multiple_of(core * c, 128), c)]

    def strip_other(ref, n):
        _, _, _, c = parts[n]
        return ref.at[:, pl.ds(pl.multiple_of((1 - core) * c, 128), c)]

    along_z = []
    for i in range(1, SPAN):
        z = (ka + i) % SPAN
        for n, (src, dst, _, _) in enumerate(parts):
            along_z.append(
                far(piece(src, n), piece(dst.at[ka], n), send_z.at[n, i - 1], recv_z.at[n, i - 1], pb, z)
            )
    for copy in along_z:
        copy.start()

    for i in range(1, SPAN):
        far(wq4.at[quarter], wqs.at[(ka - i) % SPAN], send_q.at[0], recv_q.at[i - 1], pb, ka).wait_recv()
    own_q.wait()
    pltpu.make_async_copy(start, starts, recv_s).wait()

    def project(b, carry):
        xb = xg[b].reshape(rows, D)
        at = pl.multiple_of(b * rows, rows)
        for dst, col in ((qs, 0), (ks, WIDE), (vs, 2 * WIDE)):
            w = wqs[:, :, col : col + WIDE].reshape(D, WIDE)
            out = dot_nn(xb, w).astype(BF)
            for h in range(LOCAL):
                dst[h, pl.ds(at, rows), :] = out[:, h * HEAD : (h + 1) * HEAD]
        return carry

    lax.fori_loop(0, SPAN, project, 0)

    in_plane = []

    def begin_plane():
        for i in range(1, SPAN):
            z = (ka - i) % SPAN
            for n, (src, dst, _, _) in enumerate(parts):
                far(piece(src, n), piece(dst.at[z], n), send_z.at[n, 0], recv_z.at[n, i - 1], pb, ka).wait_recv()
                for m, p in enumerate(plane):
                    copy = far(
                        piece(dst.at[z], n), piece(dst.at[z], n),
                        send_p.at[n, i - 1, m], recv_p.at[n, i - 1, m], p, ka,
                    )
                    copy.start()
                    in_plane.append(copy)

    across = []

    def begin_across():
        for i in range(1, SPAN):
            z = (ka - i) % SPAN
            for n, (src, dst, _, _) in enumerate(parts):
                for m in range(3):
                    far(
                        piece(dst.at[z], n), piece(dst.at[z], n),
                        send_p.at[n, i - 1, m], recv_p.at[n, i - 1, m], pb, ka,
                    ).wait_recv()
                copy = far(
                    strip(dst.at[z], n), strip(dst.at[z], n), send_c.at[n, i - 1], recv_c.at[n, i - 1], sibling, ka
                )
                copy.start()
                across.append(copy)

    scale = LOG2E / math.sqrt(HEAD)
    one = starts[0:1, 0:1] > (SPAN // 2) * rows + 0.5
    sub = 256

    def attend_block(b):
        for h in range(LOCAL):
            for part in range(rows // sub):
                row0 = b * rows + part * sub
                q = qs[h, row0 : row0 + sub, :]

                def full(kb, state, q=q, h=h):
                    acc, tot = state
                    at = pl.multiple_of(kb * rows, rows)
                    s = dot_nt(q, ks[h, pl.ds(at, rows), :]) * scale
                    up, down = jnp.exp2(s - 1.0), jnp.exp2(-s - 1.0)
                    tot = tot + fold_lanes(up + down)
                    acc = acc + dot_nn((up - down).astype(BF), vs[h, pl.ds(at, rows), :])
                    return acc, tot

                state = (jnp.zeros((sub, HEAD), F32), jnp.zeros((sub, 128), F32))
                if b >= SPAN // 2:
                    acc, tot = lax.fori_loop(0, SPAN // 2, full, state)
                    state = (jnp.where(one, acc, 0.0), jnp.where(one, tot, 0.0))
                    state = lax.fori_loop(SPAN // 2, b, full, state)
                else:
                    state = lax.fori_loop(0, b, full, state)
                acc, tot = state
                width = (part + 1) * sub
                s = dot_nt(q, ks[h, b * rows : b * rows + width, :]) * scale
                seen = (
                    lax.broadcasted_iota(jnp.int32, (sub, width), 0) + part * sub
                    >= lax.broadcasted_iota(jnp.int32, (sub, width), 1)
                )
                up = jnp.where(seen, jnp.exp2(s - 1.0), 0.0)
                down = jnp.where(seen, jnp.exp2(-s - 1.0), 0.0)
                tot = tot + fold_lanes(up + down)
                acc = acc + dot_nn((up - down).astype(BF), vs[h, b * rows : b * rows + width, :])
                total = jnp.sum(tot, axis=1, keepdims=True)
                heads = acc / total
                ahs[h, row0 : row0 + sub, :] = heads
                tots[h, row0 : row0 + sub, :] = jnp.broadcast_to(total, (sub, HEAD))

    send_back = []
    for b in range(SPAN):
        attend_block(b)
        joined = jnp.concatenate(
            [ahs[h, b * rows : (b + 1) * rows, :] for h in range(LOCAL)], axis=1
        )
        ob[b] = joined.astype(BF)
        if b == 0:
            begin_plane()
        if b == 2:
            begin_across()
        remote = far(ob.at[b], ohome.at[quarter], send_o.at[b], recv_o.at[quarter], base + side, b)
        mine = (core == side) & (ka == b)

        @pl.when(jnp.logical_not(mine))
        def _():
            remote.start()

        @pl.when(mine)
        def _():
            pltpu.make_async_copy(ob.at[b], ohome.at[quarter], recv_o.at[quarter]).start()

        send_back.append((mine, remote))

    saves = [
        pltpu.make_async_copy(src, dst, out_sem.at[n])
        for n, (src, dst) in enumerate(
            (
                (xg, xg_out), (wqs, wq_out), (qs, q_out), (ks, k_out), (vs, v_out),
                (ahs, ah_out), (tots, tot_out), (starts, start_out),
            )
        )
    ]
    for copy in saves:
        copy.start()

    for i in range(1, SPAN):
        z = (ka - i) % SPAN
        for n, (src, dst, _, _) in enumerate(parts):
            far(
                strip_other(dst.at[z], n), strip_other(dst.at[z], n),
                send_c.at[n, 0], recv_c.at[n, i - 1], pb, ka,
            ).wait_recv()
    for n in range(SPAN):
        far(ob.at[0], ohome.at[n], send_o.at[0], recv_o.at[n], pb, ka).wait_recv()
    for copy in saves + own_w:
        copy.wait()
    for copy in out_x + out_q + along_z + in_plane + across:
        copy.wait_send()
    for n in range(3):
        spread[(0, 1, 3)[n]].wait_send()

    @pl.when(depth == 1)
    def _():
        spread[2].wait_send()
        spread[4].wait_send()

    @pl.when(at_home)
    def _():
        remote, _ = near_copies()
        for copy in remote:
            copy.wait_send()

    @pl.when(home_u == 0)
    def _():
        for copy in start_copies():
            copy.wait_send()

    for mine, remote in send_back:

        @pl.when(jnp.logical_not(mine))
        def _():
            remote.wait_send()


def forward_call(xa, wq4, start, wo, wu, wd):
    rows = xa.shape[0]
    group = rows * SPAN
    anyspace = pl.BlockSpec(memory_space=pl.ANY)
    vmem = pl.BlockSpec(memory_space=pltpu.VMEM)
    shape = jax.ShapeDtypeStruct
    dma = pltpu.SemaphoreType.DMA
    outs = (
        shape((SPAN, rows, WIDE), BF),
        shape((SPAN, 2, rows // 2, D), BF),
        shape((SPAN, D // SPAN, 3 * WIDE), BF),
        shape((LOCAL, group, HEAD), BF),
        shape((LOCAL, group, HEAD), BF),
        shape((LOCAL, group, HEAD), BF),
        shape((LOCAL, group, HEAD), F32),
        shape((LOCAL, group, HEAD), F32),
        shape((8, 128), F32),
        shape((SPAN,) + wo.shape, BF),
        shape((SPAN,) + wu.shape, BF),
        shape((SPAN,) + wd.shape, BF),
    )
    vm = pltpu.VMEM
    scratch = [
        vm((SPAN, 2, rows // 2, D), BF),
        vm((SPAN, D // SPAN, 3 * WIDE), BF),
        vm((LOCAL, group, HEAD), BF),
        vm((LOCAL, group, HEAD), BF),
        vm((LOCAL, group, HEAD), BF),
        vm((LOCAL, group, HEAD), F32),
        vm((LOCAL, group, HEAD), F32),
        vm((SPAN, rows, WIDE), BF),
        vm((8, 128), F32),
        dma((9,)), dma((SPAN, 2)), dma((3,)), dma((3,)), dma((3,)), dma, dma((SPAN,)), dma((SPAN,)),
        dma((3, 3)), dma((3, 3)), dma((3, 3, 3)), dma((3, 3, 3)), dma((3, 3)), dma((3, 3)), dma((4,)), dma((8,)),
    ]
    return pl.pallas_call(
        forward_kernel,
        out_shape=outs,
        in_specs=[vmem, anyspace, vmem, anyspace, anyspace, anyspace],
        out_specs=(anyspace,) * len(outs),
        scratch_shapes=scratch,
        compiler_params=pltpu.CompilerParams(
            collective_id=0, has_side_effects=True, vmem_limit_bytes=56 << 20
        ),
        name="forward_attention",
    )(xa, wq4, start, wo, wu, wd)


def backward_kernel(
    dah, xg_in, wq_in, q_in, k_in, v_in, ah_in, tot_in, starts,
    dxh, gq,
    da, xg, wqs, qs, ks, vs, ahs, tots, dms, deltas, dqs, dp, own, mate, back,
    send_a, recv_a, send_m, recv_m, send_h, recv_h, in_sem,
):
    pb = lax.axis_index("pb")
    ka = lax.axis_index("ka")
    core = pb % 2
    base = pb - core
    side = ka // 2
    depth = mirror(ka, side)
    quarter = 2 * depth + core
    sibling = sibling_of(pb)
    rows = dah.shape[1]
    half = rows // 2

    greet(
        [(pb, (ka + i) % SPAN) for i in range(1, SPAN)]
        + [(sibling, (ka + i) % SPAN) for i in range(SPAN)]
    )
    loads = [
        pltpu.make_async_copy(src, dst, in_sem.at[n])
        for n, (src, dst) in enumerate(
            (
                (q_in, qs), (k_in, ks), (v_in, vs), (ah_in, ahs), (tot_in, tots), (xg_in, xg), (wq_in, wqs),
            )
        )
    ]
    for copy in loads:
        copy.start()

    def outgoing(n):
        worker_depth, worker_core = n // 2, n % 2
        target, where = base + worker_core, mirror(worker_depth, core)
        mine = (target == pb) & (where == ka)
        return mine, far(dah.at[n], da.at[ka], send_a.at[n], recv_a.at[ka], target, where)

    for n in range(SPAN):
        mine, remote = outgoing(n)

        @pl.when(jnp.logical_not(mine))
        def _():
            remote.start()

        @pl.when(mine)
        def _():
            pltpu.make_async_copy(dah.at[n], da.at[ka], recv_a.at[ka]).start()

    for copy in loads[:5]:
        copy.wait()
    for b in range(SPAN):
        far(dah.at[0], da.at[b], send_a.at[0], recv_a.at[b], pb, ka).wait_recv()

    scale = LOG2E / math.sqrt(HEAD)
    unit = 1.0 / math.sqrt(HEAD)
    one = jnp.where(starts[0:1, 0:1] > (SPAN // 2) * rows + 0.5, 1.0, 0.0)
    sub = 256

    for b in range(SPAN):
        block = da[b].astype(F32)
        for h in range(LOCAL):
            rows_b = slice(b * rows, (b + 1) * rows)
            scaled = block[:, h * HEAD : (h + 1) * HEAD] / tots[h, rows_b, :]
            dms[h, rows_b, :] = scaled.astype(BF)
            deltas[h, :, rows_b] = lax.dot_general(
                jnp.ones((8, HEAD), F32), scaled * ahs[h, rows_b, :],
                (((1,), (1,)), ((), ())), precision=lax.Precision.HIGHEST, preferred_element_type=F32,
            )

    def per_head(h, carry):
        dqs[...] = jnp.zeros_like(dqs)

        def per_block(kb, carry):
            for part in range(rows // sub):
                at = pl.multiple_of(kb * rows + part * sub, sub)
                keys = ks[h, pl.ds(at, sub), :]
                values = vs[h, pl.ds(at, sub), :]

                def terms(row0, width):
                    q = qs[h, pl.ds(row0, width), :]
                    dm = dms[h, pl.ds(row0, width), :]
                    s = dot_nt(keys, q) * scale
                    up, down = jnp.exp2(s - 1.0), jnp.exp2(-s - 1.0)
                    dsig = dot_nt(values, dm)
                    delta = deltas[h, 0:1, pl.ds(row0, width)]
                    return q, dm, up, down, dsig, delta

                def use(q, dm, expo, sine, dsig, delta):
                    ds = (expo * dsig - sine * delta).astype(BF)
                    return dot_nn(ds, q), dot_nn(sine.astype(BF), dm), dot_tn(ds, keys)

                width = rows - part * sub
                q, dm, up, down, dsig, delta = terms(at, width)
                seen = lax.broadcasted_iota(jnp.int32, (sub, width), 0) <= lax.broadcasted_iota(
                    jnp.int32, (sub, width), 1
                )
                up = jnp.where(seen, up, 0.0)
                down = jnp.where(seen, down, 0.0)
                dk, dv, dq = use(q, dm, up + down, up - down, dsig, delta)
                dqs[pl.ds(at, width), :] += dq

                def later(qb, state):
                    dk, dv = state
                    row0 = pl.multiple_of(qb * rows, rows)
                    q, dm, up, down, dsig, delta = terms(row0, rows)
                    dk1, dv1, dq1 = use(q, dm, up + down, up - down, dsig, delta)
                    same = jnp.where(qb // 2 == kb // 2, 1.0, 0.0)
                    keep = jnp.maximum(one, same) > 0.5
                    dqs[pl.ds(row0, rows), :] += jnp.where(keep, dq1, 0.0)
                    return dk + jnp.where(keep, dk1, 0.0), dv + jnp.where(keep, dv1, 0.0)

                dk, dv = lax.fori_loop(kb + 1, SPAN, later, (dk, dv))
                ks_out = pl.ds(at, sub)
                dp[1, h, ks_out, :] = (dk * unit).astype(BF)
                dp[2, h, ks_out, :] = dv.astype(BF)
            return carry

        lax.fori_loop(0, SPAN, per_block, 0)
        dp[0, h] = (dqs[...] * unit).astype(BF)
        return carry

    lax.fori_loop(0, LOCAL, per_head, 0)

    loads[5].wait()
    loads[6].wait()
    weight = wqs[...].reshape(D, 3 * WIDE)
    total = jnp.zeros((D, 3 * WIDE), F32)

    def joined(b):
        rows_b = slice(b * rows, (b + 1) * rows)
        return jnp.concatenate(
            [dp[part, h, rows_b, :] for part in range(3) for h in range(LOCAL)], axis=1
        )

    def home_copy(b, d):
        return far(back.at[b], dxh.at[depth, core], send_h.at[b], recv_h.at[depth, core], base + side, b)

    swaps = []
    for b in range(SPAN):
        part = dot_nt(joined(b), weight)
        own[b] = part.astype(BF).reshape(2, half, D)
        copy = far(own.at[b, 1 - core], mate.at[b], send_m.at[b], recv_m.at[b], sibling, ka)
        copy.start()
        swaps.append(copy)
    grad = dot_tn(xg[0].reshape(rows, D), joined(0))
    for b in range(1, SPAN):
        grad = grad + dot_tn(xg[b].reshape(rows, D), joined(b))
    gq[...] = grad.astype(BF).reshape(gq.shape)
    for b in range(SPAN):
        far(own.at[b, 0], mate.at[b], send_m.at[b], recv_m.at[b], sibling, ka).wait_recv()
        back[b] = (own[b, core].astype(F32) + mate[b].astype(F32)).astype(BF)
        mine = (core == side) & (ka == b)
        remote = home_copy(b, depth)

        @pl.when(jnp.logical_not(mine))
        def _():
            remote.start()

        @pl.when(mine)
        def _():
            pltpu.make_async_copy(back.at[b], dxh.at[depth, core], recv_h.at[depth, core]).start()

    for d in range(2):
        for k in range(2):
            far(back.at[0], dxh.at[d, k], send_h.at[0], recv_h.at[d, k], pb, ka).wait_recv()
    for copy in swaps:
        copy.wait_send()
    for n in range(SPAN):
        mine, remote = outgoing(n)

        @pl.when(jnp.logical_not(mine))
        def _():
            remote.wait_send()

        mine_b = (core == side) & (ka == n)
        remote_b = home_copy(n, depth)

        @pl.when(jnp.logical_not(mine_b))
        def _():
            remote_b.wait_send()


def backward_call(dah, xg, wq, q, k, v, ah, tot, starts):
    rows = dah.shape[1]
    group = rows * SPAN
    anyspace = pl.BlockSpec(memory_space=pl.ANY)
    vmem = pl.BlockSpec(memory_space=pltpu.VMEM)
    shape = jax.ShapeDtypeStruct
    dma = pltpu.SemaphoreType.DMA
    vm = pltpu.VMEM
    scratch = [
        vm((SPAN, rows, WIDE), BF),
        vm(xg.shape, BF),
        vm(wq.shape, BF),
        vm(q.shape, BF),
        vm(q.shape, BF),
        vm(q.shape, BF),
        vm(q.shape, F32),
        vm(q.shape, F32),
        vm(q.shape, BF),
        vm((LOCAL, 8, group), F32),
        vm((group, HEAD), F32),
        vm((3, LOCAL, group, HEAD), BF),
        vm((SPAN, 2, rows // 2, D), BF),
        vm((SPAN, rows // 2, D), BF),
        vm((SPAN, rows // 2, D), BF),
        dma((SPAN,)), dma((SPAN,)), dma((SPAN,)), dma((SPAN,)), dma((SPAN,)), dma((2, 2)), dma((7,)),
    ]
    return pl.pallas_call(
        backward_kernel,
        out_shape=(
            shape((2, 2, rows // 2, D), BF),
            shape((SPAN, D // SPAN, 3 * WIDE), BF),
        ),
        in_specs=[anyspace] * 8 + [vmem],
        out_specs=(anyspace, vmem),
        scratch_shapes=scratch,
        compiler_params=pltpu.CompilerParams(
            collective_id=1, has_side_effects=True, vmem_limit_bytes=56 << 20
        ),
        name="backward_attention",
    )(dah, xg, wq, q, k, v, ah, tot, starts)


def reduce_kernel(outer, count, *refs):
    ins, gq = refs[:count], refs[count]
    refs = refs[count + 1 :]
    outs, out_q = refs[:count], refs[count]
    refs = refs[count + 1 :]
    halves, mates, fours, sums, zs, fins, slots = (refs[i * count : (i + 1) * count] for i in range(7))
    refs = refs[7 * count :]
    fours_q, sum_q, zq, fin_q, slots_q = refs[:5]
    (
        own_sem, send_m, recv_m, send_p, recv_p, send_z, recv_z, send_o, recv_o,
        send_g, recv_g, send_c, recv_c, keep_sem,
    ) = refs[5:]
    pb = lax.axis_index("pb")
    ka = lax.axis_index("ka")
    core = pb % 2
    sibling = sibling_of(pb)
    plane = neighbours(pb)
    rank = (pb // 2) % 4
    where = pb // 8
    beyond = [(pb + 8 * o) % (8 * outer) for o in range(1, outer)]
    greet(
        [(pb, (ka + i) % SPAN) for i in range(1, SPAN)]
        + [(sibling, ka)]
        + [(p, ka) for p in plane]
        + [(p, ka) for p in beyond]
    )

    def columns(ref, k):
        width = ref.shape[-1] // 2
        return pl.ds(pl.multiple_of(k * width, 128), width)

    def quarter(ref, r):
        height = ref.shape[-2] // 4
        return pl.ds(pl.multiple_of(r * height, 16), height)

    started = []

    def begin(copy):
        copy.start()
        started.append(copy)
        return copy

    local = []
    for n in range(count):
        src = ins[n]
        copy = pltpu.make_async_copy(src.at[:, :, columns(src, core)], halves[n], own_sem.at[n])
        copy.start()
        local.append(copy)
        begin(far(src.at[:, :, columns(src, 1 - core)], mates[n], send_m.at[n], recv_m.at[n], sibling, ka))
    for m, p in enumerate(plane):
        begin(far(gq.at[:, quarter(gq, (p // 2) % 4), :], fours_q.at[m], send_p.at[count, m], recv_p.at[count, m], p, ka))

    for n in range(count):
        local[n].wait()
        far(mates[n], mates[n], send_m.at[n], recv_m.at[n], sibling, ka).wait_recv()

        def add(z, carry, n=n):
            halves[n][z] = (halves[n][z].astype(F32) + mates[n][z].astype(F32)).astype(BF)
            return carry

        lax.fori_loop(0, SPAN, add, 0)
        for m, p in enumerate(plane):
            begin(
                far(
                    halves[n].at[:, quarter(halves[n], (p // 2) % 4), :], fours[n].at[m],
                    send_p.at[n, m], recv_p.at[n, m], p, ka,
                )
            )

    for m, p in enumerate(plane):
        far(fours_q.at[m], fours_q.at[m], send_p.at[count, m], recv_p.at[count, m], p, ka).wait_recv()
    mine = quarter(gq, rank)
    sum_q[...] = (
        gq[:, mine, :].astype(F32) + fours_q[0].astype(F32) + fours_q[1].astype(F32) + fours_q[2].astype(F32)
    ).astype(BF)
    for i in range(1, SPAN):
        z = (ka + i) % SPAN
        begin(far(sum_q.at[z], zq.at[ka], send_z.at[count, i - 1], recv_z.at[count, i - 1], pb, z))
    zq[ka] = sum_q[ka]

    for n in range(count):
        for m, p in enumerate(plane):
            far(fours[n].at[m], fours[n].at[m], send_p.at[n, m], recv_p.at[n, m], p, ka).wait_recv()
        held = quarter(halves[n], rank)

        def add(z, carry, n=n, held=held):
            total = halves[n][z, held, :].astype(F32)
            for m in range(3):
                total = total + fours[n][m, z].astype(F32)
            sums[n][z] = total.astype(BF)
            return carry

        lax.fori_loop(0, SPAN, add, 0)
        for i in range(1, SPAN):
            z = (ka + i) % SPAN
            begin(far(sums[n].at[z], zs[n].at[i - 1], send_z.at[n, i - 1], recv_z.at[n, i - 1], pb, z))

    for i in range(1, SPAN):
        z = (ka - i) % SPAN
        far(zq.at[z], zq.at[z], send_z.at[count, i - 1], recv_z.at[count, i - 1], pb, z).wait_recv()
    for d in range(2):
        fin_q[d] = (zq[d].astype(F32) + zq[SPAN - 1 - d].astype(F32)).astype(BF)

    for n in range(count):
        for i in range(1, SPAN):
            far(zs[n].at[i - 1], zs[n].at[i - 1], send_z.at[n, i - 1], recv_z.at[n, i - 1], pb, ka).wait_recv()
        total = sums[n][ka].astype(F32)
        for i in range(3):
            total = total + zs[n][i].astype(F32)
        fins[n][...] = total.astype(BF)

    if outer > 1:
        for n in range(count + 1):
            fin = fin_q if n == count else fins[n]
            slot = slots_q if n == count else slots[n]
            for o, p in enumerate(beyond):
                far(fin, slot.at[where], send_o.at[n, o], recv_o.at[n, o], p, ka).start()
            slot[where] = fin[...]
        for n in range(count + 1):
            slot = slots_q if n == count else slots[n]
            for o in range(outer - 1):
                far(slot.at[0], slot.at[0], send_o.at[n, o], recv_o.at[n, o], pb, ka).wait_recv()
            total = slot[0].astype(F32)
            for o in range(1, outer):
                total = total + slot[o].astype(F32)
            for o in range(outer - 1):
                far(slot.at[0], slot.at[0], send_o.at[n, o], recv_o.at[n, o], pb, ka).wait_send()
            (fin_q if n == count else fins[n])[...] = total.astype(BF)

    def piece(n, r):
        out = outs[n]
        return out.at[quarter(out, r), columns(out, core)]

    keeps = []
    for n in range(count):
        copy = pltpu.make_async_copy(fins[n], piece(n, rank), keep_sem.at[n])
        copy.start()
        keeps.append(copy)
        for m, p in enumerate(plane):
            begin(far(fins[n], piece(n, rank), send_g.at[n, m], recv_g.at[n, m], p, ka))
    rows_q = quarter(out_q, rank)
    for d in range(2):
        copy = pltpu.make_async_copy(fin_q.at[d], out_q.at[2 * d + core, rows_q], keep_sem.at[count + d])
        copy.start()
        keeps.append(copy)
        for m, p in enumerate(plane):
            begin(far(fin_q.at[d], out_q.at[2 * d + core, rows_q], send_g.at[count + d, m], recv_g.at[count + d, m], p, ka))
    for copy in keeps:
        copy.wait()
    for n in range(count):
        for m, p in enumerate(plane):
            got = piece(n, (p // 2) % 4)
            far(got, got, send_g.at[n, m], recv_g.at[n, m], p, ka).wait_recv()
        strip = outs[n].at[:, columns(outs[n], core)]
        begin(far(strip, strip, send_c.at[n], recv_c.at[n], sibling, ka))
    for d in range(2):
        for m, p in enumerate(plane):
            got = out_q.at[2 * d + core, quarter(out_q, (p // 2) % 4)]
            far(got, got, send_g.at[count + d, m], recv_g.at[count + d, m], p, ka).wait_recv()
        strip = out_q.at[2 * d + core]
        begin(far(strip, strip, send_c.at[count + d], recv_c.at[count + d], sibling, ka))
    for n in range(count):
        strip = outs[n].at[:, columns(outs[n], 1 - core)]
        far(strip, strip, send_c.at[n], recv_c.at[n], sibling, ka).wait_recv()
    for d in range(2):
        strip = out_q.at[2 * d + 1 - core]
        far(strip, strip, send_c.at[count + d], recv_c.at[count + d], sibling, ka).wait_recv()
    for copy in started:
        copy.wait_send()


def reduce_call(parts, gq):
    outer = lax.axis_size("pb") // 8
    count = len(parts)
    anyspace = pl.BlockSpec(memory_space=pl.ANY)
    vmem = pl.BlockSpec(memory_space=pltpu.VMEM)
    shape = jax.ShapeDtypeStruct
    dma = pltpu.SemaphoreType.DMA
    vm = pltpu.VMEM
    small = [(p.shape[1] // 4, p.shape[2] // 2) for p in parts]
    sq = (gq.shape[1] // 4, gq.shape[2])
    beyond = max(outer - 1, 1)
    held = outer if outer > 1 else 1
    scratch = (
        [vm((SPAN, p.shape[1], p.shape[2] // 2), BF) for p in parts]
        + [vm((SPAN, p.shape[1], p.shape[2] // 2), BF) for p in parts]
        + [vm((3, SPAN) + s, BF) for s in small]
        + [vm((SPAN,) + s, BF) for s in small]
        + [vm((3,) + s, BF) for s in small]
        + [vm(s, BF) for s in small]
        + [vm((held,) + (s if outer > 1 else (16, 128)), BF) for s in small]
        + [
            vm((3, SPAN) + sq, BF),
            vm((SPAN,) + sq, BF),
            vm((SPAN,) + sq, BF),
            vm((2,) + sq, BF),
            vm((held, 2) + (sq if outer > 1 else (16, 128)), BF),
        ]
        + [
            dma((count,)), dma((count,)), dma((count,)), dma((count + 1, 3)), dma((count + 1, 3)),
            dma((count + 1, 3)), dma((count + 1, 3)), dma((count + 1, beyond)), dma((count + 1, beyond)),
            dma((count + 2, 3)), dma((count + 2, 3)), dma((count + 2,)), dma((count + 2,)), dma((count + 2,)),
        ]
    )
    return pl.pallas_call(
        functools.partial(reduce_kernel, outer, count),
        out_shape=tuple(shape(p.shape[1:], BF) for p in parts) + (shape((SPAN,) + gq.shape[1:], BF),),
        in_specs=[anyspace] * count + [vmem],
        out_specs=(anyspace,) * (count + 1),
        scratch_shapes=scratch,
        compiler_params=pltpu.CompilerParams(
            collective_id=2, has_side_effects=True, vmem_limit_bytes=56 << 20
        ),
        name="reduce_gradients",
    )(*parts, gq)


def normalize(values):
    center = values - jnp.mean(values, axis=1, keepdims=True)
    inverse = lax.rsqrt(jnp.mean(center * center, axis=1, keepdims=True) + 1e-05)
    return center * inverse, inverse


def norm_back(cot, norm, inverse):
    return inverse * (
        cot - jnp.mean(cot, axis=1, keepdims=True) - norm * jnp.mean(cot * norm, axis=1, keepdims=True)
    )


def gelu_tanh(values):
    return jax.nn.gelu(values, approximate=True)


def body(layer_input, second_start, gain_attn, w_qkv, w_out, gain_mlp, w_up, w_down, d_output):
    rows = layer_input.shape[0]
    kv_index = lax.axis_index("ka")
    inputs32 = layer_input.astype(F32)
    norm_one, inverse_one = normalize(inputs32)
    attn_in = (norm_one * gain_attn).astype(BF)
    wq4 = w_qkv.reshape(D // SPAN, 3, SPAN, WIDE).transpose(2, 0, 1, 3).reshape(SPAN, D // SPAN, 3 * WIDE)
    start = jnp.full((8, 128), second_start[0].astype(F32), F32)
    (o_home, xg, wq, q, k, v, ah, tot, starts, wo_g, wu_g, wd_g) = forward_call(
        attn_in, wq4, start, w_out, w_up, w_down
    )
    full_out = wo_g.reshape(D, D)
    full_up = wu_g.reshape(D, -1)
    full_down = wd_g.reshape(-1, D)
    attn_low = o_home.transpose(1, 0, 2).reshape(rows, D)
    attn_branch = dot_nn(attn_low, full_out)
    middle = inputs32 + attn_branch
    norm_two, inverse_two = normalize(middle)
    mlp_in = (norm_two * gain_mlp).astype(BF)
    up_proj = dot_nn(mlp_in, full_up)
    activated = gelu_tanh(up_proj).astype(BF)
    mlp_branch = dot_nn(activated, full_down)
    output = (middle + mlp_branch).astype(BF)
    squares = jnp.stack(
        [jnp.sum(t * t) for t in (inputs32, attn_branch, middle, mlp_branch)]
    )
    d_act = dot_nt(d_output, full_down)
    d_w_down = dot_tn(activated, d_output).astype(BF)
    d_up = jax.vjp(gelu_tanh, up_proj)[1](d_act)[0].astype(BF)
    d_w_up = dot_tn(mlp_in, d_up).astype(BF)
    d_mlp_in = dot_nt(d_up, full_up)
    d_middle = d_output.astype(F32) + norm_back(d_mlp_in * gain_mlp, norm_two, inverse_two)
    g_middle = d_middle.astype(BF)
    d_w_out = dot_tn(attn_low, g_middle).astype(BF)
    d_attn = dot_nt(g_middle, full_out).astype(BF)
    dah = d_attn.reshape(rows, SPAN, WIDE).transpose(1, 0, 2)
    dxh, gq = backward_call(dah, xg, wq, q, k, v, ah, tot, starts)
    d_attn_in = (dxh[0].astype(F32) + dxh[1].astype(F32)).reshape(rows, D)
    d_input = d_middle + norm_back(d_attn_in * gain_attn, norm_one, inverse_one)
    extra = jnp.zeros((SPAN, D // 12, D), BF)
    extra = extra.at[:, 0, 0].set(squares.astype(BF))
    go = jnp.concatenate([d_w_out.reshape(SPAN, D // SPAN, D), extra], axis=1)
    fd, fu, fo, fq = reduce_call(
        (d_w_down.reshape(SPAN, -1, D), d_w_up.reshape(SPAN, D // SPAN, -1), go), gq
    )
    total_down = fd.astype(F32)
    total_up = fu.astype(F32)
    total_out = fo[: D // SPAN].astype(F32)
    total_qkv = (
        fq.reshape(SPAN, D // SPAN, 3, WIDE).transpose(1, 2, 0, 3).reshape(D // SPAN, 3 * D).astype(F32)
    )

    def gain_grad(weight, grad, gain):
        own = lax.dynamic_slice_in_dim(gain, kv_index * (D // SPAN), D // SPAN)
        return jnp.sum(weight.astype(F32) * grad, axis=1) / own

    total_gain_attn = gain_grad(w_qkv, total_qkv, gain_attn)
    total_gain_mlp = gain_grad(w_up, total_up, gain_mlp)
    entry_count = rows * SPAN * lax.axis_size("pb") * D
    rms = jnp.sqrt(fo[D // SPAN, 0:1].astype(F32) / entry_count)
    return (
        output, d_input, total_gain_attn, total_qkv, total_out, total_gain_mlp, total_up, total_down, rms,
    )


def solution(mesh):
    if mesh.shape["ka"] != SPAN or mesh.shape["pb"] % 8:
        raise ValueError("unsupported mesh")
    placed = (
        P(("pb", "ka"), None), P("pb"), P(), P("ka", None), P("ka", None), P(), P("ka", None), P("ka", None),
        P(("pb", "ka"), None),
    )
    return jax.shard_map(
        body,
        mesh=mesh,
        in_specs=placed,
        out_specs=(
            P(("pb", "ka"), None), P(("pb", "ka"), None), P("ka"), P("ka", None), P("ka", None), P("ka"),
            P("ka", None), P("ka", None), P("ka"),
        ),
        check_vma=False,
    )
```

```python
import functools
import math

import jax
import jax.numpy as jnp
from jax import lax
from jax.experimental import pallas as pl
from jax.experimental.pallas import tpu as pltpu
from jax.sharding import PartitionSpec as P

D = 768
HEADS = 12
HEAD = 64
SPAN = 4
LOCAL = HEADS // SPAN
WIDE = LOCAL * HEAD
LOG2E = 1.4426950408889634
MESH = pl.DeviceIdType.MESH
BF = jnp.bfloat16
F32 = jnp.float32


def mirror(depth, side):
    return depth + side * (SPAN - 1 - 2 * depth)


def neighbours(pb):
    across_x = pb + 2 - 4 * ((pb // 2) % 2)
    across_y = pb + 4 - 8 * ((pb // 4) % 2)
    across_both = across_x + 4 - 8 * ((across_x // 4) % 2)
    return across_x, across_y, across_both


def sibling_of(pb):
    return pb + 1 - 2 * (pb % 2)


def far(src, dst, send_sem, recv_sem, pb, ka):
    return pltpu.make_async_remote_copy(
        src, dst, send_sem, recv_sem, device_id=(pb, ka), device_id_type=MESH
    )


def greet(peers):
    barrier = pltpu.get_barrier_semaphore()
    for peer in peers:
        pl.semaphore_signal(barrier, 1, device_id=peer, device_id_type=MESH)
    pl.semaphore_wait(barrier, len(peers))


def dot_nt(left, right):
    return lax.dot_general(left, right, (((1,), (1,)), ((), ())), preferred_element_type=F32)


def dot_tn(left, right):
    return lax.dot_general(left, right, (((0,), (0,)), ((), ())), preferred_element_type=F32)


def dot_nn(left, right):
    return jnp.dot(left, right, preferred_element_type=F32)


def fold_lanes(tile):
    out = tile[:, :128]
    for at in range(128, tile.shape[1], 128):
        out = out + tile[:, at : at + 128]
    return out


def forward_kernel(
    xa, wq4, start, wo, wu, wd,
    ohome, xg_out, wq_out, q_out, k_out, v_out, ah_out, tot_out, start_out, wog, wug, wdg,
    xg, wqs, qs, ks, vs, ahs, tots, ob, starts, wo_own, wu_own, wd_own,
    send_x, recv_x, send_q, recv_q, send_w, recv_w, send_s, recv_s, send_o, recv_o,
    send_z, recv_z, send_p, recv_p, send_c, recv_c, own_sem, out_sem,
):
    pb = lax.axis_index("pb")
    ka = lax.axis_index("ka")
    core = pb % 2
    base = pb - core
    side = ka // 2
    depth = mirror(ka, side)
    home_u = mirror(ka, core)
    quarter = 2 * depth + core
    sibling = sibling_of(pb)
    plane = neighbours(pb)
    rows = xa.shape[0]
    half = rows // 2
    rank = (pb // 2) % 4

    greet(
        [(pb, (ka + i) % SPAN) for i in range(1, SPAN)]
        + [(sibling, (ka + i) % SPAN) for i in range(SPAN)]
        + [(p, ka) for p in plane]
    )

    odd = (((home_u + 1) // 2) % 2) * (1 - home_u // 2)
    goal = mirror(1 - odd, core)
    out_x = [
        far(xa.at[pl.ds(h * half, half)], xg.at[ka, h], send_x.at[h], recv_x.at[ka, h], base + h, goal)
        for h in range(2)
    ]
    for copy in out_x:
        copy.start()

    at_home = core == side

    def near_copies():
        remote = [
            far(xa.at[pl.ds(h * half, half)], xg.at[ka, h], send_x.at[2 + h], recv_x.at[ka, h], sibling, ka)
            for h in range(2)
        ]
        local = [
            pltpu.make_async_copy(xa.at[pl.ds(h * half, half)], xg.at[ka, h], recv_x.at[ka, h])
            for h in range(2)
        ]
        return remote, local

    @pl.when(at_home)
    def _():
        remote, local = near_copies()
        for copy in remote + local:
            copy.start()

    def start_copies():
        out = []
        for n, (d, k) in enumerate(((0, 1), (1, 0), (1, 1))):
            target = base + (core + k) % 2
            out.append(far(start, starts, send_s.at[n], recv_s, target, mirror(d, core)))
        return out

    @pl.when(home_u == 0)
    def _():
        for copy in start_copies():
            copy.start()
        pltpu.make_async_copy(start, starts, recv_s).start()

    height = wq4.shape[1] // 4

    def lines(ref, r):
        return ref.at[pl.ds(pl.multiple_of(r * height, 16), height)]

    out_q = []
    for i in range(1, SPAN):
        z = (ka + i) % SPAN
        zd = mirror(z, z // 2)
        out_q.append(
            far(
                lines(wq4.at[2 * zd + core], rank), lines(wqs.at[ka], rank),
                send_q.at[i - 1], recv_q.at[i - 1], pb, z,
            )
        )
    for copy in out_q:
        copy.start()
    own_q = pltpu.make_async_copy(wq4.at[quarter], wqs.at[ka], own_sem.at[0])
    own_q.start()
    own_w = [
        pltpu.make_async_copy(src, dst, own_sem.at[1 + n])
        for n, (src, dst) in enumerate(((wo, wo_own), (wu, wu_own), (wd, wd_own)))
    ]

    spread = []
    for i in range(3):
        u = (1 - depth) if i == 0 else i + 1
        b = mirror(u, side)
        far(xg.at[b, core], xg.at[b, core], send_x.at[4], recv_x.at[b, core], pb, ka).wait_recv()
        copy = far(xg.at[b, core], xg.at[b, core], send_x.at[4 + i], recv_x.at[b, core], sibling, ka)
        copy.start()
        spread.append(copy)
        if i >= 1:
            onward = far(
                xg.at[b, core], xg.at[b, core], send_x.at[6 + i], recv_x.at[b, core], pb, mirror(0, side)
            )

            @pl.when(depth == 1)
            def _():
                onward.start()

            spread.append(onward)
        if i == 0:
            for n in range(1, SPAN):
                mine_q = lines(wqs.at[(ka - n) % SPAN], rank)
                far(mine_q, mine_q, send_q.at[0], recv_q.at[n - 1], pb, ka).wait_recv()
                for m, p in enumerate(plane):
                    copy = far(mine_q, mine_q, send_w.at[n - 1, m], recv_w.at[n - 1, m], p, ka)
                    copy.start()
                    out_q.append(copy)
    b_near = ka
    for h in range(2):
        far(xg.at[b_near, h], xg.at[b_near, h], send_x.at[4], recv_x.at[b_near, h], pb, ka).wait_recv()
    for i in range(3):
        u = (1 - depth) if i == 0 else i + 1
        b = mirror(u, side)
        far(xg.at[b, 1 - core], xg.at[b, 1 - core], send_x.at[4], recv_x.at[b, 1 - core], pb, ka).wait_recv()

    parts = (
        (wd, wdg, wd.shape[0] // 4, wd.shape[1] // 2),
        (wu, wug, wu.shape[0] // 4, wu.shape[1] // 2),
        (wo, wog, wo.shape[0] // 4, wo.shape[1] // 2),
    )

    def piece(ref, n):
        _, _, r, c = parts[n]
        return ref.at[pl.ds(pl.multiple_of(rank * r, 16), r), pl.ds(pl.multiple_of(core * c, 128), c)]

    def strip(ref, n):
        _, _, _, c = parts[n]
        return ref.at[:, pl.ds(pl.multiple_of(core * c, 128), c)]

    def strip_other(ref, n):
        _, _, _, c = parts[n]
        return ref.at[:, pl.ds(pl.multiple_of((1 - core) * c, 128), c)]

    along_z = []
    for n, (src, dst, _, _) in enumerate(parts):
        for i in range(1, SPAN):
            z = (ka + i) % SPAN
            along_z.append(
                far(piece(src, n), piece(dst.at[ka], n), send_z.at[n, i - 1], recv_z.at[n, i - 1], pb, z)
            )
    for copy in along_z + own_w:
        copy.start()

    for i in range(1, SPAN):
        for m, p in enumerate(plane):
            theirs = lines(wqs.at[(ka - i) % SPAN], (p // 2) % 4)
            far(theirs, theirs, send_w.at[i - 1, m], recv_w.at[i - 1, m], p, ka).wait_recv()
    own_q.wait()
    pltpu.make_async_copy(start, starts, recv_s).wait()

    def project(b, carry):
        xb = xg[b].reshape(rows, D)
        at = pl.multiple_of(b * rows, rows)
        for dst, col in ((qs, 0), (ks, WIDE), (vs, 2 * WIDE)):
            w = wqs[:, :, col : col + WIDE].reshape(D, WIDE)
            out = dot_nn(xb, w).astype(BF)
            for h in range(LOCAL):
                dst[h, pl.ds(at, rows), :] = out[:, h * HEAD : (h + 1) * HEAD]
        return carry

    lax.fori_loop(0, SPAN, project, 0)

    in_plane = []

    def part_of(n, i, r):
        dst, height, width = parts[n][1:]
        return dst.at[
            (ka - i) % SPAN, pl.ds(pl.multiple_of(r * height, 16), height),
            pl.ds(pl.multiple_of(core * width, 128), width),
        ]

    def plane_copy(n, i, m, r, p):
        ref = part_of(n, i, r)
        return far(ref, ref, send_p.at[n, i - 1, m], recv_p.at[n, i - 1, m], p, ka)

    def begin_plane(n):
        for i in range(1, SPAN):
            ref = part_of(n, i, rank)
            far(ref, ref, send_z.at[n, 0], recv_z.at[n, i - 1], pb, ka).wait_recv()
            for m in range(2):
                copy = plane_copy(n, i, m, rank, plane[m])
                copy.start()
                in_plane.append(copy)

    def pass_on(n):
        first = n % 2
        r = (plane[first] // 2) % 4
        for i in range(1, SPAN):
            plane_copy(n, i, first, r, pb).wait_recv()
            copy = plane_copy(n, i, 2, r, plane[1 - first])
            copy.start()
            in_plane.append(copy)

    across = []

    def begin_across(n):
        other = 1 - n % 2
        dst = parts[n][1]
        for i in range(1, SPAN):
            plane_copy(n, i, other, (plane[other] // 2) % 4, pb).wait_recv()
            plane_copy(n, i, 2, (plane[2] // 2) % 4, pb).wait_recv()
            z = (ka - i) % SPAN
            copy = far(
                strip(dst.at[z], n), strip(dst.at[z], n), send_c.at[n, i - 1], recv_c.at[n, i - 1], sibling, ka
            )
            copy.start()
            across.append(copy)

    scale = LOG2E / math.sqrt(HEAD)
    one = starts[0:1, 0:1] > (SPAN // 2) * rows + 0.5
    sub = 256

    def attend_block(b, after=()):
        for h in range(LOCAL):
            for part in range(rows // sub):
                row0 = b * rows + part * sub
                q = qs[h, row0 : row0 + sub, :]

                def full(kb, state, q=q, h=h):
                    acc, tot = state
                    at = pl.multiple_of(kb * rows, rows)
                    s = dot_nt(q, ks[h, pl.ds(at, rows), :]) * scale
                    up, down = jnp.exp2(s - 1.0), jnp.exp2(-s - 1.0)
                    tot = tot + fold_lanes(up + down)
                    acc = acc + dot_nn((up - down).astype(BF), vs[h, pl.ds(at, rows), :])
                    return acc, tot

                state = (jnp.zeros((sub, HEAD), F32), jnp.zeros((sub, 128), F32))
                if b >= SPAN // 2:
                    acc, tot = lax.fori_loop(0, SPAN // 2, full, state)
                    state = (jnp.where(one, acc, 0.0), jnp.where(one, tot, 0.0))
                    state = lax.fori_loop(SPAN // 2, b, full, state)
                else:
                    state = lax.fori_loop(0, b, full, state)
                acc, tot = state
                width = (part + 1) * sub
                s = dot_nt(q, ks[h, b * rows : b * rows + width, :]) * scale
                seen = (
                    lax.broadcasted_iota(jnp.int32, (sub, width), 0) + part * sub
                    >= lax.broadcasted_iota(jnp.int32, (sub, width), 1)
                )
                up = jnp.where(seen, jnp.exp2(s - 1.0), 0.0)
                down = jnp.where(seen, jnp.exp2(-s - 1.0), 0.0)
                tot = tot + fold_lanes(up + down)
                acc = acc + dot_nn((up - down).astype(BF), vs[h, b * rows : b * rows + width, :])
                total = jnp.sum(tot, axis=1, keepdims=True)
                heads = acc / total
                ahs[h, row0 : row0 + sub, :] = heads
                tots[h, row0 : row0 + sub, :] = jnp.broadcast_to(total, (sub, HEAD))
            for step in after[h : h + 1]:
                step()

    send_back = []
    hooks = {3: (functools.partial(begin_plane, 0), functools.partial(begin_plane, 1))}
    for b in range(SPAN):
        attend_block(b, hooks.get(b, ()))
        joined = jnp.concatenate(
            [ahs[h, b * rows : (b + 1) * rows, :] for h in range(LOCAL)], axis=1
        )
        ob[b] = joined.astype(BF)
        remote = far(ob.at[b], ohome.at[quarter], send_o.at[b], recv_o.at[quarter], base + side, b)
        mine = (core == side) & (ka == b)

        @pl.when(jnp.logical_not(mine))
        def _():
            remote.start()

        @pl.when(mine)
        def _():
            pltpu.make_async_copy(ob.at[b], ohome.at[quarter], recv_o.at[quarter]).start()

        send_back.append((mine, remote))

    for copy in own_w:
        copy.wait()
    begin_plane(2)
    for n in range(3):
        pass_on(n)
    for n in range(3):
        begin_across(n)
    saves = [
        pltpu.make_async_copy(src, dst, out_sem.at[n])
        for n, (src, dst) in enumerate(
            (
                (xg, xg_out), (wqs, wq_out), (qs, q_out), (ks, k_out), (vs, v_out),
                (ahs, ah_out), (tots, tot_out), (starts, start_out),
                (wo_own, wog.at[ka]), (wu_own, wug.at[ka]), (wd_own, wdg.at[ka]),
            )
        )
    ]
    for copy in saves:
        copy.start()

    for i in range(1, SPAN):
        z = (ka - i) % SPAN
        for n, (src, dst, _, _) in enumerate(parts):
            far(
                strip_other(dst.at[z], n), strip_other(dst.at[z], n),
                send_c.at[n, 0], recv_c.at[n, i - 1], pb, ka,
            ).wait_recv()
    for n in range(SPAN):
        far(ob.at[0], ohome.at[n], send_o.at[0], recv_o.at[n], pb, ka).wait_recv()
    for copy in saves:
        copy.wait()
    for copy in out_x + out_q + along_z + in_plane + across:
        copy.wait_send()
    for n in range(3):
        spread[(0, 1, 3)[n]].wait_send()

    @pl.when(depth == 1)
    def _():
        spread[2].wait_send()
        spread[4].wait_send()

    @pl.when(at_home)
    def _():
        remote, _ = near_copies()
        for copy in remote:
            copy.wait_send()

    @pl.when(home_u == 0)
    def _():
        for copy in start_copies():
            copy.wait_send()

    for mine, remote in send_back:

        @pl.when(jnp.logical_not(mine))
        def _():
            remote.wait_send()


def forward_call(xa, wq4, start, wo, wu, wd):
    rows = xa.shape[0]
    group = rows * SPAN
    anyspace = pl.BlockSpec(memory_space=pl.ANY)
    vmem = pl.BlockSpec(memory_space=pltpu.VMEM)
    shape = jax.ShapeDtypeStruct
    dma = pltpu.SemaphoreType.DMA
    outs = (
        shape((SPAN, rows, WIDE), BF),
        shape((SPAN, 2, rows // 2, D), BF),
        shape((SPAN, D // SPAN, 3 * WIDE), BF),
        shape((LOCAL, group, HEAD), BF),
        shape((LOCAL, group, HEAD), BF),
        shape((LOCAL, group, HEAD), BF),
        shape((LOCAL, group, HEAD), F32),
        shape((LOCAL, group, HEAD), F32),
        shape((8, 128), F32),
        shape((SPAN,) + wo.shape, BF),
        shape((SPAN,) + wu.shape, BF),
        shape((SPAN,) + wd.shape, BF),
    )
    vm = pltpu.VMEM
    scratch = [
        vm((SPAN, 2, rows // 2, D), BF),
        vm((SPAN, D // SPAN, 3 * WIDE), BF),
        vm((LOCAL, group, HEAD), BF),
        vm((LOCAL, group, HEAD), BF),
        vm((LOCAL, group, HEAD), BF),
        vm((LOCAL, group, HEAD), F32),
        vm((LOCAL, group, HEAD), F32),
        vm((SPAN, rows, WIDE), BF),
        vm((8, 128), F32),
        vm(wo.shape, BF),
        vm(wu.shape, BF),
        vm(wd.shape, BF),
        dma((9,)), dma((SPAN, 2)), dma((3,)), dma((3,)), dma((3, 3)), dma((3, 3)), dma((3,)), dma,
        dma((SPAN,)), dma((SPAN,)),
        dma((3, 3)), dma((3, 3)), dma((3, 3, 3)), dma((3, 3, 3)), dma((3, 3)), dma((3, 3)), dma((4,)), dma((11,)),
    ]
    return pl.pallas_call(
        forward_kernel,
        out_shape=outs,
        in_specs=[vmem, anyspace, vmem, anyspace, anyspace, anyspace],
        out_specs=(anyspace,) * len(outs),
        scratch_shapes=scratch,
        compiler_params=pltpu.CompilerParams(
            collective_id=0, has_side_effects=True, vmem_limit_bytes=56 << 20
        ),
        name="forward_attention",
    )(xa, wq4, start, wo, wu, wd)


CHUNKS = (
    (0, 0, 384, 0, 384),
    (0, 384, 384, 0, 384),
    (1, 0, 192, 0, 768),
    (1, 0, 192, 768, 768),
    (2, 0, 256, 0, 384),
)


def backward_kernel(
    outer, dah, xg_in, wq_in, q_in, k_in, v_in, ah_in, tot_in, starts, gd, gu, go,
    dxh, fd, fu, fo, fq,
    da, xg, wqs, qs, ks, vs, ahs, tots, dms, deltas, dqs, dp, own, mate, back, gq,
    *refs,
):
    count = len(CHUNKS)
    halves, mates, fours, sums, zs, fins, slots = (refs[i * count : (i + 1) * count] for i in range(7))
    refs = refs[7 * count :]
    fours_q, sum_q, zq, fin_q, slots_q = refs[:5]
    (
        send_a, recv_a, send_m, recv_m, send_h, recv_h, in_sem,
        own_sem, send_n, recv_n, send_p, recv_p, send_z, recv_z, send_o, recv_o,
        send_g, recv_g, send_c, recv_c, keep_sem,
    ) = refs[5:]
    pb = lax.axis_index("pb")
    ka = lax.axis_index("ka")
    core = pb % 2
    base = pb - core
    side = ka // 2
    depth = mirror(ka, side)
    sibling = sibling_of(pb)
    plane = neighbours(pb)
    rank = (pb // 2) % 4
    where = pb // 8
    beyond = [(pb + 8 * o) % (8 * outer) for o in range(1, outer)]
    rows = dah.shape[1]
    half = rows // 2

    greet(
        [(pb, (ka + i) % SPAN) for i in range(1, SPAN)]
        + [(sibling, (ka + i) % SPAN) for i in range(SPAN)]
        + [(p, ka) for p in plane]
        + [(p, ka) for p in beyond]
    )

    def outgoing(n):
        worker_depth, worker_core = n // 2, n % 2
        target, spot = base + worker_core, mirror(worker_depth, core)
        mine = (target == pb) & (spot == ka)
        return mine, far(dah.at[n], da.at[ka], send_a.at[n], recv_a.at[ka], target, spot)

    for n in range(SPAN):
        mine, remote = outgoing(n)

        @pl.when(jnp.logical_not(mine))
        def _():
            remote.start()

        @pl.when(mine)
        def _():
            pltpu.make_async_copy(dah.at[n], da.at[ka], recv_a.at[ka]).start()

    sources = (gd, gu, go)
    results = (fd, fu, fo)

    def block_of(ref, n, k, row0, height):
        _, _, _, col0, width = CHUNKS[n]
        at = pl.multiple_of(k * (ref.shape[-1] // 2) + col0, 128)
        return pl.ds(row0, height), pl.ds(at, width)

    def source(n, k):
        a, row0, height, _, _ = CHUNKS[n]
        r, c = block_of(sources[a], n, k, row0, height)
        return sources[a].at[:, r, c]

    def quarter(n, r):
        height = CHUNKS[n][2] // 4
        return pl.ds(pl.multiple_of(r * height, 16), height)

    def landing(n, r):
        a, row0, height, _, _ = CHUNKS[n]
        rr, c = block_of(results[a], n, core, pl.multiple_of(row0 + r * (height // 4), 16), height // 4)
        return results[a].at[rr, c]

    def strip(n, k):
        a, row0, height, _, _ = CHUNKS[n]
        r, c = block_of(results[a], n, k, row0, height)
        return results[a].at[r, c]

    def local_half(n):
        return pltpu.make_async_copy(source(n, core), halves[n], own_sem.at[n])

    def to_sibling(n):
        return far(source(n, 1 - core), mates[n], send_n.at[n], recv_n.at[n], sibling, ka)

    def to_plane(n, m):
        p = plane[m]
        return far(
            halves[n].at[:, quarter(n, (p // 2) % 4), :], fours[n].at[m], send_p.at[n, m], recv_p.at[n, m], p, ka
        )

    def to_owner(n, i):
        z = (ka + i) % SPAN
        return far(sums[n].at[z], zs[n].at[i - 1], send_z.at[n, i - 1], recv_z.at[n, i - 1], pb, z)

    def keep(n):
        return pltpu.make_async_copy(fins[n], landing(n, rank), keep_sem.at[n])

    def to_all(n, m):
        return far(fins[n], landing(n, rank), send_g.at[n, m], recv_g.at[n, m], plane[m], ka)

    def to_twin(n):
        return far(strip(n, core), strip(n, core), send_c.at[n], recv_c.at[n], sibling, ka)

    def merge_sibling(n):
        local_half(n).wait()
        to_sibling(n).wait_recv()

        def add(z, carry):
            halves[n][z] = (halves[n][z].astype(F32) + mates[n][z].astype(F32)).astype(BF)
            return carry

        lax.fori_loop(0, SPAN, add, 0)
        for m in range(3):
            to_plane(n, m).start()

    def merge_plane(n):
        for m in range(3):
            to_plane(n, m).wait_recv()
        held = quarter(n, rank)

        def add(z, carry):
            total = halves[n][z, held, :].astype(F32)
            for m in range(3):
                total = total + fours[n][m, z].astype(F32)
            sums[n][z] = total.astype(BF)
            return carry

        lax.fori_loop(0, SPAN, add, 0)
        for i in range(1, SPAN):
            to_owner(n, i).start()

    def merge_beyond(fin, slot, n):
        for o, p in enumerate(beyond):
            far(fin, slot.at[where], send_o.at[n, o], recv_o.at[n, o], p, ka).start()
        slot[where] = fin[...]
        for o in range(outer - 1):
            far(slot.at[0], slot.at[0], send_o.at[n, o], recv_o.at[n, o], pb, ka).wait()
        total = slot[0].astype(F32)
        for o in range(1, outer):
            total = total + slot[o].astype(F32)
        fin[...] = total.astype(BF)

    def merge_z(n):
        for i in range(1, SPAN):
            to_owner(n, i).wait_recv()
        total = sums[n][ka].astype(F32)
        for i in range(3):
            total = total + zs[n][i].astype(F32)
        fins[n][...] = total.astype(BF)
        if outer > 1:
            merge_beyond(fins[n], slots[n], n)
        keep(n).start()
        for m in range(3):
            to_all(n, m).start()

    def pass_twin(n):
        keep(n).wait()
        for m in range(3):
            got = landing(n, (plane[m] // 2) % 4)
            far(got, got, send_g.at[n, m], recv_g.at[n, m], pb, ka).wait_recv()
        to_twin(n).start()

    def finish(n):
        got = strip(n, 1 - core)
        far(got, got, send_c.at[n], recv_c.at[n], sibling, ka).wait_recv()
        to_sibling(n).wait_send()
        for m in range(3):
            to_plane(n, m).wait_send()
            to_all(n, m).wait_send()
        for i in range(1, SPAN):
            to_owner(n, i).wait_send()
        to_twin(n).wait_send()

    for n in range(count):
        local_half(n).start()
        to_sibling(n).start()

    loads = [
        pltpu.make_async_copy(src, dst, in_sem.at[n])
        for n, (src, dst) in enumerate(
            (
                (q_in, qs), (k_in, ks), (v_in, vs), (ah_in, ahs), (tot_in, tots), (xg_in, xg), (wq_in, wqs),
            )
        )
    ]
    for copy in loads:
        copy.start()

    for n in range(count):
        merge_sibling(n)

    for copy in loads[:5]:
        copy.wait()
    for b in range(SPAN):
        far(dah.at[0], da.at[b], send_a.at[0], recv_a.at[b], pb, ka).wait_recv()

    scale = LOG2E / math.sqrt(HEAD)
    unit = 1.0 / math.sqrt(HEAD)
    one = jnp.where(starts[0:1, 0:1] > (SPAN // 2) * rows + 0.5, 1.0, 0.0)
    sub = 256

    for b in range(SPAN):
        block = da[b].astype(F32)
        for h in range(LOCAL):
            rows_b = slice(b * rows, (b + 1) * rows)
            scaled = block[:, h * HEAD : (h + 1) * HEAD] / tots[h, rows_b, :]
            dms[h, rows_b, :] = scaled.astype(BF)
            deltas[h, :, rows_b] = lax.dot_general(
                jnp.ones((8, HEAD), F32), scaled * ahs[h, rows_b, :],
                (((1,), (1,)), ((), ())), precision=lax.Precision.HIGHEST, preferred_element_type=F32,
            )

    def piece(i, carry):
        h = i // SPAN
        kb = i % SPAN

        @pl.when(kb == 0)
        def _():
            dqs[...] = jnp.zeros_like(dqs)

        for part in range(rows // sub):
            at = pl.multiple_of(kb * rows + part * sub, sub)
            keys = ks[h, pl.ds(at, sub), :]
            values = vs[h, pl.ds(at, sub), :]

            def terms(row0, width):
                q = qs[h, pl.ds(row0, width), :]
                dm = dms[h, pl.ds(row0, width), :]
                s = dot_nt(keys, q) * scale
                up, down = jnp.exp2(s - 1.0), jnp.exp2(-s - 1.0)
                dsig = dot_nt(values, dm)
                delta = deltas[h, 0:1, pl.ds(row0, width)]
                return q, dm, up, down, dsig, delta

            def use(q, dm, expo, sine, dsig, delta):
                ds = (expo * dsig - sine * delta).astype(BF)
                return dot_nn(ds, q), dot_nn(sine.astype(BF), dm), dot_tn(ds, keys)

            width = rows - part * sub
            q, dm, up, down, dsig, delta = terms(at, width)
            seen = lax.broadcasted_iota(jnp.int32, (sub, width), 0) <= lax.broadcasted_iota(
                jnp.int32, (sub, width), 1
            )
            up = jnp.where(seen, up, 0.0)
            down = jnp.where(seen, down, 0.0)
            dk, dv, dq = use(q, dm, up + down, up - down, dsig, delta)
            dqs[pl.ds(at, width), :] += dq

            def later(qb, state):
                dk, dv = state
                row0 = pl.multiple_of(qb * rows, rows)
                q, dm, up, down, dsig, delta = terms(row0, rows)
                dk1, dv1, dq1 = use(q, dm, up + down, up - down, dsig, delta)
                same = jnp.where(qb // 2 == kb // 2, 1.0, 0.0)
                keep_it = jnp.maximum(one, same) > 0.5
                dqs[pl.ds(row0, rows), :] += jnp.where(keep_it, dq1, 0.0)
                return dk + jnp.where(keep_it, dk1, 0.0), dv + jnp.where(keep_it, dv1, 0.0)

            dk, dv = lax.fori_loop(kb + 1, SPAN, later, (dk, dv))
            ks_out = pl.ds(at, sub)
            dp[1, h, ks_out, :] = (dk * unit).astype(BF)
            dp[2, h, ks_out, :] = dv.astype(BF)

        @pl.when(kb == SPAN - 1)
        def _():
            dp[0, h] = (dqs[...] * unit).astype(BF)

        for at_piece, step, n in HOOKS:

            @pl.when(i == at_piece)
            def _(step=step, n=n):
                steps[step](n)

        return carry

    steps = {"plane": merge_plane, "z": merge_z, "twin": pass_twin}
    lax.fori_loop(0, LOCAL * SPAN, piece, 0)

    loads[5].wait()
    loads[6].wait()
    weight = wqs[...].reshape(D, 3 * WIDE)

    def joined(b):
        rows_b = slice(b * rows, (b + 1) * rows)
        return jnp.concatenate(
            [dp[part, h, rows_b, :] for part in range(3) for h in range(LOCAL)], axis=1
        )

    def home_copy(b):
        return far(back.at[b], dxh.at[depth, core], send_h.at[b], recv_h.at[depth, core], base + side, b)

    def swap(b):
        return far(own.at[b, 1 - core], mate.at[b], send_m.at[b], recv_m.at[b], sibling, ka)

    grad = dot_tn(xg[0].reshape(rows, D), joined(0))
    for b in range(1, SPAN):
        grad = grad + dot_tn(xg[b].reshape(rows, D), joined(b))
    gq[...] = grad.astype(BF).reshape(gq.shape)
    height_q = gq.shape[1] // 4

    def lines(r):
        return pl.ds(pl.multiple_of(r * height_q, 16), height_q)

    def q_plane(m):
        p = plane[m]
        return far(
            gq.at[:, lines((p // 2) % 4), :], fours_q.at[m], send_p.at[count, m], recv_p.at[count, m], p, ka
        )

    def q_owner(i):
        z = (ka + i) % SPAN
        return far(sum_q.at[z], zq.at[ka], send_z.at[count, i - 1], recv_z.at[count, i - 1], pb, z)

    def q_landing(d, r):
        return fq.at[2 * d + core, lines(r)]

    def q_all(d, m):
        return far(fin_q.at[d], q_landing(d, rank), send_g.at[count + d, m], recv_g.at[count + d, m], plane[m], ka)

    def q_twin(d):
        ref = fq.at[2 * d + core]
        return far(ref, ref, send_c.at[count + d], recv_c.at[count + d], sibling, ka)

    for m in range(3):
        q_plane(m).start()

    for b in range(SPAN):
        own[b] = dot_nt(joined(b), weight).astype(BF).reshape(2, half, D)
        swap(b).start()

    for b in range(SPAN):
        swap(b).wait_recv()
        back[b] = (own[b, core].astype(F32) + mate[b].astype(F32)).astype(BF)
        mine = (core == side) & (ka == b)

        @pl.when(jnp.logical_not(mine))
        def _():
            home_copy(b).start()

        @pl.when(mine)
        def _():
            pltpu.make_async_copy(back.at[b], dxh.at[depth, core], recv_h.at[depth, core]).start()

    done = {(step, n) for _, step, n in HOOKS}

    def rest(step):
        for n in range(count):
            if (step, n) not in done:
                steps[step](n)

    rest("plane")
    for m in range(3):
        q_plane(m).wait_recv()
    mine_q = lines(rank)
    sum_q[...] = (
        gq[:, mine_q, :].astype(F32) + fours_q[0].astype(F32) + fours_q[1].astype(F32) + fours_q[2].astype(F32)
    ).astype(BF)
    for i in range(1, SPAN):
        q_owner(i).start()
    zq[ka] = sum_q[ka]
    rest("z")
    for i in range(1, SPAN):
        z = (ka - i) % SPAN
        far(zq.at[z], zq.at[z], send_z.at[count, i - 1], recv_z.at[count, i - 1], pb, z).wait_recv()
    for d in range(2):
        fin_q[d] = (zq[d].astype(F32) + zq[SPAN - 1 - d].astype(F32)).astype(BF)
    if outer > 1:
        merge_beyond(fin_q, slots_q, count)
    q_keep = [pltpu.make_async_copy(fin_q.at[d], q_landing(d, rank), keep_sem.at[count + d]) for d in range(2)]
    for d in range(2):
        q_keep[d].start()
        for m in range(3):
            q_all(d, m).start()
    rest("twin")
    for d in range(2):
        q_keep[d].wait()
        for m in range(3):
            got = q_landing(d, (plane[m] // 2) % 4)
            far(got, got, send_g.at[count + d, m], recv_g.at[count + d, m], pb, ka).wait_recv()
        q_twin(d).start()
    for d in range(2):
        got = fq.at[2 * d + 1 - core]
        far(got, got, send_c.at[count + d], recv_c.at[count + d], sibling, ka).wait_recv()
    for n in range(count):
        finish(n)
    for d in range(2):
        for k in range(2):
            far(back.at[0], dxh.at[d, k], send_h.at[0], recv_h.at[d, k], pb, ka).wait_recv()
    for m in range(3):
        q_plane(m).wait_send()
        for d in range(2):
            q_all(d, m).wait_send()
    for i in range(1, SPAN):
        q_owner(i).wait_send()
    for d in range(2):
        q_twin(d).wait_send()
    for n in range(SPAN):
        swap(n).wait_send()
        mine, remote = outgoing(n)

        @pl.when(jnp.logical_not(mine))
        def _():
            remote.wait_send()

        mine_b = (core == side) & (ka == n)

        @pl.when(jnp.logical_not(mine_b))
        def _():
            home_copy(n).wait_send()


HOOKS = (
    (1, "plane", 0),
    (4, "plane", 1),
    (5, "z", 0),
    (7, "plane", 2),
    (8, "z", 1),
    (8, "twin", 0),
    (10, "plane", 3),
    (11, "z", 2),
    (11, "twin", 1),
)


def backward_call(dah, xg, wq, q, k, v, ah, tot, starts, gd, gu, go):
    outer = lax.axis_size("pb") // 8
    rows = dah.shape[1]
    group = rows * SPAN
    count = len(CHUNKS)
    anyspace = pl.BlockSpec(memory_space=pl.ANY)
    vmem = pl.BlockSpec(memory_space=pltpu.VMEM)
    shape = jax.ShapeDtypeStruct
    dma = pltpu.SemaphoreType.DMA
    vm = pltpu.VMEM
    big = [(h, w) for _, _, h, _, w in CHUNKS]
    small = [(h // 4, w) for h, w in big]
    sq = (wq.shape[1] // 4, wq.shape[2])
    beyond = max(outer - 1, 1)
    held = max(outer, 1)
    spare = (16, 128)
    scratch = (
        [
            vm((SPAN, rows, WIDE), BF),
            vm(xg.shape, BF),
            vm(wq.shape, BF),
            vm(q.shape, BF),
            vm(q.shape, BF),
            vm(q.shape, BF),
            vm(q.shape, F32),
            vm(q.shape, F32),
            vm(q.shape, BF),
            vm((LOCAL, 8, group), F32),
            vm((group, HEAD), F32),
            vm((3, LOCAL, group, HEAD), BF),
            vm((SPAN, 2, rows // 2, D), BF),
            vm((SPAN, rows // 2, D), BF),
            vm((SPAN, rows // 2, D), BF),
            vm(wq.shape, BF),
        ]
        + [vm((SPAN,) + s, BF) for s in big]
        + [vm((SPAN,) + s, BF) for s in big]
        + [vm((3, SPAN) + s, BF) for s in small]
        + [vm((SPAN,) + s, BF) for s in small]
        + [vm((3,) + s, BF) for s in small]
        + [vm(s, BF) for s in small]
        + [vm((held,) + (s if outer > 1 else spare), BF) for s in small]
        + [
            vm((3, SPAN) + sq, BF),
            vm((SPAN,) + sq, BF),
            vm((SPAN,) + sq, BF),
            vm((2,) + sq, BF),
            vm((held, 2) + (sq if outer > 1 else spare), BF),
        ]
        + [
            dma((SPAN,)), dma((SPAN,)), dma((SPAN,)), dma((SPAN,)), dma((SPAN,)), dma((2, 2)), dma((7,)),
            dma((count,)), dma((count,)), dma((count,)), dma((count + 1, 3)), dma((count + 1, 3)),
            dma((count + 1, 3)), dma((count + 1, 3)), dma((count + 1, beyond)), dma((count + 1, beyond)),
            dma((count + 2, 3)), dma((count + 2, 3)), dma((count + 2,)), dma((count + 2,)), dma((count + 2,)),
        ]
    )
    return pl.pallas_call(
        functools.partial(backward_kernel, outer),
        out_shape=(
            shape((2, 2, rows // 2, D), BF),
            shape(gd.shape[1:], BF),
            shape(gu.shape[1:], BF),
            shape(go.shape[1:], BF),
            shape(wq.shape, BF),
        ),
        in_specs=[anyspace] * 8 + [vmem] + [anyspace] * 3,
        out_specs=(anyspace,) * 5,
        scratch_shapes=scratch,
        compiler_params=pltpu.CompilerParams(
            collective_id=1, has_side_effects=True, vmem_limit_bytes=60 << 20
        ),
        name="backward_attention",
    )(dah, xg, wq, q, k, v, ah, tot, starts, gd, gu, go)


def normalize(values):
    center = values - jnp.mean(values, axis=1, keepdims=True)
    inverse = lax.rsqrt(jnp.mean(center * center, axis=1, keepdims=True) + 1e-05)
    return center * inverse, inverse


def norm_back(cot, norm, inverse):
    return inverse * (
        cot - jnp.mean(cot, axis=1, keepdims=True) - norm * jnp.mean(cot * norm, axis=1, keepdims=True)
    )


def gelu_tanh(values):
    return jax.nn.gelu(values, approximate=True)


def body(layer_input, second_start, gain_attn, w_qkv, w_out, gain_mlp, w_up, w_down, d_output):
    rows = layer_input.shape[0]
    kv_index = lax.axis_index("ka")
    inputs32 = layer_input.astype(F32)
    norm_one, inverse_one = normalize(inputs32)
    attn_in = (norm_one * gain_attn).astype(BF)
    wq4 = w_qkv.reshape(D // SPAN, 3, SPAN, WIDE).transpose(2, 0, 1, 3).reshape(SPAN, D // SPAN, 3 * WIDE)
    start = jnp.full((8, 128), second_start[0].astype(F32), F32)
    (o_home, xg, wq, q, k, v, ah, tot, starts, wo_g, wu_g, wd_g) = forward_call(
        attn_in, wq4, start, w_out, w_up, w_down
    )
    full_out = wo_g.reshape(D, D)
    full_up = wu_g.reshape(D, -1)
    full_down = wd_g.reshape(-1, D)
    attn_low = o_home.transpose(1, 0, 2).reshape(rows, D)
    attn_branch = dot_nn(attn_low, full_out)
    middle = inputs32 + attn_branch
    norm_two, inverse_two = normalize(middle)
    mlp_in = (norm_two * gain_mlp).astype(BF)
    up_proj = dot_nn(mlp_in, full_up)
    activated = gelu_tanh(up_proj).astype(BF)
    mlp_branch = dot_nn(activated, full_down)
    output = (middle + mlp_branch).astype(BF)
    squares = jnp.stack(
        [jnp.sum(t * t) for t in (inputs32, attn_branch, middle, mlp_branch)]
    )
    d_act = dot_nt(d_output, full_down)
    d_w_down = dot_tn(activated, d_output).astype(BF)
    d_up = jax.vjp(gelu_tanh, up_proj)[1](d_act)[0].astype(BF)
    d_w_up = dot_tn(mlp_in, d_up).astype(BF)
    d_mlp_in = dot_nt(d_up, full_up)
    d_middle = d_output.astype(F32) + norm_back(d_mlp_in * gain_mlp, norm_two, inverse_two)
    g_middle = d_middle.astype(BF)
    d_w_out = dot_tn(attn_low, g_middle).astype(BF)
    d_attn = dot_nt(g_middle, full_out).astype(BF)
    dah = d_attn.reshape(rows, SPAN, WIDE).transpose(1, 0, 2)
    extra = jnp.zeros((SPAN, D // 12, D), BF)
    extra = extra.at[:, 0, 0].set(squares.astype(BF))
    go = jnp.concatenate([d_w_out.reshape(SPAN, D // SPAN, D), extra], axis=1)
    dxh, fd, fu, fo, fq = backward_call(
        dah, xg, wq, q, k, v, ah, tot, starts,
        d_w_down.reshape(SPAN, -1, D), d_w_up.reshape(SPAN, D // SPAN, -1), go,
    )
    d_attn_in = (dxh[0].astype(F32) + dxh[1].astype(F32)).reshape(rows, D)
    d_input = d_middle + norm_back(d_attn_in * gain_attn, norm_one, inverse_one)
    total_down = fd.astype(F32)
    total_up = fu.astype(F32)
    total_out = fo[: D // SPAN].astype(F32)
    total_qkv = (
        fq.reshape(SPAN, D // SPAN, 3, WIDE).transpose(1, 2, 0, 3).reshape(D // SPAN, 3 * D).astype(F32)
    )

    def gain_grad(weight, grad, gain):
        own = lax.dynamic_slice_in_dim(gain, kv_index * (D // SPAN), D // SPAN)
        return jnp.sum(weight.astype(F32) * grad, axis=1) / own

    total_gain_attn = gain_grad(w_qkv, total_qkv, gain_attn)
    total_gain_mlp = gain_grad(w_up, total_up, gain_mlp)
    entry_count = rows * SPAN * lax.axis_size("pb") * D
    rms = jnp.sqrt(fo[D // SPAN, 0:1].astype(F32) / entry_count)
    return (
        output, d_input, total_gain_attn, total_qkv, total_out, total_gain_mlp, total_up, total_down, rms,
    )


def solution(mesh):
    if mesh.shape["ka"] != SPAN or mesh.shape["pb"] % 8:
        raise ValueError("unsupported mesh")
    placed = (
        P(("pb", "ka"), None), P("pb"), P(), P("ka", None), P("ka", None), P(), P("ka", None), P("ka", None),
        P(("pb", "ka"), None),
    )
    return jax.shard_map(
        body,
        mesh=mesh,
        in_specs=placed,
        out_specs=(
            P(("pb", "ka"), None), P(("pb", "ka"), None), P("ka"), P("ka", None), P("ka", None), P("ka"),
            P("ka", None), P("ka", None), P("ka"),
        ),
        check_vma=False,
    )
```

```python
import functools
import math

import jax
import jax.numpy as jnp
from jax import lax
from jax.experimental import pallas as pl
from jax.experimental.pallas import tpu as pltpu
from jax.sharding import PartitionSpec as P

D = 768
HEADS = 12
HEAD = 64
SPAN = 4
LOCAL = HEADS // SPAN
WIDE = LOCAL * HEAD
LOG2E = 1.4426950408889634
MESH = pl.DeviceIdType.MESH
BF = jnp.bfloat16
F32 = jnp.float32


def mirror(depth, side):
    return depth + side * (SPAN - 1 - 2 * depth)


def neighbours(pb):
    across_x = pb + 2 - 4 * ((pb // 2) % 2)
    across_y = pb + 4 - 8 * ((pb // 4) % 2)
    across_both = across_x + 4 - 8 * ((across_x // 4) % 2)
    return across_x, across_y, across_both


def sibling_of(pb):
    return pb + 1 - 2 * (pb % 2)


def centred(values):
    center = values - jnp.mean(values, axis=1, keepdims=True)
    inverse = lax.rsqrt(jnp.mean(center * center, axis=1, keepdims=True) + 1e-05)
    return center * inverse, inverse


def norm_back(cot, norm, inverse):
    return inverse * (
        cot - jnp.mean(cot, axis=1, keepdims=True) - norm * jnp.mean(cot * norm, axis=1, keepdims=True)
    )


def far(src, dst, send_sem, recv_sem, pb, ka):
    return pltpu.make_async_remote_copy(
        src, dst, send_sem, recv_sem, device_id=(pb, ka), device_id_type=MESH
    )


def greet(peers):
    barrier = pltpu.get_barrier_semaphore()
    for peer in peers:
        pl.semaphore_signal(barrier, 1, device_id=peer, device_id_type=MESH)
    pl.semaphore_wait(barrier, len(peers))


def dot_nt(left, right):
    return lax.dot_general(left, right, (((1,), (1,)), ((), ())), preferred_element_type=F32)


def dot_tn(left, right):
    return lax.dot_general(left, right, (((0,), (0,)), ((), ())), preferred_element_type=F32)


def dot_nn(left, right):
    return jnp.dot(left, right, preferred_element_type=F32)


def fold_lanes(tile):
    out = tile[:, :128]
    for at in range(128, tile.shape[1], 128):
        out = out + tile[:, at : at + 128]
    return out


PIECES = (
    (0, 0, 192, 0, 384),
    (1, 0, 192, 0, 768),
    (1, 0, 192, 768, 768),
    (2, 0, 384, 0, 384),
    (2, 384, 384, 0, 384),
)
FORWARD_STEPS = (
    (),
    (("plane", 0),),
    (("plane", 1), ("pass", 0)),
    (("plane", 2),),
    (("pass", 1), ("across", 0)),
    (("plane", 3),),
)
AFTER_HEADS = (("pass", 2), ("plane", 4), ("across", 1), ("pass", 3), ("across", 2), ("pass", 4))
AFTER_BRANCH = (("across", 3), ("across", 4))
AFTER_NORM = ()


def forward_kernel(
    x_in, second, gain_one, w_qkv, gain_two, d_out, wo, wu, wd,
    output, mid_out, dah_out, gd_out, gu_out, go_out,
    xg_out, wq_out, q_out, k_out, v_out, ah_out, tot_out, start_out,
    xa, wq4, start, xg, wqs, qs, ks, vs, ahs, tots, ob, starts, ohome, wog, wug, wdg,
    mid, mlp_in, macc, dacc, gd, gu, go, dah, final,
    send_x, recv_x, send_q, recv_q, send_w, recv_w, send_s, recv_s, send_o, recv_o,
    send_z, recv_z, send_p, recv_p, send_c, recv_c, own_sem, out_sem, gd_sem, gu_sem,
):
    pb = lax.axis_index("pb")
    ka = lax.axis_index("ka")
    core = pb % 2
    base = pb - core
    side = ka // 2
    depth = mirror(ka, side)
    home_u = mirror(ka, core)
    quarter = 2 * depth + core
    sibling = sibling_of(pb)
    plane = neighbours(pb)
    rows = x_in.shape[0]
    rank = (pb // 2) % 4

    greet(
        [(pb, (ka + i) % SPAN) for i in range(1, SPAN)]
        + [(sibling, (ka + i) % SPAN) for i in range(SPAN)]
        + [(p, ka) for p in plane]
    )

    start[...] = jnp.full(start.shape, second[0].astype(F32), F32)
    for n in range(SPAN):
        for part in range(3):
            col = part * D + n * WIDE
            wq4[n, :, part * WIDE : (part + 1) * WIDE] = w_qkv[:, col : col + WIDE]
    height = wq4.shape[1] // 4

    def lines(ref, r):
        return ref.at[pl.ds(pl.multiple_of(r * height, 16), height)]

    out_q = []
    for i in range(1, SPAN):
        z = (ka + i) % SPAN
        zd = mirror(z, z // 2)
        out_q.append(
            far(
                lines(wq4.at[2 * zd + core], rank), lines(wqs.at[ka], rank),
                send_q.at[i - 1], recv_q.at[i - 1], pb, z,
            )
        )
    for copy in out_q:
        copy.start()
    own_q = pltpu.make_async_copy(wq4.at[quarter], wqs.at[ka], own_sem.at[0])
    own_q.start()

    step_rows = 128

    def first_norm(r, carry):
        at = pl.ds(pl.multiple_of(r * step_rows, step_rows), step_rows)
        norm, _ = centred(x_in[at, :].astype(F32))
        xa[at, :] = (norm * gain_one[...]).astype(BF)
        return carry

    lax.fori_loop(0, rows // step_rows, first_norm, 0)

    tick = rows // 4
    odd = (((home_u + 1) // 2) % 2) * (1 - home_u // 2)
    goal = mirror(1 - odd, core)
    out_x = [
        far(xa.at[pl.ds(t * tick, tick)], xg.at[ka, t], send_x.at[t], recv_x.at[ka, t], base + t // 2, goal)
        for t in (0, 2, 1, 3)
    ]
    for copy in out_x:
        copy.start()

    at_home = core == side

    def near_copies():
        return [
            far(xa.at[pl.ds(t * tick, tick)], xg.at[ka, t], send_x.at[4 + t], recv_x.at[ka, t], sibling, ka)
            for t in range(4)
        ]

    @pl.when(at_home)
    def _():
        for copy in near_copies():
            copy.start()
        for t in range(4):
            xg[ka, t] = xa[t * tick : (t + 1) * tick, :]

    def start_copies():
        out = []
        for n, (d, k) in enumerate(((0, 1), (1, 0), (1, 1))):
            target = base + (core + k) % 2
            out.append(far(start, starts, send_s.at[n], recv_s, target, mirror(d, core)))
        return out

    @pl.when(home_u == 0)
    def _():
        for copy in start_copies():
            copy.start()
        pltpu.make_async_copy(start, starts, recv_s).start()

    own_w = [
        pltpu.make_async_copy(src, dst.at[ka], own_sem.at[1 + n])
        for n, (src, dst) in enumerate(((wo, wog), (wu, wug), (wd, wdg)))
    ]

    arrays = ((wo, wog), (wu, wug), (wd, wdg))

    def area(n, ref, k, r=None):
        _, row0, height, col0, width = PIECES[n]
        at = pl.ds(pl.multiple_of(k * (ref.shape[-1] // 2) + col0, 128), width)
        if r is None:
            return ref.at[pl.ds(row0, height), at]
        return ref.at[pl.ds(pl.multiple_of(row0 + r * (height // 4), 16), height // 4), at]

    def z_copy(n, i):
        src, dst = arrays[PIECES[n][0]]
        return far(
            area(n, src, core, rank), area(n, dst.at[ka], core, rank),
            send_z.at[n, i - 1], recv_z.at[n, i - 1], pb, (ka + i) % SPAN,
        )

    def start_along_z():
        for n in range(len(PIECES)):
            for i in (2, 1, 3):
                z_copy(n, i).start()

    @pl.when(depth == 0)
    def _():
        start_along_z()

    for copy in own_w:
        copy.start()

    def chunk_copies(i, t):
        u = (1 - depth) if i == 0 else i + 1
        b = mirror(u, side)
        n = 2 * i + t
        t = 2 * core + t
        got = xg.at[b, t]
        here = far(got, got, send_x.at[8 + n], recv_x.at[b, t], pb, ka)
        onward = far(got, got, send_x.at[14 + n - 2], recv_x.at[b, t], pb, mirror(0, side)) if i else None
        return here, onward, far(got, got, send_x.at[8 + n], recv_x.at[b, t], sibling, ka)

    def pass_chunk(i, t, inner):
        here, onward, beside = chunk_copies(i, t)
        here.wait_recv()
        if inner and i:
            onward.start()
        beside.start()

    def beside_arrived(i):
        u = (1 - depth) if i == 0 else i + 1
        b = mirror(u, side)
        for t in range(2):
            got = xg.at[b, 2 * (1 - core) + t]
            far(got, got, send_x.at[8], recv_x.at[b, 2 * (1 - core) + t], pb, ka).wait_recv()

    for n in range(1, SPAN):
        mine_q = lines(wqs.at[(ka - n) % SPAN], rank)
        far(mine_q, mine_q, send_q.at[0], recv_q.at[n - 1], pb, ka).wait_recv()
        for m, p in enumerate(plane):
            copy = far(mine_q, mine_q, send_w.at[n - 1, m], recv_w.at[n - 1, m], p, ka)
            copy.start()
            out_q.append(copy)

    @pl.when(depth == 1)
    def _():
        pass_chunk(1, 0, True)
        pass_chunk(1, 1, True)

    pass_chunk(0, 0, False)
    pass_chunk(0, 1, False)
    for i in range(1, SPAN):
        for m, p in enumerate(plane):
            theirs = lines(wqs.at[(ka - i) % SPAN], (p // 2) % 4)
            far(theirs, theirs, send_w.at[i - 1, m], recv_w.at[i - 1, m], p, ka).wait_recv()
    own_q.wait()
    pltpu.make_async_copy(start, starts, recv_s).wait()

    def project(u):
        b = mirror(u, side)
        xb = xg[b].reshape(rows, D)
        at = pl.multiple_of(b * rows, rows)
        for dst, col in ((qs, 0), (ks, WIDE), (vs, 2 * WIDE)):
            w = wqs[:, :, col : col + WIDE].reshape(D, WIDE)
            out = dot_nn(xb, w).astype(BF)
            for h in range(LOCAL):
                dst[h, pl.ds(at, rows), :] = out[:, h * HEAD : (h + 1) * HEAD]

    def plane_copy(n, i, m, r, p):
        ref = area(n, arrays[PIECES[n][0]][1].at[(ka - i) % SPAN], core, r)
        return far(ref, ref, send_p.at[n, i - 1, m], recv_p.at[n, i - 1, m], p, ka)

    def rank_of(m):
        return (plane[m] // 2) % 4

    def begin_plane(n):
        for i in range(1, SPAN):
            z_copy(n, i).wait_recv()
            for m in range(2):
                plane_copy(n, i, m, rank, plane[m]).start()

    def pass_on(n):
        first = n % 2
        for i in range(1, SPAN):
            plane_copy(n, i, first, rank_of(first), pb).wait_recv()
            plane_copy(n, i, 2, rank_of(first), plane[1 - first]).start()

    def across_copy(n, i):
        ref = area(n, arrays[PIECES[n][0]][1].at[(ka - i) % SPAN], core)
        return far(ref, ref, send_c.at[n, i - 1], recv_c.at[n, i - 1], sibling, ka)

    def begin_across(n):
        other = 1 - n % 2
        for i in range(1, SPAN):
            plane_copy(n, i, other, rank_of(other), pb).wait_recv()
            plane_copy(n, i, 2, rank_of(2), pb).wait_recv()
            across_copy(n, i).start()

    def arrived(n):
        for i in range(1, SPAN):
            ref = area(n, arrays[PIECES[n][0]][1].at[(ka - i) % SPAN], 1 - core)
            far(ref, ref, send_c.at[n, i - 1], recv_c.at[n, i - 1], pb, ka).wait_recv()

    def weights_sent():
        for n in range(len(PIECES)):
            for i in range(1, SPAN):
                z_copy(n, i).wait_send()
                for m in range(3):
                    plane_copy(n, i, m, rank, pb).wait_send()
                across_copy(n, i).wait_send()

    scale = LOG2E / math.sqrt(HEAD)
    one = jnp.where(starts[0:1, 0:1] > (SPAN // 2) * rows + 0.5, 1.0, 0.0)
    sub = 256

    def attend_own(u):
        b = mirror(u, side)

        def head(h, carry):
            for part in range(rows // sub):
                width = (part + 1) * sub
                at = pl.multiple_of(b * rows, rows)
                row0 = pl.multiple_of(b * rows + part * sub, sub)
                s = dot_nt(qs[h, pl.ds(row0, sub), :], ks[h, pl.ds(at, width), :]) * scale
                seen = (
                    lax.broadcasted_iota(jnp.int32, (sub, width), 0) + part * sub
                    >= lax.broadcasted_iota(jnp.int32, (sub, width), 1)
                )
                up = jnp.where(seen, jnp.exp2(s - 1.0), 0.0)
                down = jnp.where(seen, jnp.exp2(-s - 1.0), 0.0)
                tots[h, pl.ds(row0, sub), :] = fold_lanes(up + down)
                ahs[h, pl.ds(row0, sub), :] = dot_nn((up - down).astype(BF), vs[h, pl.ds(at, width), :])
            return carry

        lax.fori_loop(0, LOCAL, head, 0)

    def attend_pair(high, low):
        qb = high + side * (SPAN - 1 - low - high)
        kb = low + side * (SPAN - 1 - low - high)
        same = jnp.where(qb // 2 == kb // 2, 1.0, 0.0)
        keep = jnp.maximum(one, same) > 0.5

        def head(h, carry):
            at = pl.multiple_of(kb * rows, rows)
            for part in range(rows // sub):
                row0 = pl.multiple_of(qb * rows + part * sub, sub)
                s = dot_nt(qs[h, pl.ds(row0, sub), :], ks[h, pl.ds(at, rows), :]) * scale
                up, down = jnp.exp2(s - 1.0), jnp.exp2(-s - 1.0)
                tots[h, pl.ds(row0, sub), :] += jnp.where(keep, fold_lanes(up + down), 0.0)
                ahs[h, pl.ds(row0, sub), :] += jnp.where(
                    keep, dot_nn((up - down).astype(BF), vs[h, pl.ds(at, rows), :]), 0.0
                )
            return carry

        lax.fori_loop(0, LOCAL, head, 0)

    actions = {"plane": begin_plane, "pass": pass_on, "across": begin_across}

    def run_steps(todo):
        for step, n in todo:
            actions[step](n)

    def home_copy(b):
        return far(ob.at[b], ohome.at[quarter], send_o.at[b], recv_o.at[quarter], base + side, b)

    def send_home(u):
        b = mirror(u, side)
        at = pl.ds(pl.multiple_of(b * rows, rows), rows)
        done = []
        for h in range(LOCAL):
            total = jnp.sum(tots[h, at, :], axis=1, keepdims=True)
            heads = ahs[h, at, :] / total
            ahs[h, at, :] = heads
            tots[h, at, :] = jnp.broadcast_to(total, (rows, 128))
            done.append(heads)
        ob[b] = jnp.concatenate(done, axis=1).astype(BF)
        mine = (core == side) & (ka == b)

        @pl.when(jnp.logical_not(mine))
        def _():
            home_copy(b).start()

        @pl.when(mine)
        def _():
            pltpu.make_async_copy(ob.at[b], ohome.at[quarter], recv_o.at[quarter]).start()

    @pl.when(jnp.logical_not(at_home))
    def _():
        for t in range(4):
            far(xg.at[ka, t], xg.at[ka, t], send_x.at[8], recv_x.at[ka, t], pb, ka).wait_recv()

    project(depth)
    attend_own(depth)

    @pl.when(depth == 1)
    def _():
        pass_chunk(2, 0, True)
        pass_chunk(2, 1, True)
        start_along_z()

    run_steps(FORWARD_STEPS[0])
    beside_arrived(0)
    project(1 - depth)
    attend_own(1 - depth)
    attend_pair(1, 0)

    @pl.when(side == 0)
    def _():
        send_home(0)
        send_home(1)

    run_steps(FORWARD_STEPS[1])

    @pl.when(depth == 0)
    def _():
        pass_chunk(1, 0, False)
        pass_chunk(1, 1, False)

    beside_arrived(1)
    project(2)
    attend_own(2)
    attend_pair(2, 1)
    attend_pair(2, 0)

    @pl.when(side == 0)
    def _():
        send_home(2)

    run_steps(FORWARD_STEPS[2])

    @pl.when(depth == 0)
    def _():
        pass_chunk(2, 0, False)
        pass_chunk(2, 1, False)

    beside_arrived(2)
    project(3)
    attend_own(3)

    @pl.when(side == 1)
    def _():
        send_home(3)

    for low in (2, 1, 0):
        attend_pair(3, low)

        @pl.when(side == 1)
        def _(low=low):
            send_home(low)

        run_steps(FORWARD_STEPS[5 - low])

    @pl.when(side == 0)
    def _():
        send_home(3)

    saves = [
        pltpu.make_async_copy(src, dst, out_sem.at[n])
        for n, (src, dst) in enumerate(
            (
                (xg, xg_out), (wqs, wq_out), (qs, q_out), (ks, k_out), (vs, v_out),
                (ahs, ah_out), (tots, tot_out), (starts, start_out),
            )
        )
    ]
    for copy in saves:
        copy.start()

    run_steps(AFTER_HEADS)
    own_w[0].wait()
    arrived(0)
    for n in range(SPAN):
        far(ob.at[0], ohome.at[n], send_o.at[0], recv_o.at[n], pb, ka).wait_recv()

    branch = dot_nn(ohome[0], wog[0])
    for n in range(1, SPAN):
        branch = branch + dot_nn(ohome[n], wog[n])
    mid[...] = branch
    run_steps(AFTER_BRANCH)

    def second_norm(r, sums):
        at = pl.ds(pl.multiple_of(r * step_rows, step_rows), step_rows)
        x32 = x_in[at, :].astype(F32)
        term = mid[at, :]
        middle = x32 + term
        norm, _ = centred(middle)
        mid[at, :] = middle
        mlp_in[at, :] = (norm * gain_two[...]).astype(BF)
        return tuple(
            s + fold_lanes(jnp.sum(t * t, axis=0, keepdims=True))
            for s, t in zip(sums, (x32, term, middle))
        )

    zero = jnp.zeros((1, 128), F32)
    sums = lax.fori_loop(0, rows // step_rows, second_norm, (zero, zero, zero))
    run_steps(AFTER_NORM)
    for n in range(1, len(PIECES)):
        arrived(n)
    own_w[1].wait()
    own_w[2].wait()
    macc[...] = jnp.zeros_like(macc)
    dacc[...] = jnp.zeros_like(dacc)

    def store_pair(f, slot):
        cols = pl.ds(pl.multiple_of(f * D, D), D)
        return (
            pltpu.make_async_copy(gd.at[slot], gd_out.at[f], gd_sem.at[slot]),
            pltpu.make_async_copy(gu.at[slot], gu_out.at[:, :, cols], gu_sem.at[slot]),
        )

    root = math.sqrt(2.0 / math.pi)

    def feed(f, carry):
        slot = f % 2
        w_up = wug[:, :, pl.ds(pl.multiple_of(f * D, D), D)].reshape(D, D)
        w_down = wdg[f]
        up = dot_nn(mlp_in[...], w_up)
        bend = jnp.tanh(root * (up + 0.044715 * (up * up * up)))
        act = (0.5 * up * (1.0 + bend)).astype(BF)
        slope = 0.5 * (1.0 + bend) + 0.5 * up * (1.0 - bend * bend) * (root * (1.0 + 0.134145 * (up * up)))
        macc[...] += dot_nn(act, w_down)
        d_up = (slope * dot_nt(d_out[...], w_down)).astype(BF)
        dacc[...] += dot_nt(d_up, w_up)

        @pl.when(f >= 2)
        def _():
            for copy in store_pair(f - 2, slot):
                copy.wait()

        gd[slot] = dot_tn(act, d_out[...]).astype(BF)
        gu[slot] = dot_tn(mlp_in[...], d_up).astype(BF).reshape(gu.shape[1:])
        for copy in store_pair(f, slot):
            copy.start()
        return carry

    lax.fori_loop(0, SPAN, feed, 0)

    def finish_rows(r, total):
        at = pl.ds(pl.multiple_of(r * step_rows, step_rows), step_rows)
        middle = mid[at, :]
        norm, inverse = centred(middle)
        term = macc[at, :]
        final[at, :] = (middle + term).astype(BF)
        d_middle = d_out[at, :].astype(F32) + norm_back(dacc[at, :] * gain_two[...], norm, inverse)
        mid[at, :] = d_middle
        mlp_in[at, :] = d_middle.astype(BF)
        return total + fold_lanes(jnp.sum(term * term, axis=0, keepdims=True))

    last = lax.fori_loop(0, rows // step_rows, finish_rows, zero)
    ends = [
        pltpu.make_async_copy(src, dst, out_sem.at[8 + n])
        for n, (src, dst) in enumerate(((mid, mid_out), (final, output)))
    ]
    for copy in ends:
        copy.start()
    corner = (lax.broadcasted_iota(jnp.int32, (64, D), 0) == 0) & (
        lax.broadcasted_iota(jnp.int32, (64, D), 1) == 0
    )
    for n in range(SPAN):
        dah[n] = dot_nt(mlp_in[...], wog[n]).astype(BF)
        go[n, : D // SPAN, :] = dot_tn(ohome[n], mlp_in[...]).astype(BF)
        value = jnp.sum((sums + (last,))[n], axis=1, keepdims=True)
        go[n, D // SPAN :, :] = jnp.where(corner, value, 0.0).astype(BF)
    ends += [
        pltpu.make_async_copy(src, dst, out_sem.at[10 + n])
        for n, (src, dst) in enumerate(((dah, dah_out), (go, go_out)))
    ]
    for copy in ends[2:]:
        copy.start()
    for f in range(2, SPAN):
        for copy in store_pair(f, f % 2):
            copy.wait()
    for copy in saves + ends:
        copy.wait()
    for copy in out_x + out_q:
        copy.wait_send()
    weights_sent()
    for i in range(3):
        for t in range(2):
            _, onward, beside = chunk_copies(i, t)
            beside.wait_send()
            if i:

                @pl.when(depth == 1)
                def _(onward=onward):
                    onward.wait_send()

    @pl.when(at_home)
    def _():
        for copy in near_copies():
            copy.wait_send()

    @pl.when(home_u == 0)
    def _():
        for copy in start_copies():
            copy.wait_send()

    for b in range(SPAN):
        mine = (core == side) & (ka == b)

        @pl.when(jnp.logical_not(mine))
        def _(b=b):
            home_copy(b).wait_send()


def forward_call(x_in, second, gain_one, w_qkv, gain_two, d_out, wo, wu, wd):
    rows = x_in.shape[0]
    group = rows * SPAN
    anyspace = pl.BlockSpec(memory_space=pl.ANY)
    vmem = pl.BlockSpec(memory_space=pltpu.VMEM)
    shape = jax.ShapeDtypeStruct
    dma = pltpu.SemaphoreType.DMA
    vm = pltpu.VMEM
    count = len(PIECES)
    tokens = (SPAN, 4, rows // 4, D)
    columns = (SPAN, D // SPAN, 3 * WIDE)
    heads = (LOCAL, group, HEAD)
    outs = (
        shape((rows, D), BF),
        shape((rows, D), F32),
        shape((SPAN, rows, WIDE), BF),
        shape((SPAN, D, D), BF),
        shape((SPAN, D // SPAN, SPAN * D), BF),
        shape((SPAN, D // SPAN + 64, D), BF),
        shape(tokens, BF),
        shape(columns, BF),
        shape(heads, BF),
        shape(heads, BF),
        shape(heads, BF),
        shape(heads, F32),
        shape((LOCAL, group, 128), F32),
        shape((8, 128), F32),
    )
    scratch = [
        vm((rows, D), BF),
        vm(columns, BF),
        vm((8, 128), F32),
        vm(tokens, BF),
        vm(columns, BF),
        vm(heads, BF),
        vm(heads, BF),
        vm(heads, BF),
        vm(heads, F32),
        vm((LOCAL, group, 128), F32),
        vm((SPAN, rows, WIDE), BF),
        vm((8, 128), F32),
        vm((SPAN, rows, WIDE), BF),
        vm((SPAN,) + wo.shape, BF),
        vm((SPAN,) + wu.shape, BF),
        vm((SPAN,) + wd.shape, BF),
        vm((rows, D), F32),
        vm((rows, D), BF),
        vm((rows, D), F32),
        vm((rows, D), F32),
        vm((2, D, D), BF),
        vm((2, SPAN, D // SPAN, D), BF),
        vm((SPAN, D // SPAN + 64, D), BF),
        vm((SPAN, rows, WIDE), BF),
        vm((rows, D), BF),
        dma((18,)), dma((SPAN, 4)), dma((3,)), dma((3,)), dma((3, 3)), dma((3, 3)), dma((3,)), dma,
        dma((SPAN,)), dma((SPAN,)),
        dma((count, 3)), dma((count, 3)), dma((count, 3, 3)), dma((count, 3, 3)), dma((count, 3)), dma((count, 3)),
        dma((4,)), dma((12,)), dma((2,)), dma((2,)),
    ]
    return pl.pallas_call(
        forward_kernel,
        out_shape=outs,
        in_specs=[vmem, pl.BlockSpec(memory_space=pltpu.SMEM), vmem, vmem, vmem, vmem] + [anyspace] * 3,
        out_specs=(anyspace,) * len(outs),
        scratch_shapes=scratch,
        compiler_params=pltpu.CompilerParams(
            collective_id=0, has_side_effects=True, vmem_limit_bytes=60 << 20
        ),
        name="forward_layer",
    )(x_in, second, gain_one, w_qkv, gain_two, d_out, wo, wu, wd)


CHUNKS = (
    (0, 0, 384, 0, 384),
    (0, 384, 384, 0, 384),
    (1, 0, 192, 0, 768),
    (1, 0, 192, 768, 768),
    (2, 0, 256, 0, 384),
)


def backward_kernel(
    outer, dah, xg_in, wq_in, q_in, k_in, v_in, ah_in, tot_in, starts, gd, gu, go, x_in, gain_one, mid_in,
    d_input, fd, fu, fo, qkv_out,
    da, xg, wqs, qs, ks, vs, dms, deltas, dqs, dks, dvs, joint, own, mate, back, grad_q, gq,
    x_own, mid, dxh, fq, qkv,
    *refs,
):
    count = len(CHUNKS)
    halves, mates, firsts, seconds, zs, fins, slots = (refs[i * count : (i + 1) * count] for i in range(7))
    refs = refs[7 * count :]
    fours_q, sum_q, zq, fin_q, slots_q = refs[:5]
    (
        send_a, recv_a, send_m, recv_m, send_h, recv_h, in_sem, out_sem,
        own_sem, send_n, recv_n, send_p, recv_p, send_z, recv_z, send_o, recv_o,
        send_g, recv_g, send_c, recv_c, keep_sem,
    ) = refs[5:]
    pb = lax.axis_index("pb")
    ka = lax.axis_index("ka")
    core = pb % 2
    base = pb - core
    side = ka // 2
    depth = mirror(ka, side)
    sibling = sibling_of(pb)
    plane = neighbours(pb)
    rank = (pb // 2) % 4
    where = pb // 8
    beyond = [(pb + 8 * o) % (8 * outer) for o in range(1, outer)]
    rows = dah.shape[1]
    half = rows // 2

    greet(
        [(pb, (ka + i) % SPAN) for i in range(1, SPAN)]
        + [(sibling, (ka + i) % SPAN) for i in range(SPAN)]
        + [(p, ka) for p in plane]
        + [(p, ka) for p in beyond]
    )

    def outgoing(n):
        worker_depth, worker_core = n // 2, n % 2
        target, spot = base + worker_core, mirror(worker_depth, core)
        mine = (target == pb) & (spot == ka)
        return mine, far(dah.at[n], da.at[ka], send_a.at[n], recv_a.at[ka], target, spot)

    for n in range(SPAN):
        mine, remote = outgoing(n)

        @pl.when(jnp.logical_not(mine))
        def _():
            remote.start()

        @pl.when(mine)
        def _():
            pltpu.make_async_copy(dah.at[n], da.at[ka], recv_a.at[ka]).start()

    sources = (gd, gu, go)
    results = (fd, fu, fo)

    def block_of(ref, n, k, row0, height):
        _, _, _, col0, width = CHUNKS[n]
        at = pl.multiple_of(k * (ref.shape[-1] // 2) + col0, 128)
        return pl.ds(row0, height), pl.ds(at, width)

    def source(n, k):
        a, row0, height, _, _ = CHUNKS[n]
        r, c = block_of(sources[a], n, k, row0, height)
        return sources[a].at[:, r, c]

    def quarter(n, r):
        height = CHUNKS[n][2] // 4
        return pl.ds(pl.multiple_of(r * height, 16), height)

    def landing(n, r):
        a, row0, height, _, _ = CHUNKS[n]
        rr, c = block_of(results[a], n, core, pl.multiple_of(row0 + r * (height // 4), 16), height // 4)
        return results[a].at[rr, c]

    def strip(n, k):
        a, row0, height, _, _ = CHUNKS[n]
        r, c = block_of(results[a], n, k, row0, height)
        return results[a].at[r, c]

    def local_half(n):
        return pltpu.make_async_copy(source(n, core), halves[n], own_sem.at[n])

    def to_sibling(n):
        return far(source(n, 1 - core), mates[n], send_n.at[n], recv_n.at[n], sibling, ka)

    def rank_of(m):
        return (plane[m] // 2) % 4

    def to_first(n, m):
        first = n % 2
        r = rank_of((first, 2)[m])
        return far(
            halves[n].at[:, quarter(n, r), :], firsts[n].at[m], send_p.at[n, m], recv_p.at[n, m], plane[first], ka
        )

    def to_second(n):
        other = 1 - n % 2
        return far(
            halves[n].at[:, quarter(n, rank_of(other)), :], seconds[n], send_p.at[n, 2], recv_p.at[n, 2],
            plane[other], ka,
        )

    def to_owner(n, i):
        z = (ka + i) % SPAN
        return far(
            halves[n].at[z, quarter(n, rank), :], zs[n].at[i - 1], send_z.at[n, i - 1], recv_z.at[n, i - 1], pb, z
        )

    def keep(n):
        return pltpu.make_async_copy(fins[n], landing(n, rank), keep_sem.at[n])

    def to_all(n, m):
        return far(fins[n], landing(n, rank), send_g.at[n, m], recv_g.at[n, m], plane[m], ka)

    def to_twin(n):
        return far(strip(n, core), strip(n, core), send_c.at[n], recv_c.at[n], sibling, ka)

    def merge_sibling(n):
        local_half(n).wait()
        to_sibling(n).wait_recv()

        def add(z, carry):
            halves[n][z] = (halves[n][z].astype(F32) + mates[n][z].astype(F32)).astype(BF)
            return carry

        lax.fori_loop(0, SPAN, add, 0)
        for m in (1, 0):
            to_first(n, m).start()

    def merge_first(n):
        for m in (1, 0):
            to_first(n, m).wait_recv()
            held = quarter(n, (rank, rank_of(1 - n % 2))[m])

            def add(z, carry):
                halves[n][z, held, :] = (halves[n][z, held, :].astype(F32) + firsts[n][m, z].astype(F32)).astype(BF)
                return carry

            lax.fori_loop(0, SPAN, add, 0)
            if m:
                to_second(n).start()

    def merge_second(n):
        to_second(n).wait_recv()
        held = quarter(n, rank)

        def add(z, carry):
            halves[n][z, held, :] = (halves[n][z, held, :].astype(F32) + seconds[n][z].astype(F32)).astype(BF)
            return carry

        lax.fori_loop(0, SPAN, add, 0)
        for i in (2, 1, 3):
            to_owner(n, i).start()

    def merge_beyond(fin, slot, n):
        for o, p in enumerate(beyond):
            far(fin, slot.at[where], send_o.at[n, o], recv_o.at[n, o], p, ka).start()
        slot[where] = fin[...]
        for o in range(outer - 1):
            far(slot.at[0], slot.at[0], send_o.at[n, o], recv_o.at[n, o], pb, ka).wait()
        total = slot[0].astype(F32)
        for o in range(1, outer):
            total = total + slot[o].astype(F32)
        fin[...] = total.astype(BF)

    def merge_z(n):
        for i in range(1, SPAN):
            to_owner(n, i).wait_recv()
        total = halves[n][ka, quarter(n, rank), :].astype(F32)
        for i in range(3):
            total = total + zs[n][i].astype(F32)
        fins[n][...] = total.astype(BF)
        if outer > 1:
            merge_beyond(fins[n], slots[n], n)
        keep(n).start()
        for m in range(3):
            to_all(n, m).start()

    def pass_twin(n):
        keep(n).wait()
        for m in range(3):
            got = landing(n, (plane[m] // 2) % 4)
            far(got, got, send_g.at[n, m], recv_g.at[n, m], pb, ka).wait_recv()
        to_twin(n).start()

    def finish(n):
        got = strip(n, 1 - core)
        far(got, got, send_c.at[n], recv_c.at[n], sibling, ka).wait_recv()
        to_sibling(n).wait_send()
        for m in range(3):
            to_all(n, m).wait_send()
        for m in range(2):
            to_first(n, m).wait_send()
        to_second(n).wait_send()
        for i in range(1, SPAN):
            to_owner(n, i).wait_send()
        to_twin(n).wait_send()

    for n in range(count):
        local_half(n).start()
        to_sibling(n).start()

    loads = [
        pltpu.make_async_copy(src, dst, in_sem.at[n])
        for n, (src, dst) in enumerate(
            (
                (ah_in, dks), (tot_in, dvs), (q_in, qs), (k_in, ks), (v_in, vs), (xg_in, xg), (wq_in, wqs),
                (x_in, x_own), (mid_in, mid),
            )
        )
    ]
    for copy in loads:
        copy.start()
    dqs[...] = jnp.zeros_like(dqs)

    for n in range(count):
        merge_sibling(n)

    for copy in loads[:5]:
        copy.wait()
    for b in range(SPAN):
        far(dah.at[0], da.at[b], send_a.at[0], recv_a.at[b], pb, ka).wait_recv()

    scale = LOG2E / math.sqrt(HEAD)
    unit = 1.0 / math.sqrt(HEAD)
    one = jnp.where(starts[0:1, 0:1] > (SPAN // 2) * rows + 0.5, 1.0, 0.0)
    sub = 256

    for b in range(SPAN):
        block = da[b].astype(F32)
        for h in range(LOCAL):
            rows_b = slice(b * rows, (b + 1) * rows)
            scaled = block[:, h * HEAD : (h + 1) * HEAD] / dvs[h, rows_b, :HEAD]
            dms[h, rows_b, :] = scaled.astype(BF)
            deltas[h, :, rows_b] = lax.dot_general(
                jnp.ones((8, HEAD), F32), scaled * dks[h, rows_b, :],
                (((1,), (1,)), ((), ())), precision=lax.Precision.HIGHEST, preferred_element_type=F32,
            )
            dvs[h, rows_b, :] = jnp.zeros((rows, 128), F32)
            dks[h, rows_b, :] = jnp.zeros((rows, HEAD), F32)

    def tile(h, row0, height, at, width, seen=None, keep_it=None):
        q = qs[h, pl.ds(row0, height), :]
        dm = dms[h, pl.ds(row0, height), :]
        keys = ks[h, pl.ds(at, width), :]
        s = dot_nt(keys, q) * scale
        up, down = jnp.exp2(s - 1.0), jnp.exp2(-s - 1.0)
        if seen is not None:
            up = jnp.where(seen, up, 0.0)
            down = jnp.where(seen, down, 0.0)
        expo, sine = up + down, up - down
        dsig = dot_nt(vs[h, pl.ds(at, width), :], dm)
        delta = deltas[h, 0:1, pl.ds(row0, height)]
        ds = (expo * dsig - sine * delta).astype(BF)
        dk, dv, dq = dot_nn(ds, q), dot_nn(sine.astype(BF), dm), dot_tn(ds, keys)
        if keep_it is not None:
            dk, dv, dq = (jnp.where(keep_it, t, 0.0) for t in (dk, dv, dq))
        dks[h, pl.ds(at, width), :] += dk
        dvs[h, pl.ds(at, width), :HEAD] += dv
        dqs[h, pl.ds(row0, height), :] += dq

    def attend_own(u):
        b = mirror(u, side)

        def head(h, carry):
            for part in range(rows // sub):
                height = rows - part * sub
                at = pl.multiple_of(b * rows + part * sub, sub)
                seen = lax.broadcasted_iota(jnp.int32, (sub, height), 0) <= lax.broadcasted_iota(
                    jnp.int32, (sub, height), 1
                )
                tile(h, at, height, at, sub, seen=seen)
            return carry

        lax.fori_loop(0, LOCAL, head, 0)

    def attend_pair(high, low):
        qb = high + side * (SPAN - 1 - low - high)
        kb = low + side * (SPAN - 1 - low - high)
        same = jnp.where(qb // 2 == kb // 2, 1.0, 0.0)
        keep_it = jnp.maximum(one, same) > 0.5

        def head(h, carry):
            for part in range(rows // sub):
                tile(
                    h, pl.multiple_of(qb * rows, rows), rows,
                    pl.multiple_of(kb * rows + part * sub, sub), sub, keep_it=keep_it,
                )
            return carry

        lax.fori_loop(0, LOCAL, head, 0)

    def home_copy(b):
        return far(back.at[b], dxh.at[depth, core], send_h.at[b], recv_h.at[depth, core], base + side, b)

    def swap(u):
        return far(own.at[u % 2, 1 - core], mate.at[u], send_m.at[u], recv_m.at[u], sibling, ka)

    half = rows // 2

    def block_done(u):
        b = mirror(u, side)
        at = pl.ds(pl.multiple_of(b * rows, rows), rows)
        joint[...] = jnp.concatenate(
            [(dqs[h, at, :] * unit).astype(BF) for h in range(LOCAL)]
            + [(dks[h, at, :] * unit).astype(BF) for h in range(LOCAL)]
            + [dvs[h, at, :HEAD].astype(BF) for h in range(LOCAL)],
            axis=1,
        )
        if u < 2:
            swap(u + 2).wait_send()
        own[u % 2] = dot_nt(joint[...], wqs[...].reshape(D, 3 * WIDE)).astype(BF).reshape(2, half, D)
        swap(u).start()
        part = dot_tn(xg[b].reshape(rows, D), joint[...])
        if u == SPAN - 1:
            grad_q[...] = part
        else:
            grad_q[...] += part

    def send_home(u):
        b = mirror(u, side)
        swap(u).wait_recv()
        back[b] = (own[u % 2, core].astype(F32) + mate[u].astype(F32)).astype(BF)
        mine = (core == side) & (ka == b)

        @pl.when(jnp.logical_not(mine))
        def _():
            home_copy(b).start()

        @pl.when(mine)
        def _():
            pltpu.make_async_copy(back.at[b], dxh.at[depth, core], recv_h.at[depth, core]).start()

    steps = {"first": merge_first, "second": merge_second, "z": merge_z, "twin": pass_twin, "home": send_home}
    todo = [list(row) for row in BACKWARD_STEPS]

    def run_next():
        for step, n in todo.pop(0):
            steps[step](n)

    run_next()
    loads[5].wait()
    loads[6].wait()
    for high in range(SPAN - 1, -1, -1):
        attend_own(high)
        run_next()
        for low in range(high - 1, -1, -1):
            attend_pair(high, low)
            run_next()
        block_done(high)
    gq[...] = grad_q[...].astype(BF).reshape(gq.shape)
    height_q = gq.shape[1] // 4

    def lines(r):
        return pl.ds(pl.multiple_of(r * height_q, 16), height_q)

    def q_plane(m):
        return far(
            gq.at[:, lines(rank_of(m)), :], fours_q.at[m], send_p.at[count, m], recv_p.at[count, m], plane[m], ka
        )

    def q_owner(i):
        z = (ka + i) % SPAN
        return far(sum_q.at[z], zq.at[ka], send_z.at[count, i - 1], recv_z.at[count, i - 1], pb, z)

    def q_landing(d, r):
        return fq.at[2 * d + core, lines(r)]

    def q_all(d, m):
        return far(fin_q.at[d], q_landing(d, rank), send_g.at[count + d, m], recv_g.at[count + d, m], plane[m], ka)

    def q_twin(d):
        ref = fq.at[2 * d + core]
        return far(ref, ref, send_c.at[count + d], recv_c.at[count + d], sibling, ka)

    for m in range(3):
        q_plane(m).start()
    send_home(0)
    run_next()

    for m in range(3):
        q_plane(m).wait_recv()
    mine_q = lines(rank)
    sum_q[...] = (
        gq[:, mine_q, :].astype(F32) + fours_q[0].astype(F32) + fours_q[1].astype(F32) + fours_q[2].astype(F32)
    ).astype(BF)
    for i in (2, 1, 3):
        q_owner(i).start()
    zq[ka] = sum_q[ka]
    run_next()
    for d in range(2):
        for k in range(2):
            far(back.at[0], dxh.at[d, k], send_h.at[0], recv_h.at[d, k], pb, ka).wait_recv()
    loads[7].wait()
    loads[8].wait()
    step_rows = 128

    def input_rows(r, carry):
        at = pl.ds(pl.multiple_of(r * step_rows, step_rows), step_rows)
        inner = pl.ds(pl.multiple_of((r % 2) * step_rows, step_rows), step_rows)
        cot = dxh[0, r // 2, inner, :].astype(F32) + dxh[1, r // 2, inner, :].astype(F32)
        norm, inverse = centred(x_own[at, :].astype(F32))
        mid[at, :] = mid[at, :] + norm_back(cot * gain_one[...], norm, inverse)
        return carry

    lax.fori_loop(0, rows // step_rows, input_rows, 0)
    out_copy = pltpu.make_async_copy(mid, d_input, out_sem.at[0])
    out_copy.start()
    for i in range(1, SPAN):
        z = (ka - i) % SPAN
        far(zq.at[z], zq.at[z], send_z.at[count, i - 1], recv_z.at[count, i - 1], pb, z).wait_recv()
    for d in range(2):
        fin_q[d] = (zq[d].astype(F32) + zq[SPAN - 1 - d].astype(F32)).astype(BF)
    if outer > 1:
        merge_beyond(fin_q, slots_q, count)
    for d in range(2):
        fq[2 * d + core, lines(rank), :] = fin_q[d]
        for m in range(3):
            q_all(d, m).start()
    run_next()
    for d in range(2):
        for m in range(3):
            got = q_landing(d, rank_of(m))
            far(got, got, send_g.at[count + d, m], recv_g.at[count + d, m], pb, ka).wait_recv()
        q_twin(d).start()
    for d in range(2):
        got = fq.at[2 * d + 1 - core]
        far(got, got, send_c.at[count + d], recv_c.at[count + d], sibling, ka).wait_recv()
    for n in range(SPAN):
        for part in range(3):
            col = part * D + n * WIDE
            qkv[:, col : col + WIDE] = fq[n, :, part * WIDE : (part + 1) * WIDE].astype(F32)
    qkv_copy = pltpu.make_async_copy(qkv, qkv_out, out_sem.at[1])
    qkv_copy.start()
    for n in range(count):
        finish(n)
    for m in range(3):
        q_plane(m).wait_send()
        for d in range(2):
            q_all(d, m).wait_send()
    for i in range(1, SPAN):
        q_owner(i).wait_send()
    for d in range(2):
        q_twin(d).wait_send()
        swap(d).wait_send()
    for n in range(SPAN):
        mine, remote = outgoing(n)

        @pl.when(jnp.logical_not(mine))
        def _():
            remote.wait_send()

        mine_b = (core == side) & (ka == n)

        @pl.when(jnp.logical_not(mine_b))
        def _():
            home_copy(n).wait_send()

    out_copy.wait()
    qkv_copy.wait()


BACKWARD_STEPS = (
    (("first", 0), ("first", 1)),
    (),
    (("second", 0), ("second", 1)),
    (("first", 2), ("first", 3)),
    (("z", 0), ("z", 1)),
    (("home", 3),),
    (("second", 2), ("second", 3), ("twin", 0), ("twin", 1)),
    (("first", 4),),
    (("home", 2), ("z", 2), ("z", 3)),
    (("second", 4),),
    (("home", 1), ("twin", 2), ("twin", 3)),
    (("z", 4),),
    (("twin", 4),),
    (),
)


def backward_call(dah, xg, wq, q, k, v, ah, tot, starts, gd, gu, go, x_in, gain_one, mid):
    outer = lax.axis_size("pb") // 8
    rows = dah.shape[1]
    group = rows * SPAN
    count = len(CHUNKS)
    anyspace = pl.BlockSpec(memory_space=pl.ANY)
    vmem = pl.BlockSpec(memory_space=pltpu.VMEM)
    shape = jax.ShapeDtypeStruct
    dma = pltpu.SemaphoreType.DMA
    vm = pltpu.VMEM
    big = [(h, w) for _, _, h, _, w in CHUNKS]
    small = [(h // 4, w) for h, w in big]
    sq = (wq.shape[1] // 4, wq.shape[2])
    beyond = max(outer - 1, 1)
    held = max(outer, 1)
    spare = (16, 128)
    half = rows // 2
    scratch = (
        [
            vm((SPAN, rows, WIDE), BF),
            vm(xg.shape, BF),
            vm(wq.shape, BF),
            vm(q.shape, BF),
            vm(q.shape, BF),
            vm(q.shape, BF),
            vm(q.shape, BF),
            vm((LOCAL, 8, group), F32),
            vm(q.shape, F32),
            vm(q.shape, F32),
            vm(tot.shape, F32),
            vm((rows, 3 * WIDE), BF),
            vm((2, 2, half, D), BF),
            vm((SPAN, half, D), BF),
            vm((SPAN, half, D), BF),
            vm((D, 3 * WIDE), F32),
            vm(wq.shape, BF),
            vm(x_in.shape, BF),
            vm(mid.shape, F32),
            vm((2, 2, half, D), BF),
            vm(wq.shape, BF),
            vm((D // SPAN, 3 * D), F32),
        ]
        + [vm((SPAN,) + s, BF) for s in big]
        + [vm((SPAN,) + s, BF) for s in big]
        + [vm((2, SPAN) + s, BF) for s in small]
        + [vm((SPAN,) + s, BF) for s in small]
        + [vm((3,) + s, BF) for s in small]
        + [vm(s, BF) for s in small]
        + [vm((held,) + (s if outer > 1 else spare), BF) for s in small]
        + [
            vm((3, SPAN) + sq, BF),
            vm((SPAN,) + sq, BF),
            vm((SPAN,) + sq, BF),
            vm((2,) + sq, BF),
            vm((held, 2) + (sq if outer > 1 else spare), BF),
        ]
        + [
            dma((SPAN,)), dma((SPAN,)), dma((SPAN,)), dma((SPAN,)), dma((SPAN,)), dma((2, 2)), dma((9,)), dma((2,)),
            dma((count,)), dma((count,)), dma((count,)), dma((count + 1, 3)), dma((count + 1, 3)),
            dma((count + 1, 3)), dma((count + 1, 3)), dma((count + 1, beyond)), dma((count + 1, beyond)),
            dma((count + 2, 3)), dma((count + 2, 3)), dma((count + 2,)), dma((count + 2,)), dma((count + 2,)),
        ]
    )
    return pl.pallas_call(
        functools.partial(backward_kernel, outer),
        out_shape=(
            shape((rows, D), F32),
            shape(gd.shape[1:], BF),
            shape(gu.shape[1:], BF),
            shape(go.shape[1:], BF),
            shape((D // SPAN, 3 * D), F32),
        ),
        in_specs=[anyspace] * 8 + [vmem] + [anyspace] * 4 + [vmem, anyspace],
        out_specs=(anyspace,) * 5,
        scratch_shapes=scratch,
        compiler_params=pltpu.CompilerParams(
            collective_id=1, has_side_effects=True, vmem_limit_bytes=60 << 20
        ),
        name="backward_attention",
    )(dah, xg, wq, q, k, v, ah, tot, starts, gd, gu, go, x_in, gain_one, mid)


def body(layer_input, second_start, gain_attn, w_qkv, w_out, gain_mlp, w_up, w_down, d_output):
    rows = layer_input.shape[0]
    kv_index = lax.axis_index("ka")
    (output, d_middle, dah, gd, gu, go, xg, wq, q, k, v, ah, tot, starts) = forward_call(
        layer_input, second_start, gain_attn[None, :], w_qkv, gain_mlp[None, :], d_output, w_out, w_up, w_down
    )
    d_input, fd, fu, fo, total_qkv = backward_call(
        dah, xg, wq, q, k, v, ah, tot, starts, gd, gu, go, layer_input, gain_attn[None, :], d_middle
    )
    total_down = fd.astype(F32)
    total_up = fu.astype(F32)
    total_out = fo[: D // SPAN].astype(F32)
    def gain_grad(weight, grad, gain):
        own = lax.dynamic_slice_in_dim(gain, kv_index * (D // SPAN), D // SPAN)
        return jnp.sum(weight.astype(F32) * grad, axis=1) / own

    total_gain_attn = gain_grad(w_qkv, total_qkv, gain_attn)
    total_gain_mlp = gain_grad(w_up, total_up, gain_mlp)
    entry_count = rows * SPAN * lax.axis_size("pb") * D
    rms = jnp.sqrt(fo[D // SPAN, 0:1].astype(F32) / entry_count)
    return (
        output, d_input, total_gain_attn, total_qkv, total_out, total_gain_mlp, total_up, total_down, rms,
    )


def solution(mesh):
    if mesh.shape["ka"] != SPAN or mesh.shape["pb"] % 8:
        raise ValueError("unsupported mesh")
    placed = (
        P(("pb", "ka"), None), P("pb"), P(), P("ka", None), P("ka", None), P(), P("ka", None), P("ka", None),
        P(("pb", "ka"), None),
    )
    return jax.shard_map(
        body,
        mesh=mesh,
        in_specs=placed,
        out_specs=(
            P(("pb", "ka"), None), P(("pb", "ka"), None), P("ka"), P("ka", None), P("ka", None), P("ka"),
            P("ka", None), P("ka", None), P("ka"),
        ),
        check_vma=False,
    )
```

```python
import functools
import math

import jax
import jax.numpy as jnp
from jax import lax
from jax.experimental import pallas as pl
from jax.experimental.pallas import tpu as pltpu
from jax.sharding import PartitionSpec as P

D = 768
HEADS = 12
HEAD = 64
SPAN = 4
LOCAL = HEADS // SPAN
WIDE = LOCAL * HEAD
LOG2E = 1.4426950408889634
MESH = pl.DeviceIdType.MESH
BF = jnp.bfloat16
F32 = jnp.float32


def mirror(depth, side):
    return depth + side * (SPAN - 1 - 2 * depth)


def neighbours(pb):
    across_x = pb + 2 - 4 * ((pb // 2) % 2)
    across_y = pb + 4 - 8 * ((pb // 4) % 2)
    across_both = across_x + 4 - 8 * ((across_x // 4) % 2)
    return across_x, across_y, across_both


def sibling_of(pb):
    return pb + 1 - 2 * (pb % 2)


def centred(values):
    center = values - jnp.mean(values, axis=1, keepdims=True)
    inverse = lax.rsqrt(jnp.mean(center * center, axis=1, keepdims=True) + 1e-05)
    return center * inverse, inverse


def norm_back(cot, norm, inverse):
    return inverse * (
        cot - jnp.mean(cot, axis=1, keepdims=True) - norm * jnp.mean(cot * norm, axis=1, keepdims=True)
    )


def far(src, dst, send_sem, recv_sem, pb, ka):
    return pltpu.make_async_remote_copy(
        src, dst, send_sem, recv_sem, device_id=(pb, ka), device_id_type=MESH
    )


def greet(peers):
    barrier = pltpu.get_barrier_semaphore()
    for peer in peers:
        pl.semaphore_signal(barrier, 1, device_id=peer, device_id_type=MESH)
    pl.semaphore_wait(barrier, len(peers))


def dot_nt(left, right):
    return lax.dot_general(left, right, (((1,), (1,)), ((), ())), preferred_element_type=F32)


def dot_tn(left, right):
    return lax.dot_general(left, right, (((0,), (0,)), ((), ())), preferred_element_type=F32)


def dot_nn(left, right):
    return jnp.dot(left, right, preferred_element_type=F32)


def fold_lanes(tile):
    out = tile[:, :128]
    for at in range(128, tile.shape[1], 128):
        out = out + tile[:, at : at + 128]
    return out


THIRDS = 3
EARLY = 5
PIECES = 1 + 2 * THIRDS
FORWARD_STEPS = ((), (), (('plane', 0),), (('plane', 1),), (('plane', 2), ('pass', 0)), (('plane', 3), ('pass', 1), ('across', 0)))
AFTER_HEADS = (('pass', 2), ('across', 1), ('plane', 4))
AFTER_BRANCH = (('across', 2), ('pass', 3))
AFTER_NORM = (('pass', 4), ('across', 3))
AFTER_THIRD = ((('across', 4), ('plane', 5), ('plane', 6)), (('pass', 5), ('pass', 6), ('across', 5), ('across', 6)), ())


def forward_kernel(
    x_in, second, gain_one, w_qkv, gain_two, d_out, wo, wu, wd,
    output, mid_out, dah_out, gd_out, gu_out, go_out,
    xg_out, wq_out, q_out, k_out, v_out, ah_out, tot_out, start_out,
    xa, wq4, start, xg, wqs, qs, ks, vs, ahs, tots, ob, starts, ohome, wog, wug, wdg,
    mid, mlp_in, macc, dacc, gd, gu, go, dah, final,
    send_x, recv_x, send_q, recv_q, send_w, recv_w, send_s, recv_s, send_o, recv_o,
    send_z, recv_z, send_p, recv_p, send_c, recv_c, own_sem, out_sem, gd_sem, gu_sem,
):
    pb = lax.axis_index("pb")
    ka = lax.axis_index("ka")
    core = pb % 2
    base = pb - core
    side = ka // 2
    depth = mirror(ka, side)
    home_u = mirror(ka, core)
    quarter = 2 * depth + core
    sibling = sibling_of(pb)
    plane = neighbours(pb)
    rows = x_in.shape[0]
    rank = (pb // 2) % 4

    greet(
        [(pb, (ka + i) % SPAN) for i in range(1, SPAN)]
        + [(sibling, (ka + i) % SPAN) for i in range(SPAN)]
        + [(p, ka) for p in plane]
    )

    start[...] = jnp.full(start.shape, second[0].astype(F32), F32)
    for n in range(SPAN):
        for part in range(3):
            col = part * D + n * WIDE
            wq4[n, :, part * WIDE : (part + 1) * WIDE] = w_qkv[:, col : col + WIDE]
    height = wq4.shape[1] // 4

    def lines(ref, r):
        return ref.at[pl.ds(pl.multiple_of(r * height, 16), height)]

    out_q = []
    for i in range(1, SPAN):
        z = (ka + i) % SPAN
        zd = mirror(z, z // 2)
        out_q.append(
            far(
                lines(wq4.at[2 * zd + core], rank), lines(wqs.at[ka], rank),
                send_q.at[i - 1], recv_q.at[i - 1], pb, z,
            )
        )
    for copy in out_q:
        copy.start()
    own_q = pltpu.make_async_copy(wq4.at[quarter], wqs.at[ka], own_sem.at[0])
    own_q.start()

    step_rows = 128

    def first_norm(r, carry):
        at = pl.ds(pl.multiple_of(r * step_rows, step_rows), step_rows)
        norm, _ = centred(x_in[at, :].astype(F32))
        xa[at, :] = (norm * gain_one[...]).astype(BF)
        return carry

    lax.fori_loop(0, rows // step_rows, first_norm, 0)

    tick = rows // 4
    odd = (((home_u + 1) // 2) % 2) * (1 - home_u // 2)
    goal = mirror(1 - odd, core)
    out_x = [
        far(xa.at[pl.ds(t * tick, tick)], xg.at[ka, t], send_x.at[t], recv_x.at[ka, t], base + t // 2, goal)
        for t in (0, 2, 1, 3)
    ]
    for copy in out_x:
        copy.start()

    at_home = core == side

    def near_copies():
        return [
            far(xa.at[pl.ds(t * tick, tick)], xg.at[ka, t], send_x.at[4 + t], recv_x.at[ka, t], sibling, ka)
            for t in range(4)
        ]

    @pl.when(at_home)
    def _():
        for copy in near_copies():
            copy.start()
        for t in range(4):
            xg[ka, t] = xa[t * tick : (t + 1) * tick, :]

    def start_copies():
        out = []
        for n, (d, k) in enumerate(((0, 1), (1, 0), (1, 1))):
            target = base + (core + k) % 2
            out.append(far(start, starts, send_s.at[n], recv_s, target, mirror(d, core)))
        return out

    @pl.when(home_u == 0)
    def _():
        for copy in start_copies():
            copy.start()
        pltpu.make_async_copy(start, starts, recv_s).start()

    own_w = [
        pltpu.make_async_copy(wo, wog.at[ka], own_sem.at[1]),
        pltpu.make_async_copy(wd, wdg.at[ka], own_sem.at[2]),
    ]
    strip = D // THIRDS
    for part in range(THIRDS):
        for z in range(SPAN):
            own_w.append(
                pltpu.make_async_copy(
                    wu.at[:, z * D + part * strip : z * D + (part + 1) * strip],
                    wug.at[ka, part, :, z * strip : (z + 1) * strip],
                    own_sem.at[3 + part * SPAN + z],
                )
            )
    for copy in own_w:
        copy.start()

    def area(n, z, k, r=None):
        if n == 0:
            ref, row0, height, width = wog.at[z], 0, D // SPAN, D // 2
        elif n % 2:
            ref, row0, height, width = wug.at[z, n // 2], 0, D // SPAN, SPAN * strip // 2
        else:
            ref, row0, height, width = wdg.at[z], (n // 2 - 1) * strip, strip, D // 2
        at = pl.ds(pl.multiple_of(k * width, 128), width)
        if r is None:
            return ref.at[pl.ds(row0, height), at]
        return ref.at[pl.ds(pl.multiple_of(row0 + r * (height // 4), 16), height // 4), at]

    def z_copy(n, i):
        ref = area(n, ka, core, rank)
        return far(ref, ref, send_z.at[n, i - 1], recv_z.at[n, i - 1], pb, (ka + i) % SPAN)

    def z_arrival(n, i):
        ref = area(n, (ka - i) % SPAN, core, rank)
        return far(ref, ref, send_z.at[n, i - 1], recv_z.at[n, i - 1], pb, ka)

    def start_along_z():
        for copy in own_w:
            copy.wait()
        for n in range(EARLY):
            for i in (2, 1, 3):
                z_copy(n, i).start()

    @pl.when(depth == 0)
    def _():
        start_along_z()

    def chunk_copies(i, t):
        u = (1 - depth) if i == 0 else i + 1
        b = mirror(u, side)
        n = 2 * i + t
        t = 2 * core + t
        got = xg.at[b, t]
        here = far(got, got, send_x.at[8 + n], recv_x.at[b, t], pb, ka)
        onward = far(got, got, send_x.at[14 + n - 2], recv_x.at[b, t], pb, mirror(0, side)) if i else None
        return here, onward, far(got, got, send_x.at[8 + n], recv_x.at[b, t], sibling, ka)

    def pass_chunk(i, t, inner):
        here, onward, beside = chunk_copies(i, t)
        here.wait_recv()
        if inner and i:
            onward.start()
        beside.start()

    def beside_arrived(i):
        u = (1 - depth) if i == 0 else i + 1
        b = mirror(u, side)
        for t in range(2):
            got = xg.at[b, 2 * (1 - core) + t]
            far(got, got, send_x.at[8], recv_x.at[b, 2 * (1 - core) + t], pb, ka).wait_recv()

    for n in range(1, SPAN):
        mine_q = lines(wqs.at[(ka - n) % SPAN], rank)
        far(mine_q, mine_q, send_q.at[0], recv_q.at[n - 1], pb, ka).wait_recv()
        for m, p in enumerate(plane):
            copy = far(mine_q, mine_q, send_w.at[n - 1, m], recv_w.at[n - 1, m], p, ka)
            copy.start()
            out_q.append(copy)

    @pl.when(depth == 1)
    def _():
        pass_chunk(1, 0, True)
        pass_chunk(1, 1, True)

    pass_chunk(0, 0, False)
    pass_chunk(0, 1, False)
    for i in range(1, SPAN):
        for m, p in enumerate(plane):
            theirs = lines(wqs.at[(ka - i) % SPAN], (p // 2) % 4)
            far(theirs, theirs, send_w.at[i - 1, m], recv_w.at[i - 1, m], p, ka).wait_recv()
    own_q.wait()
    pltpu.make_async_copy(start, starts, recv_s).wait()

    def project(u):
        b = mirror(u, side)
        xb = xg[b].reshape(rows, D)
        at = pl.multiple_of(b * rows, rows)
        for dst, col in ((qs, 0), (ks, WIDE), (vs, 2 * WIDE)):
            w = wqs[:, :, col : col + WIDE].reshape(D, WIDE)
            out = dot_nn(xb, w).astype(BF)
            for h in range(LOCAL):
                dst[h, pl.ds(at, rows), :] = out[:, h * HEAD : (h + 1) * HEAD]

    def plane_copy(n, i, m, r, p):
        ref = area(n, (ka - i) % SPAN, core, r)
        return far(ref, ref, send_p.at[n, i - 1, m], recv_p.at[n, i - 1, m], p, ka)

    def rank_of(m):
        return (plane[m] // 2) % 4

    def begin_plane(n):
        for i in range(1, SPAN):
            z_arrival(n, i).wait_recv()
            for m in range(2):
                plane_copy(n, i, m, rank, plane[m]).start()

    def pass_on(n):
        first = n % 2
        for i in range(1, SPAN):
            plane_copy(n, i, first, rank_of(first), pb).wait_recv()
            plane_copy(n, i, 2, rank_of(first), plane[1 - first]).start()

    def across_copy(n, i):
        ref = area(n, (ka - i) % SPAN, core)
        return far(ref, ref, send_c.at[n, i - 1], recv_c.at[n, i - 1], sibling, ka)

    def begin_across(n):
        other = 1 - n % 2
        for i in range(1, SPAN):
            plane_copy(n, i, other, rank_of(other), pb).wait_recv()
            plane_copy(n, i, 2, rank_of(2), pb).wait_recv()
            across_copy(n, i).start()

    def arrived(n):
        for i in range(1, SPAN):
            ref = area(n, (ka - i) % SPAN, 1 - core)
            far(ref, ref, send_c.at[n, i - 1], recv_c.at[n, i - 1], pb, ka).wait_recv()

    def weights_sent():
        for n in range(PIECES):
            for i in range(1, SPAN):
                z_copy(n, i).wait_send()
                for m in range(3):
                    plane_copy(n, i, m, rank, pb).wait_send()
                across_copy(n, i).wait_send()

    scale = LOG2E / math.sqrt(HEAD)
    one = jnp.where(starts[0:1, 0:1] > (SPAN // 2) * rows + 0.5, 1.0, 0.0)
    sub = 256

    def attend_own(u):
        b = mirror(u, side)

        def head(h, carry):
            for part in range(rows // sub):
                width = (part + 1) * sub
                at = pl.multiple_of(b * rows, rows)
                row0 = pl.multiple_of(b * rows + part * sub, sub)
                s = dot_nt(qs[h, pl.ds(row0, sub), :], ks[h, pl.ds(at, width), :]) * scale
                seen = (
                    lax.broadcasted_iota(jnp.int32, (sub, width), 0) + part * sub
                    >= lax.broadcasted_iota(jnp.int32, (sub, width), 1)
                )
                up = jnp.where(seen, jnp.exp2(s - 1.0), 0.0)
                down = jnp.where(seen, jnp.exp2(-s - 1.0), 0.0)
                tots[h, pl.ds(row0, sub), :] = fold_lanes(up + down)
                ahs[h, pl.ds(row0, sub), :] = dot_nn((up - down).astype(BF), vs[h, pl.ds(at, width), :])
            return carry

        lax.fori_loop(0, LOCAL, head, 0)

    def attend_pair(high, low):
        qb = high + side * (SPAN - 1 - low - high)
        kb = low + side * (SPAN - 1 - low - high)
        same = jnp.where(qb // 2 == kb // 2, 1.0, 0.0)
        keep = jnp.maximum(one, same) > 0.5

        def head(h, carry):
            at = pl.multiple_of(kb * rows, rows)
            for part in range(rows // sub):
                row0 = pl.multiple_of(qb * rows + part * sub, sub)
                s = dot_nt(qs[h, pl.ds(row0, sub), :], ks[h, pl.ds(at, rows), :]) * scale
                up, down = jnp.exp2(s - 1.0), jnp.exp2(-s - 1.0)
                tots[h, pl.ds(row0, sub), :] += jnp.where(keep, fold_lanes(up + down), 0.0)
                ahs[h, pl.ds(row0, sub), :] += jnp.where(
                    keep, dot_nn((up - down).astype(BF), vs[h, pl.ds(at, rows), :]), 0.0
                )
            return carry

        lax.fori_loop(0, LOCAL, head, 0)

    actions = {"plane": begin_plane, "pass": pass_on, "across": begin_across}

    def run_steps(todo):
        for step, n in todo:
            actions[step](n)

    def home_copy(b):
        return far(ob.at[b], ohome.at[quarter], send_o.at[b], recv_o.at[quarter], base + side, b)

    def send_home(u):
        b = mirror(u, side)
        at = pl.ds(pl.multiple_of(b * rows, rows), rows)
        done = []
        for h in range(LOCAL):
            total = jnp.sum(tots[h, at, :], axis=1, keepdims=True)
            heads = ahs[h, at, :] / total
            ahs[h, at, :] = heads
            tots[h, at, :] = jnp.broadcast_to(total, (rows, 128))
            done.append(heads)
        ob[b] = jnp.concatenate(done, axis=1).astype(BF)
        mine = (core == side) & (ka == b)

        @pl.when(jnp.logical_not(mine))
        def _():
            home_copy(b).start()

        @pl.when(mine)
        def _():
            pltpu.make_async_copy(ob.at[b], ohome.at[quarter], recv_o.at[quarter]).start()

    @pl.when(jnp.logical_not(at_home))
    def _():
        for t in range(4):
            far(xg.at[ka, t], xg.at[ka, t], send_x.at[8], recv_x.at[ka, t], pb, ka).wait_recv()

    project(depth)
    attend_own(depth)

    @pl.when(depth == 1)
    def _():
        pass_chunk(2, 0, True)
        pass_chunk(2, 1, True)
        start_along_z()

    run_steps(FORWARD_STEPS[0])
    beside_arrived(0)
    project(1 - depth)
    attend_own(1 - depth)
    attend_pair(1, 0)

    @pl.when(side == 0)
    def _():
        send_home(0)
        send_home(1)

    run_steps(FORWARD_STEPS[1])

    @pl.when(depth == 0)
    def _():
        pass_chunk(1, 0, False)
        pass_chunk(1, 1, False)

    beside_arrived(1)
    project(2)
    attend_own(2)
    attend_pair(2, 1)
    attend_pair(2, 0)

    @pl.when(side == 0)
    def _():
        send_home(2)

    run_steps(FORWARD_STEPS[2])

    @pl.when(depth == 0)
    def _():
        pass_chunk(2, 0, False)
        pass_chunk(2, 1, False)

    beside_arrived(2)
    project(3)
    attend_own(3)

    @pl.when(side == 1)
    def _():
        send_home(3)

    for low in (2, 1, 0):
        attend_pair(3, low)

        @pl.when(side == 1)
        def _(low=low):
            send_home(low)

        run_steps(FORWARD_STEPS[5 - low])

    @pl.when(side == 0)
    def _():
        send_home(3)

    for n in range(EARLY, PIECES):
        for i in (2, 1, 3):
            z_copy(n, i).start()
    saves = [
        pltpu.make_async_copy(src, dst, out_sem.at[n])
        for n, (src, dst) in enumerate(
            (
                (xg, xg_out), (wqs, wq_out), (qs, q_out), (ks, k_out), (vs, v_out),
                (ahs, ah_out), (tots, tot_out), (starts, start_out),
            )
        )
    ]
    for copy in saves:
        copy.start()

    run_steps(AFTER_HEADS)
    arrived(0)
    for n in range(SPAN):
        far(ob.at[0], ohome.at[n], send_o.at[0], recv_o.at[n], pb, ka).wait_recv()

    branch = dot_nn(ohome[0], wog[0])
    for n in range(1, SPAN):
        branch = branch + dot_nn(ohome[n], wog[n])
    mid[...] = branch
    run_steps(AFTER_BRANCH)

    def second_norm(r, sums):
        at = pl.ds(pl.multiple_of(r * step_rows, step_rows), step_rows)
        x32 = x_in[at, :].astype(F32)
        term = mid[at, :]
        middle = x32 + term
        norm, _ = centred(middle)
        mid[at, :] = middle
        mlp_in[at, :] = (norm * gain_two[...]).astype(BF)
        return tuple(
            s + fold_lanes(jnp.sum(t * t, axis=0, keepdims=True))
            for s, t in zip(sums, (x32, term, middle))
        )

    zero = jnp.zeros((1, 128), F32)
    sums = lax.fori_loop(0, rows // step_rows, second_norm, (zero, zero, zero))
    run_steps(AFTER_NORM)
    macc[...] = jnp.zeros_like(macc)
    dacc[...] = jnp.zeros_like(dacc)

    def store_all(part, pair, slot):
        row0 = part * strip
        copies = [
            pltpu.make_async_copy(
                gd.at[slot], gd_out.at[pl.ds(2 * pair, 2), pl.ds(row0, strip)], gd_sem.at[slot]
            )
        ]
        for n in range(2):
            cols = pl.ds(pl.multiple_of((2 * pair + n) * D + row0, strip), strip)
            copies.append(
                pltpu.make_async_copy(
                    gu.at[slot, :, :, n * strip : (n + 1) * strip], gu_out.at[:, :, cols], gu_sem.at[slot, n]
                )
            )
        return copies

    root = math.sqrt(2.0 / math.pi)

    for part in range(THIRDS):
        arrived(1 + 2 * part)
        arrived(2 + 2 * part)

        def feed(pair, carry):
            at = pl.ds(pl.multiple_of(pair * 2 * strip, 2 * strip), 2 * strip)
            w_up = wug[:, part, :, at].reshape(D, 2 * strip)
            w_down = wdg[pl.ds(2 * pair, 2), part * strip : (part + 1) * strip, :].reshape(2 * strip, D)
            up = dot_nn(mlp_in[...], w_up)
            bend = jnp.tanh(root * (up + 0.044715 * (up * up * up)))
            act = (0.5 * up * (1.0 + bend)).astype(BF)
            slope = 0.5 * (1.0 + bend) + 0.5 * up * (1.0 - bend * bend) * (root * (1.0 + 0.134145 * (up * up)))
            macc[...] += dot_nn(act, w_down)
            d_up = (slope * dot_nt(d_out[...], w_down)).astype(BF)
            dacc[...] += dot_nt(d_up, w_up)
            if part:
                for copy in store_all(part - 1, pair, pair):
                    copy.wait()
            gd[pair] = dot_tn(act, d_out[...]).astype(BF).reshape(2, strip, D)
            gu[pair] = dot_tn(mlp_in[...], d_up).astype(BF).reshape(SPAN, D // SPAN, 2 * strip)
            for copy in store_all(part, pair, pair):
                copy.start()
            return carry

        lax.fori_loop(0, 2, feed, 0)
        run_steps(AFTER_THIRD[part])

    def finish_rows(r, total):
        at = pl.ds(pl.multiple_of(r * step_rows, step_rows), step_rows)
        middle = mid[at, :]
        norm, inverse = centred(middle)
        term = macc[at, :]
        final[at, :] = (middle + term).astype(BF)
        d_middle = d_out[at, :].astype(F32) + norm_back(dacc[at, :] * gain_two[...], norm, inverse)
        mid[at, :] = d_middle
        mlp_in[at, :] = d_middle.astype(BF)
        return total + fold_lanes(jnp.sum(term * term, axis=0, keepdims=True))

    last = lax.fori_loop(0, rows // step_rows, finish_rows, zero)
    ends = [
        pltpu.make_async_copy(src, dst, out_sem.at[8 + n])
        for n, (src, dst) in enumerate(((mid, mid_out), (final, output)))
    ]
    for copy in ends:
        copy.start()
    corner = (lax.broadcasted_iota(jnp.int32, (64, D), 0) == 0) & (
        lax.broadcasted_iota(jnp.int32, (64, D), 1) == 0
    )
    for n in range(SPAN):
        dah[n] = dot_nt(mlp_in[...], wog[n]).astype(BF)
        go[n, : D // SPAN, :] = dot_tn(ohome[n], mlp_in[...]).astype(BF)
        value = jnp.sum((sums + (last,))[n], axis=1, keepdims=True)
        go[n, D // SPAN :, :] = jnp.where(corner, value, 0.0).astype(BF)
    ends += [
        pltpu.make_async_copy(src, dst, out_sem.at[10 + n])
        for n, (src, dst) in enumerate(((dah, dah_out), (go, go_out)))
    ]
    for copy in ends[2:]:
        copy.start()
    for pair in range(2):
        for copy in store_all(THIRDS - 1, pair, pair):
            copy.wait()
    for copy in saves + ends:
        copy.wait()
    for copy in out_x + out_q:
        copy.wait_send()
    weights_sent()
    for i in range(3):
        for t in range(2):
            _, onward, beside = chunk_copies(i, t)
            beside.wait_send()
            if i:

                @pl.when(depth == 1)
                def _(onward=onward):
                    onward.wait_send()

    @pl.when(at_home)
    def _():
        for copy in near_copies():
            copy.wait_send()

    @pl.when(home_u == 0)
    def _():
        for copy in start_copies():
            copy.wait_send()

    for b in range(SPAN):
        mine = (core == side) & (ka == b)

        @pl.when(jnp.logical_not(mine))
        def _(b=b):
            home_copy(b).wait_send()


def forward_call(x_in, second, gain_one, w_qkv, gain_two, d_out, wo, wu, wd):
    rows = x_in.shape[0]
    group = rows * SPAN
    anyspace = pl.BlockSpec(memory_space=pl.ANY)
    vmem = pl.BlockSpec(memory_space=pltpu.VMEM)
    shape = jax.ShapeDtypeStruct
    dma = pltpu.SemaphoreType.DMA
    vm = pltpu.VMEM
    count = PIECES
    tokens = (SPAN, 4, rows // 4, D)
    columns = (SPAN, D // SPAN, 3 * WIDE)
    heads = (LOCAL, group, HEAD)
    outs = (
        shape((rows, D), BF),
        shape((rows, D), F32),
        shape((SPAN, rows, WIDE), BF),
        shape((SPAN, D, D), BF),
        shape((SPAN, D // SPAN, SPAN * D), BF),
        shape((SPAN, D // SPAN + 64, D), BF),
        shape(tokens, BF),
        shape(columns, BF),
        shape(heads, BF),
        shape(heads, BF),
        shape(heads, BF),
        shape(heads, F32),
        shape((LOCAL, group, 128), F32),
        shape((8, 128), F32),
    )
    scratch = [
        vm((rows, D), BF),
        vm(columns, BF),
        vm((8, 128), F32),
        vm(tokens, BF),
        vm(columns, BF),
        vm(heads, BF),
        vm(heads, BF),
        vm(heads, BF),
        vm(heads, F32),
        vm((LOCAL, group, 128), F32),
        vm((SPAN, rows, WIDE), BF),
        vm((8, 128), F32),
        vm((SPAN, rows, WIDE), BF),
        vm((SPAN,) + wo.shape, BF),
        vm((SPAN, THIRDS, D // SPAN, SPAN * D // THIRDS), BF),
        vm((SPAN,) + wd.shape, BF),
        vm((rows, D), F32),
        vm((rows, D), BF),
        vm((rows, D), F32),
        vm((rows, D), F32),
        vm((2, 2, D // THIRDS, D), BF),
        vm((2, SPAN, D // SPAN, 2 * D // THIRDS), BF),
        vm((SPAN, D // SPAN + 64, D), BF),
        vm((SPAN, rows, WIDE), BF),
        vm((rows, D), BF),
        dma((18,)), dma((SPAN, 4)), dma((3,)), dma((3,)), dma((3, 3)), dma((3, 3)), dma((3,)), dma,
        dma((SPAN,)), dma((SPAN,)),
        dma((count, 3)), dma((count, 3)), dma((count, 3, 3)), dma((count, 3, 3)), dma((count, 3)), dma((count, 3)),
        dma((3 + SPAN * THIRDS,)), dma((12,)), dma((2,)), dma((2, 2)),
    ]
    return pl.pallas_call(
        forward_kernel,
        out_shape=outs,
        in_specs=[vmem, pl.BlockSpec(memory_space=pltpu.SMEM), vmem, vmem, vmem, vmem] + [anyspace] * 3,
        out_specs=(anyspace,) * len(outs),
        scratch_shapes=scratch,
        compiler_params=pltpu.CompilerParams(
            collective_id=0, has_side_effects=True, vmem_limit_bytes=60 << 20
        ),
        name="forward_layer",
    )(x_in, second, gain_one, w_qkv, gain_two, d_out, wo, wu, wd)


CHUNKS = (
    (0, 0, 384, 0, 384),
    (0, 384, 384, 0, 384),
    (1, 0, 192, 0, 768),
    (1, 0, 192, 768, 768),
    (2, 0, 256, 0, 384),
)


def backward_kernel(
    outer, dah, xg_in, wq_in, q_in, k_in, v_in, ah_in, tot_in, starts, gd, gu, go, x_in, gain_one, mid_in,
    d_input, fd, fu, fo, qkv_out,
    da, xg, wqs, qs, ks, vs, dms, deltas, dqs, dks, dvs, joint, own, mate, back, grad_q, gq,
    x_own, mid, dxh, through, fq, qkv,
    *refs,
):
    count = len(CHUNKS)
    halves, mates, firsts, seconds, relays, zs, fins, slots = (refs[i * count : (i + 1) * count] for i in range(8))
    refs = refs[8 * count :]
    fours_q, sum_q, zq, fin_q, slots_q = refs[:5]
    (
        send_a, recv_a, send_m, recv_m, send_h, recv_h, recv_t, in_sem, out_sem,
        own_sem, send_n, recv_n, send_p, recv_p, send_z, recv_z, send_o, recv_o,
        send_g, recv_g, send_c, recv_c, keep_sem,
    ) = refs[5:]
    pb = lax.axis_index("pb")
    ka = lax.axis_index("ka")
    core = pb % 2
    base = pb - core
    side = ka // 2
    depth = mirror(ka, side)
    sibling = sibling_of(pb)
    plane = neighbours(pb)
    rank = (pb // 2) % 4
    where = pb // 8
    beyond = [(pb + 8 * o) % (8 * outer) for o in range(1, outer)]
    rows = dah.shape[1]
    half = rows // 2

    greet(
        [(pb, (ka + i) % SPAN) for i in range(1, SPAN)]
        + [(sibling, (ka + i) % SPAN) for i in range(SPAN)]
        + [(p, ka) for p in plane]
        + [(p, ka) for p in beyond]
    )

    def outgoing(n):
        worker_depth, worker_core = n // 2, n % 2
        target, spot = base + worker_core, mirror(worker_depth, core)
        mine = (target == pb) & (spot == ka)
        return mine, far(dah.at[n], da.at[ka], send_a.at[n], recv_a.at[ka], target, spot)

    for n in range(SPAN):
        mine, remote = outgoing(n)

        @pl.when(jnp.logical_not(mine))
        def _():
            remote.start()

        @pl.when(mine)
        def _():
            pltpu.make_async_copy(dah.at[n], da.at[ka], recv_a.at[ka]).start()

    sources = (gd, gu, go)
    results = (fd, fu, fo)

    def block_of(ref, n, k, row0, height):
        _, _, _, col0, width = CHUNKS[n]
        at = pl.multiple_of(k * (ref.shape[-1] // 2) + col0, 128)
        return pl.ds(row0, height), pl.ds(at, width)

    def source(n, k):
        a, row0, height, _, _ = CHUNKS[n]
        r, c = block_of(sources[a], n, k, row0, height)
        return sources[a].at[:, r, c]

    def quarter(n, r):
        height = CHUNKS[n][2] // 4
        return pl.ds(pl.multiple_of(r * height, 16), height)

    def landing(n, r):
        a, row0, height, _, _ = CHUNKS[n]
        rr, c = block_of(results[a], n, core, pl.multiple_of(row0 + r * (height // 4), 16), height // 4)
        return results[a].at[rr, c]

    def strip(n, k):
        a, row0, height, _, _ = CHUNKS[n]
        r, c = block_of(results[a], n, k, row0, height)
        return results[a].at[r, c]

    def local_half(n):
        return pltpu.make_async_copy(source(n, core), halves[n], own_sem.at[n])

    def to_sibling(n):
        return far(source(n, 1 - core), mates[n], send_n.at[n], recv_n.at[n], sibling, ka)

    def rank_of(m):
        return (plane[m] // 2) % 4

    def to_first(n, m):
        first = n % 2
        r = rank_of((first, 2)[m])
        return far(
            halves[n].at[:, quarter(n, r), :], firsts[n].at[m], send_p.at[n, m], recv_p.at[n, m], plane[first], ka
        )

    def to_second(n):
        other = 1 - n % 2
        return far(
            halves[n].at[:, quarter(n, rank_of(other)), :], seconds[n], send_p.at[n, 2], recv_p.at[n, 2],
            plane[other], ka,
        )

    inner = (ka + ka // 2) % 2
    partner = ka + 1 - 2 * (ka % 2)
    far_side = 2 - 2 * (ka // 2)

    def to_partner(n):
        return far(
            halves[n].at[partner, quarter(n, rank), :], zs[n].at[0], send_z.at[n, 0], recv_z.at[n, 0], pb, partner
        )

    def to_relay(n):
        return far(
            halves[n].at[pl.ds(far_side, 2), quarter(n, rank), :], relays[n], send_z.at[n, 1], recv_z.at[n, 2],
            pb, partner,
        )

    def to_far(n, i):
        return far(
            halves[n].at[far_side + i, quarter(n, rank), :], zs[n].at[1], send_z.at[n, 1 + i], recv_z.at[n, 1],
            pb, far_side + i,
        )

    def keep(n):
        return pltpu.make_async_copy(fins[n], landing(n, rank), keep_sem.at[n])

    def to_all(n, m):
        return far(fins[n], landing(n, rank), send_g.at[n, m], recv_g.at[n, m], plane[m], ka)

    def to_twin(n):
        return far(strip(n, core), strip(n, core), send_c.at[n], recv_c.at[n], sibling, ka)

    def merge_sibling(n):
        local_half(n).wait()
        to_sibling(n).wait_recv()

        def add(z, carry):
            halves[n][z] = (halves[n][z].astype(F32) + mates[n][z].astype(F32)).astype(BF)
            return carry

        lax.fori_loop(0, SPAN, add, 0)
        for m in (1, 0):
            to_first(n, m).start()

    def merge_first(n):
        for m in (1, 0):
            to_first(n, m).wait_recv()
            held = quarter(n, (rank, rank_of(1 - n % 2))[m])

            def add(z, carry):
                halves[n][z, held, :] = (halves[n][z, held, :].astype(F32) + firsts[n][m, z].astype(F32)).astype(BF)
                return carry

            lax.fori_loop(0, SPAN, add, 0)
            if m:
                to_second(n).start()

    def merge_second(n):
        to_second(n).wait_recv()
        held = quarter(n, rank)

        def add(z, carry):
            halves[n][z, held, :] = (halves[n][z, held, :].astype(F32) + seconds[n][z].astype(F32)).astype(BF)
            return carry

        lax.fori_loop(0, SPAN, add, 0)
        @pl.when(inner == 0)
        def _():
            to_relay(n).start()

        to_partner(n).start()

    def merge_relay(n):
        @pl.when(inner == 1)
        def _():
            to_relay(n).wait_recv()
            held = quarter(n, rank)
            for i in range(2):
                z = far_side + i
                halves[n][z, held, :] = (halves[n][z, held, :].astype(F32) + relays[n][i].astype(F32)).astype(BF)
                to_far(n, i).start()

    def merge_beyond(fin, slot, n):
        for o, p in enumerate(beyond):
            far(fin, slot.at[where], send_o.at[n, o], recv_o.at[n, o], p, ka).start()
        slot[where] = fin[...]
        for o in range(outer - 1):
            far(slot.at[0], slot.at[0], send_o.at[n, o], recv_o.at[n, o], pb, ka).wait()
        total = slot[0].astype(F32)
        for o in range(1, outer):
            total = total + slot[o].astype(F32)
        fin[...] = total.astype(BF)

    def merge_z(n):
        to_partner(n).wait_recv()
        to_far(n, 0).wait_recv()
        total = halves[n][ka, quarter(n, rank), :].astype(F32) + zs[n][0].astype(F32) + zs[n][1].astype(F32)
        fins[n][...] = total.astype(BF)
        if outer > 1:
            merge_beyond(fins[n], slots[n], n)
        keep(n).start()
        for m in range(3):
            to_all(n, m).start()

    def pass_twin(n):
        keep(n).wait()
        for m in range(3):
            got = landing(n, (plane[m] // 2) % 4)
            far(got, got, send_g.at[n, m], recv_g.at[n, m], pb, ka).wait_recv()
        to_twin(n).start()

    def finish(n):
        got = strip(n, 1 - core)
        far(got, got, send_c.at[n], recv_c.at[n], sibling, ka).wait_recv()
        to_sibling(n).wait_send()
        for m in range(3):
            to_all(n, m).wait_send()
        for m in range(2):
            to_first(n, m).wait_send()
        to_second(n).wait_send()
        to_partner(n).wait_send()

        @pl.when(inner == 0)
        def _():
            to_relay(n).wait_send()

        @pl.when(inner == 1)
        def _():
            for i in range(2):
                to_far(n, i).wait_send()

        to_twin(n).wait_send()

    for n in range(count):
        local_half(n).start()
        to_sibling(n).start()

    loads = [
        pltpu.make_async_copy(src, dst, in_sem.at[n])
        for n, (src, dst) in enumerate(
            (
                (ah_in, dks), (tot_in, dvs), (q_in, qs), (k_in, ks), (v_in, vs), (xg_in, xg), (wq_in, wqs),
                (x_in, x_own), (mid_in, mid),
            )
        )
    ]
    for copy in loads:
        copy.start()
    dqs[...] = jnp.zeros_like(dqs)

    for n in range(count):
        merge_sibling(n)

    for copy in loads[:5]:
        copy.wait()
    for b in range(SPAN):
        far(dah.at[0], da.at[b], send_a.at[0], recv_a.at[b], pb, ka).wait_recv()

    scale = LOG2E / math.sqrt(HEAD)
    unit = 1.0 / math.sqrt(HEAD)
    one = jnp.where(starts[0:1, 0:1] > (SPAN // 2) * rows + 0.5, 1.0, 0.0)
    sub = 256

    for b in range(SPAN):
        block = da[b].astype(F32)
        for h in range(LOCAL):
            rows_b = slice(b * rows, (b + 1) * rows)
            scaled = block[:, h * HEAD : (h + 1) * HEAD] / dvs[h, rows_b, :HEAD]
            dms[h, rows_b, :] = scaled.astype(BF)
            deltas[h, :, rows_b] = lax.dot_general(
                jnp.ones((8, HEAD), F32), scaled * dks[h, rows_b, :],
                (((1,), (1,)), ((), ())), precision=lax.Precision.HIGHEST, preferred_element_type=F32,
            )
            dvs[h, rows_b, :] = jnp.zeros((rows, 128), F32)
            dks[h, rows_b, :] = jnp.zeros((rows, HEAD), F32)

    def tile(h, row0, height, at, width, seen=None, keep_it=None):
        q = qs[h, pl.ds(row0, height), :]
        dm = dms[h, pl.ds(row0, height), :]
        keys = ks[h, pl.ds(at, width), :]
        s = dot_nt(keys, q) * scale
        up, down = jnp.exp2(s - 1.0), jnp.exp2(-s - 1.0)
        if seen is not None:
            up = jnp.where(seen, up, 0.0)
            down = jnp.where(seen, down, 0.0)
        expo, sine = up + down, up - down
        dsig = dot_nt(vs[h, pl.ds(at, width), :], dm)
        delta = deltas[h, 0:1, pl.ds(row0, height)]
        ds = (expo * dsig - sine * delta).astype(BF)
        dk, dv, dq = dot_nn(ds, q), dot_nn(sine.astype(BF), dm), dot_tn(ds, keys)
        if keep_it is not None:
            dk, dv, dq = (jnp.where(keep_it, t, 0.0) for t in (dk, dv, dq))
        dks[h, pl.ds(at, width), :] += dk
        dvs[h, pl.ds(at, width), :HEAD] += dv
        dqs[h, pl.ds(row0, height), :] += dq

    def attend_own(u):
        b = mirror(u, side)

        def head(h, carry):
            for part in range(rows // sub):
                height = rows - part * sub
                at = pl.multiple_of(b * rows + part * sub, sub)
                seen = lax.broadcasted_iota(jnp.int32, (sub, height), 0) <= lax.broadcasted_iota(
                    jnp.int32, (sub, height), 1
                )
                tile(h, at, height, at, sub, seen=seen)
            return carry

        lax.fori_loop(0, LOCAL, head, 0)

    def attend_pair(high, low):
        qb = high + side * (SPAN - 1 - low - high)
        kb = low + side * (SPAN - 1 - low - high)
        same = jnp.where(qb // 2 == kb // 2, 1.0, 0.0)
        keep_it = jnp.maximum(one, same) > 0.5

        def head(h, carry):
            for part in range(rows // sub):
                tile(
                    h, pl.multiple_of(qb * rows, rows), rows,
                    pl.multiple_of(kb * rows + part * sub, sub), sub, keep_it=keep_it,
                )
            return carry

        lax.fori_loop(0, LOCAL, head, 0)

    def home_copy(b):
        return far(back.at[b], dxh.at[depth, core], send_h.at[b], recv_h.at[depth, core], base + side, b)

    def swap(u):
        return far(own.at[u % 2, 1 - core], mate.at[u], send_m.at[u], recv_m.at[u], sibling, ka)

    half = rows // 2

    def block_done(u):
        b = mirror(u, side)
        at = pl.ds(pl.multiple_of(b * rows, rows), rows)
        joint[...] = jnp.concatenate(
            [(dqs[h, at, :] * unit).astype(BF) for h in range(LOCAL)]
            + [(dks[h, at, :] * unit).astype(BF) for h in range(LOCAL)]
            + [dvs[h, at, :HEAD].astype(BF) for h in range(LOCAL)],
            axis=1,
        )
        if u < 2:
            swap(u + 2).wait_send()
        own[u % 2] = dot_nt(joint[...], wqs[...].reshape(D, 3 * WIDE)).astype(BF).reshape(2, half, D)
        swap(u).start()
        part = dot_tn(xg[b].reshape(rows, D), joint[...])
        if u == SPAN - 1:
            grad_q[...] = part
        else:
            grad_q[...] += part

    def send_home(u):
        b = mirror(u, side)
        swap(u).wait_recv()
        back[b] = (own[u % 2, core].astype(F32) + mate[u].astype(F32)).astype(BF)
        if u >= 2:

            @pl.when(depth == 0)
            def _():
                to_inner(u).start()

            return
        mine = (core == side) & (ka == b)

        @pl.when(jnp.logical_not(mine))
        def _():
            home_copy(b).start()

        @pl.when(mine)
        def _():
            pltpu.make_async_copy(back.at[b], dxh.at[depth, core], recv_h.at[depth, core]).start()

    def to_inner(u):
        b = mirror(u, side)
        return far(back.at[b], through.at[u - 2], send_h.at[b], recv_t.at[u - 2], pb, mirror(1, side))

    def join_home(u):
        b = mirror(u, side)

        @pl.when(depth == 1)
        def _():
            to_inner(u).wait_recv()
            back[b] = (back[b].astype(F32) + through[u - 2].astype(F32)).astype(BF)
            home_copy(b).start()

    steps = {
        "first": merge_first, "second": merge_second, "z": merge_z, "twin": pass_twin, "home": send_home,
        "relay": merge_relay, "join": join_home,
    }
    todo = [list(row) for row in BACKWARD_STEPS]

    def run_next():
        for step, n in todo.pop(0):
            steps[step](n)

    run_next()
    loads[5].wait()
    loads[6].wait()
    for high in range(SPAN - 1, -1, -1):
        attend_own(high)
        run_next()
        for low in range(high - 1, -1, -1):
            attend_pair(high, low)
            run_next()
        block_done(high)
    gq[...] = grad_q[...].astype(BF).reshape(gq.shape)
    height_q = gq.shape[1] // 4

    def lines(r):
        return pl.ds(pl.multiple_of(r * height_q, 16), height_q)

    def q_plane(m):
        return far(
            gq.at[:, lines(rank_of(m)), :], fours_q.at[m], send_p.at[count, m], recv_p.at[count, m], plane[m], ka
        )

    def q_owner(i):
        z = (ka + i) % SPAN
        return far(sum_q.at[z], zq.at[ka], send_z.at[count, i - 1], recv_z.at[count, i - 1], pb, z)

    def q_landing(d, r):
        return fq.at[2 * d + core, lines(r)]

    def q_all(d, m):
        return far(fin_q.at[d], q_landing(d, rank), send_g.at[count + d, m], recv_g.at[count + d, m], plane[m], ka)

    def q_twin(d):
        ref = fq.at[2 * d + core]
        return far(ref, ref, send_c.at[count + d], recv_c.at[count + d], sibling, ka)

    for m in range(3):
        q_plane(m).start()
    send_home(0)
    run_next()

    for m in range(3):
        q_plane(m).wait_recv()
    mine_q = lines(rank)
    sum_q[...] = (
        gq[:, mine_q, :].astype(F32) + fours_q[0].astype(F32) + fours_q[1].astype(F32) + fours_q[2].astype(F32)
    ).astype(BF)
    for i in (2, 1, 3):
        q_owner(i).start()
    zq[ka] = sum_q[ka]
    run_next()
    def from_chip(d):
        for k in range(2):
            far(back.at[0], dxh.at[d, k], send_h.at[0], recv_h.at[d, k], pb, ka).wait_recv()

    @pl.when(mirror(ka, core) < 2)
    def _():
        from_chip(0)

    @pl.when(mirror(ka, core) >= 2)
    def _():
        dxh[0] = jnp.zeros(dxh.shape[1:], BF)

    from_chip(1)
    loads[7].wait()
    loads[8].wait()
    step_rows = 128

    def input_rows(r, carry):
        at = pl.ds(pl.multiple_of(r * step_rows, step_rows), step_rows)
        inner = pl.ds(pl.multiple_of((r % 2) * step_rows, step_rows), step_rows)
        cot = dxh[0, r // 2, inner, :].astype(F32) + dxh[1, r // 2, inner, :].astype(F32)
        norm, inverse = centred(x_own[at, :].astype(F32))
        mid[at, :] = mid[at, :] + norm_back(cot * gain_one[...], norm, inverse)
        return carry

    lax.fori_loop(0, rows // step_rows, input_rows, 0)
    out_copy = pltpu.make_async_copy(mid, d_input, out_sem.at[0])
    out_copy.start()
    for i in range(1, SPAN):
        z = (ka - i) % SPAN
        far(zq.at[z], zq.at[z], send_z.at[count, i - 1], recv_z.at[count, i - 1], pb, z).wait_recv()
    for d in range(2):
        fin_q[d] = (zq[d].astype(F32) + zq[SPAN - 1 - d].astype(F32)).astype(BF)
    if outer > 1:
        merge_beyond(fin_q, slots_q, count)
    for d in range(2):
        fq[2 * d + core, lines(rank), :] = fin_q[d]
        for m in range(3):
            q_all(d, m).start()
    run_next()
    for d in range(2):
        for m in range(3):
            got = q_landing(d, rank_of(m))
            far(got, got, send_g.at[count + d, m], recv_g.at[count + d, m], pb, ka).wait_recv()
        q_twin(d).start()
    for d in range(2):
        got = fq.at[2 * d + 1 - core]
        far(got, got, send_c.at[count + d], recv_c.at[count + d], sibling, ka).wait_recv()
    for n in range(SPAN):
        for part in range(3):
            col = part * D + n * WIDE
            qkv[:, col : col + WIDE] = fq[n, :, part * WIDE : (part + 1) * WIDE].astype(F32)
    qkv_copy = pltpu.make_async_copy(qkv, qkv_out, out_sem.at[1])
    qkv_copy.start()
    for n in range(count):
        finish(n)
    for m in range(3):
        q_plane(m).wait_send()
        for d in range(2):
            q_all(d, m).wait_send()
    for i in range(1, SPAN):
        q_owner(i).wait_send()
    for d in range(2):
        q_twin(d).wait_send()
        swap(d).wait_send()
    for n in range(SPAN):
        mine, remote = outgoing(n)

        @pl.when(jnp.logical_not(mine))
        def _():
            remote.wait_send()

        mine_b = (core == side) & (ka == n)

        @pl.when(jnp.logical_not(mine_b))
        def _():
            home_copy(n).wait_send()

    out_copy.wait()
    qkv_copy.wait()


BACKWARD_STEPS = ((('first', 0), ('first', 1)), (), (), (('first', 2), ('first', 3)), (('second', 0),), (('home', 3), ('first', 4), ('second', 1), ('relay', 0)), (('second', 2), ('join', 3), ('relay', 1)), (('second', 3), ('z', 0), ('relay', 2)), (('home', 2), ('second', 4), ('z', 1), ('relay', 3)), (('z', 2), ('join', 2), ('relay', 4)), (('home', 1), ('z', 3), ('twin', 0)), (('z', 4), ('twin', 1), ('twin', 2)), (('twin', 3),), (('twin', 4),))


def backward_call(dah, xg, wq, q, k, v, ah, tot, starts, gd, gu, go, x_in, gain_one, mid):
    outer = lax.axis_size("pb") // 8
    rows = dah.shape[1]
    group = rows * SPAN
    count = len(CHUNKS)
    anyspace = pl.BlockSpec(memory_space=pl.ANY)
    vmem = pl.BlockSpec(memory_space=pltpu.VMEM)
    shape = jax.ShapeDtypeStruct
    dma = pltpu.SemaphoreType.DMA
    vm = pltpu.VMEM
    big = [(h, w) for _, _, h, _, w in CHUNKS]
    small = [(h // 4, w) for h, w in big]
    sq = (wq.shape[1] // 4, wq.shape[2])
    beyond = max(outer - 1, 1)
    held = max(outer, 1)
    spare = (16, 128)
    half = rows // 2
    scratch = (
        [
            vm((SPAN, rows, WIDE), BF),
            vm(xg.shape, BF),
            vm(wq.shape, BF),
            vm(q.shape, BF),
            vm(q.shape, BF),
            vm(q.shape, BF),
            vm(q.shape, BF),
            vm((LOCAL, 8, group), F32),
            vm(q.shape, F32),
            vm(q.shape, F32),
            vm(tot.shape, F32),
            vm((rows, 3 * WIDE), BF),
            vm((2, 2, half, D), BF),
            vm((SPAN, half, D), BF),
            vm((SPAN, half, D), BF),
            vm((D, 3 * WIDE), F32),
            vm(wq.shape, BF),
            vm(x_in.shape, BF),
            vm(mid.shape, F32),
            vm((2, 2, half, D), BF),
            vm((2, half, D), BF),
            vm(wq.shape, BF),
            vm((D // SPAN, 3 * D), F32),
        ]
        + [vm((SPAN,) + s, BF) for s in big]
        + [vm((SPAN,) + s, BF) for s in big]
        + [vm((2, SPAN) + s, BF) for s in small]
        + [vm((SPAN,) + s, BF) for s in small]
        + [vm((2,) + s, BF) for s in small]
        + [vm((2,) + s, BF) for s in small]
        + [vm(s, BF) for s in small]
        + [vm((held,) + (s if outer > 1 else spare), BF) for s in small]
        + [
            vm((3, SPAN) + sq, BF),
            vm((SPAN,) + sq, BF),
            vm((SPAN,) + sq, BF),
            vm((2,) + sq, BF),
            vm((held, 2) + (sq if outer > 1 else spare), BF),
        ]
        + [
            dma((SPAN,)), dma((SPAN,)), dma((SPAN,)), dma((SPAN,)), dma((SPAN,)), dma((2, 2)), dma((2,)), dma((9,)), dma((2,)),
            dma((count,)), dma((count,)), dma((count,)), dma((count + 1, 3)), dma((count + 1, 3)),
            dma((count + 1, 3)), dma((count + 1, 3)), dma((count + 1, beyond)), dma((count + 1, beyond)),
            dma((count + 2, 3)), dma((count + 2, 3)), dma((count + 2,)), dma((count + 2,)), dma((count + 2,)),
        ]
    )
    return pl.pallas_call(
        functools.partial(backward_kernel, outer),
        out_shape=(
            shape((rows, D), F32),
            shape(gd.shape[1:], BF),
            shape(gu.shape[1:], BF),
            shape(go.shape[1:], BF),
            shape((D // SPAN, 3 * D), F32),
        ),
        in_specs=[anyspace] * 8 + [vmem] + [anyspace] * 4 + [vmem, anyspace],
        out_specs=(anyspace,) * 5,
        scratch_shapes=scratch,
        compiler_params=pltpu.CompilerParams(
            collective_id=1, has_side_effects=True, vmem_limit_bytes=60 << 20
        ),
        name="backward_attention",
    )(dah, xg, wq, q, k, v, ah, tot, starts, gd, gu, go, x_in, gain_one, mid)


def body(layer_input, second_start, gain_attn, w_qkv, w_out, gain_mlp, w_up, w_down, d_output):
    rows = layer_input.shape[0]
    kv_index = lax.axis_index("ka")
    (output, d_middle, dah, gd, gu, go, xg, wq, q, k, v, ah, tot, starts) = forward_call(
        layer_input, second_start, gain_attn[None, :], w_qkv, gain_mlp[None, :], d_output, w_out, w_up, w_down
    )
    d_input, fd, fu, fo, total_qkv = backward_call(
        dah, xg, wq, q, k, v, ah, tot, starts, gd, gu, go, layer_input, gain_attn[None, :], d_middle
    )
    total_down = fd.astype(F32)
    total_up = fu.astype(F32)
    total_out = fo[: D // SPAN].astype(F32)
    def gain_grad(weight, grad, gain):
        own = lax.dynamic_slice_in_dim(gain, kv_index * (D // SPAN), D // SPAN)
        return jnp.sum(weight.astype(F32) * grad, axis=1) / own

    total_gain_attn = gain_grad(w_qkv, total_qkv, gain_attn)
    total_gain_mlp = gain_grad(w_up, total_up, gain_mlp)
    entry_count = rows * SPAN * lax.axis_size("pb") * D
    rms = jnp.sqrt(fo[D // SPAN, 0:1].astype(F32) / entry_count)
    return (
        output, d_input, total_gain_attn, total_qkv, total_out, total_gain_mlp, total_up, total_down, rms,
    )


def solution(mesh):
    if mesh.shape["ka"] != SPAN or mesh.shape["pb"] % 8:
        raise ValueError("unsupported mesh")
    placed = (
        P(("pb", "ka"), None), P("pb"), P(), P("ka", None), P("ka", None), P(), P("ka", None), P("ka", None),
        P(("pb", "ka"), None),
    )
    return jax.shard_map(
        body,
        mesh=mesh,
        in_specs=placed,
        out_specs=(
            P(("pb", "ka"), None), P(("pb", "ka"), None), P("ka"), P("ka", None), P("ka", None), P("ka"),
            P("ka", None), P("ka", None), P("ka"),
        ),
        check_vma=False,
    )
```

```python
import functools
import math

import jax
import jax.numpy as jnp
from jax import lax
from jax.experimental import pallas as pl
from jax.experimental.pallas import tpu as pltpu
from jax.sharding import PartitionSpec as P

D = 768
HEADS = 12
HEAD = 64
SPAN = 4
LOCAL = HEADS // SPAN
WIDE = LOCAL * HEAD
LOG2E = 1.4426950408889634
MESH = pl.DeviceIdType.MESH
BF = jnp.bfloat16
F32 = jnp.float32


def mirror(depth, side):
    return depth + side * (SPAN - 1 - 2 * depth)


def neighbours(pb):
    across_x = pb + 2 - 4 * ((pb // 2) % 2)
    across_y = pb + 4 - 8 * ((pb // 4) % 2)
    across_both = across_x + 4 - 8 * ((across_x // 4) % 2)
    return across_x, across_y, across_both


def sibling_of(pb):
    return pb + 1 - 2 * (pb % 2)


def centred(values):
    center = values - jnp.mean(values, axis=1, keepdims=True)
    inverse = lax.rsqrt(jnp.mean(center * center, axis=1, keepdims=True) + 1e-05)
    return center * inverse, inverse


def norm_back(cot, norm, inverse):
    return inverse * (
        cot - jnp.mean(cot, axis=1, keepdims=True) - norm * jnp.mean(cot * norm, axis=1, keepdims=True)
    )


def far(src, dst, send_sem, recv_sem, pb, ka):
    return pltpu.make_async_remote_copy(
        src, dst, send_sem, recv_sem, device_id=(pb, ka), device_id_type=MESH
    )


def greet(peers):
    barrier = pltpu.get_barrier_semaphore()
    for peer in peers:
        pl.semaphore_signal(barrier, 1, device_id=peer, device_id_type=MESH)
    return barrier


def dot_nt(left, right):
    return lax.dot_general(left, right, (((1,), (1,)), ((), ())), preferred_element_type=F32)


def dot_tn(left, right):
    return lax.dot_general(left, right, (((0,), (0,)), ((), ())), preferred_element_type=F32)


def dot_nn(left, right):
    return jnp.dot(left, right, preferred_element_type=F32)


def fold_lanes(tile):
    out = tile[:, :128]
    for at in range(128, tile.shape[1], 128):
        out = out + tile[:, at : at + 128]
    return out


THIRDS = 3
EARLY = 5
PIECES = 1 + 2 * THIRDS
FORWARD_STEPS = ((), (), (('plane', 0),), (('plane', 1),), (('plane', 2), ('pass', 0)), (('plane', 3), ('pass', 1), ('across', 0)))
AFTER_HEADS = (('pass', 2), ('across', 1), ('plane', 4))
AFTER_BRANCH = (('across', 2), ('pass', 3))
AFTER_NORM = (('pass', 4), ('across', 3))
AFTER_THIRD = ((('across', 4), ('plane', 5), ('plane', 6)), (('pass', 5), ('pass', 6), ('across', 5), ('across', 6)), ())


def forward_kernel(
    x_in, second, gain_one, w_qkv, gain_two, d_out, wo, wu, wd,
    output, mid_out, dah_out, gd_out, gu_out, go_out,
    xg_out, wq_out, q_out, k_out, v_out, ah_out, tot_out, start_out,
    xa, wq4, start, xg, wqs, qs, ks, vs, ahs, tots, ob, starts, ohome, wog, wug, wdg,
    mid, mlp_in, macc, dacc, gd, gu, go, dah, final,
    send_x, recv_x, send_q, recv_q, send_w, recv_w, send_s, recv_s, send_o, recv_o,
    send_z, recv_z, send_p, recv_p, send_c, recv_c, own_sem, out_sem, gd_sem, gu_sem,
):
    pb = lax.axis_index("pb")
    ka = lax.axis_index("ka")
    core = pb % 2
    base = pb - core
    side = ka // 2
    depth = mirror(ka, side)
    home_u = mirror(ka, core)
    quarter = 2 * depth + core
    sibling = sibling_of(pb)
    plane = neighbours(pb)
    rows = x_in.shape[0]
    rank = (pb // 2) % 4

    barrier = greet(
        [(pb, (ka + i) % SPAN) for i in range(1, SPAN)]
        + [(sibling, (ka + i) % SPAN) for i in range(SPAN)]
        + [(p, ka) for p in plane]
    )

    start[...] = jnp.full(start.shape, second[0].astype(F32), F32)
    for n in range(SPAN):
        for part in range(3):
            col = part * D + n * WIDE
            wq4[n, :, part * WIDE : (part + 1) * WIDE] = w_qkv[:, col : col + WIDE]
    height = wq4.shape[1] // 4

    def lines(ref, r):
        return ref.at[pl.ds(pl.multiple_of(r * height, 16), height)]

    step_rows = 128

    def first_norm(r, carry):
        at = pl.ds(pl.multiple_of(r * step_rows, step_rows), step_rows)
        norm, _ = centred(x_in[at, :].astype(F32))
        xa[at, :] = (norm * gain_one[...].reshape(1, D)).astype(BF)
        return carry

    lax.fori_loop(0, rows // step_rows, first_norm, 0)

    pl.semaphore_wait(barrier, 2 * SPAN - 1 + 3)
    out_q = []
    for i in range(1, SPAN):
        z = (ka + i) % SPAN
        zd = mirror(z, z // 2)
        out_q.append(
            far(
                lines(wq4.at[2 * zd + core], rank), lines(wqs.at[ka], rank),
                send_q.at[i - 1], recv_q.at[i - 1], pb, z,
            )
        )
    for copy in out_q:
        copy.start()
    own_q = pltpu.make_async_copy(wq4.at[quarter], wqs.at[ka], own_sem.at[0])
    own_q.start()

    tick = rows // 4
    odd = (((home_u + 1) // 2) % 2) * (1 - home_u // 2)
    goal = mirror(1 - odd, core)
    out_x = [
        far(xa.at[pl.ds(t * tick, tick)], xg.at[ka, t], send_x.at[t], recv_x.at[ka, t], base + t // 2, goal)
        for t in (0, 2, 1, 3)
    ]
    for copy in out_x:
        copy.start()

    at_home = core == side

    def near_copies():
        return [
            far(xa.at[pl.ds(t * tick, tick)], xg.at[ka, t], send_x.at[4 + t], recv_x.at[ka, t], sibling, ka)
            for t in range(4)
        ]

    @pl.when(at_home)
    def _():
        for copy in near_copies():
            copy.start()
        for t in range(4):
            xg[ka, t] = xa[t * tick : (t + 1) * tick, :]

    def start_copies():
        out = []
        for n, (d, k) in enumerate(((0, 1), (1, 0), (1, 1))):
            target = base + (core + k) % 2
            out.append(far(start, starts, send_s.at[n], recv_s, target, mirror(d, core)))
        return out

    @pl.when(home_u == 0)
    def _():
        for copy in start_copies():
            copy.start()
        pltpu.make_async_copy(start, starts, recv_s).start()

    own_w = [
        pltpu.make_async_copy(wo, wog.at[ka], own_sem.at[1]),
        pltpu.make_async_copy(wd, wdg.at[ka], own_sem.at[2]),
    ]
    strip = D // THIRDS
    for part in range(THIRDS):
        for z in range(SPAN):
            own_w.append(
                pltpu.make_async_copy(
                    wu.at[:, z * D + part * strip : z * D + (part + 1) * strip],
                    wug.at[ka, part, :, z * strip : (z + 1) * strip],
                    own_sem.at[3 + part * SPAN + z],
                )
            )
    for copy in own_w:
        copy.start()

    def area(n, z, k, r=None):
        if n == 0:
            ref, row0, height, width = wog.at[z], 0, D // SPAN, D // 2
        elif n % 2:
            ref, row0, height, width = wug.at[z, n // 2], 0, D // SPAN, SPAN * strip // 2
        else:
            ref, row0, height, width = wdg.at[z], (n // 2 - 1) * strip, strip, D // 2
        at = pl.ds(pl.multiple_of(k * width, 128), width)
        if r is None:
            return ref.at[pl.ds(row0, height), at]
        return ref.at[pl.ds(pl.multiple_of(row0 + r * (height // 4), 16), height // 4), at]

    def z_copy(n, i):
        ref = area(n, ka, core, rank)
        return far(ref, ref, send_z.at[n, i - 1], recv_z.at[n, i - 1], pb, (ka + i) % SPAN)

    def z_arrival(n, i):
        ref = area(n, (ka - i) % SPAN, core, rank)
        return far(ref, ref, send_z.at[n, i - 1], recv_z.at[n, i - 1], pb, ka)

    def start_along_z():
        for copy in own_w:
            copy.wait()
        for n in range(EARLY):
            for i in (2, 1, 3):
                z_copy(n, i).start()

    @pl.when(depth == 0)
    def _():
        start_along_z()

    def chunk_copies(i, t):
        u = (1 - depth) if i == 0 else i + 1
        b = mirror(u, side)
        n = 2 * i + t
        t = 2 * core + t
        got = xg.at[b, t]
        here = far(got, got, send_x.at[8 + n], recv_x.at[b, t], pb, ka)
        onward = far(got, got, send_x.at[14 + n - 2], recv_x.at[b, t], pb, mirror(0, side)) if i else None
        return here, onward, far(got, got, send_x.at[8 + n], recv_x.at[b, t], sibling, ka)

    def pass_chunk(i, t, inner):
        here, onward, beside = chunk_copies(i, t)
        here.wait_recv()
        if inner and i:
            onward.start()
        beside.start()

    def beside_arrived(i):
        u = (1 - depth) if i == 0 else i + 1
        b = mirror(u, side)
        for t in range(2):
            got = xg.at[b, 2 * (1 - core) + t]
            far(got, got, send_x.at[8], recv_x.at[b, 2 * (1 - core) + t], pb, ka).wait_recv()

    for n in range(1, SPAN):
        mine_q = lines(wqs.at[(ka - n) % SPAN], rank)
        far(mine_q, mine_q, send_q.at[0], recv_q.at[n - 1], pb, ka).wait_recv()
        for m, p in enumerate(plane):
            copy = far(mine_q, mine_q, send_w.at[n - 1, m], recv_w.at[n - 1, m], p, ka)
            copy.start()
            out_q.append(copy)

    @pl.when(depth == 1)
    def _():
        pass_chunk(1, 0, True)
        pass_chunk(1, 1, True)

    pass_chunk(0, 0, False)
    pass_chunk(0, 1, False)
    for i in range(1, SPAN):
        for m, p in enumerate(plane):
            theirs = lines(wqs.at[(ka - i) % SPAN], (p // 2) % 4)
            far(theirs, theirs, send_w.at[i - 1, m], recv_w.at[i - 1, m], p, ka).wait_recv()
    own_q.wait()
    pltpu.make_async_copy(start, starts, recv_s).wait()

    def project(u):
        b = mirror(u, side)
        xb = xg[b].reshape(rows, D)
        at = pl.multiple_of(b * rows, rows)
        for dst, col in ((qs, 0), (ks, WIDE), (vs, 2 * WIDE)):
            w = wqs[:, :, col : col + WIDE].reshape(D, WIDE)
            out = dot_nn(xb, w).astype(BF)
            for h in range(LOCAL):
                dst[h, pl.ds(at, rows), :] = out[:, h * HEAD : (h + 1) * HEAD]

    def plane_copy(n, i, m, r, p):
        ref = area(n, (ka - i) % SPAN, core, r)
        return far(ref, ref, send_p.at[n, i - 1, m], recv_p.at[n, i - 1, m], p, ka)

    def rank_of(m):
        return (plane[m] // 2) % 4

    def begin_plane(n):
        for i in range(1, SPAN):
            z_arrival(n, i).wait_recv()
            for m in range(2):
                plane_copy(n, i, m, rank, plane[m]).start()

    def pass_on(n):
        first = n % 2
        for i in range(1, SPAN):
            plane_copy(n, i, first, rank_of(first), pb).wait_recv()
            plane_copy(n, i, 2, rank_of(first), plane[1 - first]).start()

    def across_copy(n, i):
        ref = area(n, (ka - i) % SPAN, core)
        return far(ref, ref, send_c.at[n, i - 1], recv_c.at[n, i - 1], sibling, ka)

    def begin_across(n):
        other = 1 - n % 2
        for i in range(1, SPAN):
            plane_copy(n, i, other, rank_of(other), pb).wait_recv()
            plane_copy(n, i, 2, rank_of(2), pb).wait_recv()
            across_copy(n, i).start()

    def arrived(n):
        for i in range(1, SPAN):
            ref = area(n, (ka - i) % SPAN, 1 - core)
            far(ref, ref, send_c.at[n, i - 1], recv_c.at[n, i - 1], pb, ka).wait_recv()

    def weights_sent():
        for n in range(PIECES):
            for i in range(1, SPAN):
                z_copy(n, i).wait_send()
                for m in range(3):
                    plane_copy(n, i, m, rank, pb).wait_send()
                across_copy(n, i).wait_send()

    scale = LOG2E / math.sqrt(HEAD)
    one = jnp.where(starts[0:1, 0:1] > (SPAN // 2) * rows + 0.5, 1.0, 0.0)
    sub = 256

    def attend_own(u):
        b = mirror(u, side)

        def head(h, carry):
            for part in range(rows // sub):
                width = (part + 1) * sub
                at = pl.multiple_of(b * rows, rows)
                row0 = pl.multiple_of(b * rows + part * sub, sub)
                s = dot_nt(qs[h, pl.ds(row0, sub), :], ks[h, pl.ds(at, width), :]) * scale
                seen = (
                    lax.broadcasted_iota(jnp.int32, (sub, width), 0) + part * sub
                    >= lax.broadcasted_iota(jnp.int32, (sub, width), 1)
                )
                up = jnp.where(seen, jnp.exp2(s - 1.0), 0.0)
                down = jnp.where(seen, jnp.exp2(-s - 1.0), 0.0)
                tots[h, pl.ds(row0, sub), :] = fold_lanes(up + down)
                ahs[h, pl.ds(row0, sub), :] = dot_nn((up - down).astype(BF), vs[h, pl.ds(at, width), :])
            return carry

        lax.fori_loop(0, LOCAL, head, 0)

    def attend_pair(high, low):
        qb = high + side * (SPAN - 1 - low - high)
        kb = low + side * (SPAN - 1 - low - high)
        same = jnp.where(qb // 2 == kb // 2, 1.0, 0.0)
        keep = jnp.maximum(one, same) > 0.5

        def head(h, carry):
            at = pl.multiple_of(kb * rows, rows)
            for part in range(rows // sub):
                row0 = pl.multiple_of(qb * rows + part * sub, sub)
                s = dot_nt(qs[h, pl.ds(row0, sub), :], ks[h, pl.ds(at, rows), :]) * scale
                up, down = jnp.exp2(s - 1.0), jnp.exp2(-s - 1.0)
                tots[h, pl.ds(row0, sub), :] += jnp.where(keep, fold_lanes(up + down), 0.0)
                ahs[h, pl.ds(row0, sub), :] += jnp.where(
                    keep, dot_nn((up - down).astype(BF), vs[h, pl.ds(at, rows), :]), 0.0
                )
            return carry

        lax.fori_loop(0, LOCAL, head, 0)

    actions = {"plane": begin_plane, "pass": pass_on, "across": begin_across}

    def run_steps(todo):
        for step, n in todo:
            actions[step](n)

    def home_copy(b):
        return far(ob.at[b], ohome.at[quarter], send_o.at[b], recv_o.at[quarter], base + side, b)

    def send_home(u):
        b = mirror(u, side)
        at = pl.ds(pl.multiple_of(b * rows, rows), rows)
        done = []
        for h in range(LOCAL):
            total = jnp.sum(tots[h, at, :], axis=1, keepdims=True)
            heads = ahs[h, at, :] / total
            ahs[h, at, :] = heads
            tots[h, at, :] = jnp.broadcast_to(total, (rows, 128))
            done.append(heads)
        ob[b] = jnp.concatenate(done, axis=1).astype(BF)
        mine = (core == side) & (ka == b)

        @pl.when(jnp.logical_not(mine))
        def _():
            home_copy(b).start()

        @pl.when(mine)
        def _():
            pltpu.make_async_copy(ob.at[b], ohome.at[quarter], recv_o.at[quarter]).start()

    @pl.when(jnp.logical_not(at_home))
    def _():
        for t in range(4):
            far(xg.at[ka, t], xg.at[ka, t], send_x.at[8], recv_x.at[ka, t], pb, ka).wait_recv()

    project(depth)
    attend_own(depth)

    @pl.when(depth == 1)
    def _():
        pass_chunk(2, 0, True)
        pass_chunk(2, 1, True)
        start_along_z()

    run_steps(FORWARD_STEPS[0])
    beside_arrived(0)
    project(1 - depth)
    attend_own(1 - depth)
    attend_pair(1, 0)

    @pl.when(side == 0)
    def _():
        send_home(0)
        send_home(1)

    run_steps(FORWARD_STEPS[1])

    @pl.when(depth == 0)
    def _():
        pass_chunk(1, 0, False)
        pass_chunk(1, 1, False)

    beside_arrived(1)
    project(2)
    attend_own(2)
    attend_pair(2, 1)
    attend_pair(2, 0)

    @pl.when(side == 0)
    def _():
        send_home(2)

    run_steps(FORWARD_STEPS[2])

    @pl.when(depth == 0)
    def _():
        pass_chunk(2, 0, False)
        pass_chunk(2, 1, False)

    beside_arrived(2)
    project(3)
    attend_own(3)

    @pl.when(side == 1)
    def _():
        send_home(3)

    for low in (2, 1, 0):
        attend_pair(3, low)

        @pl.when(side == 1)
        def _(low=low):
            send_home(low)

        run_steps(FORWARD_STEPS[5 - low])

    @pl.when(side == 0)
    def _():
        send_home(3)

    for n in range(EARLY, PIECES):
        for i in (2, 1, 3):
            z_copy(n, i).start()
    saves = [
        pltpu.make_async_copy(src, dst, out_sem.at[n])
        for n, (src, dst) in enumerate(
            (
                (xg, xg_out), (wqs, wq_out), (qs, q_out), (ks, k_out), (vs, v_out),
                (ahs, ah_out), (tots, tot_out), (starts, start_out),
            )
        )
    ]
    for copy in saves:
        copy.start()

    run_steps(AFTER_HEADS)
    arrived(0)
    for n in range(SPAN):
        far(ob.at[0], ohome.at[n], send_o.at[0], recv_o.at[n], pb, ka).wait_recv()

    branch = dot_nn(ohome[0], wog[0])
    for n in range(1, SPAN):
        branch = branch + dot_nn(ohome[n], wog[n])
    mid[...] = branch
    run_steps(AFTER_BRANCH)

    def second_norm(r, sums):
        at = pl.ds(pl.multiple_of(r * step_rows, step_rows), step_rows)
        x32 = x_in[at, :].astype(F32)
        term = mid[at, :]
        middle = x32 + term
        norm, _ = centred(middle)
        mid[at, :] = middle
        mlp_in[at, :] = (norm * gain_two[...].reshape(1, D)).astype(BF)
        return tuple(
            s + fold_lanes(jnp.sum(t * t, axis=0, keepdims=True))
            for s, t in zip(sums, (x32, term, middle))
        )

    zero = jnp.zeros((1, 128), F32)
    sums = lax.fori_loop(0, rows // step_rows, second_norm, (zero, zero, zero))
    run_steps(AFTER_NORM)
    macc[...] = jnp.zeros_like(macc)
    dacc[...] = jnp.zeros_like(dacc)

    def store_all(part, pair, slot):
        row0 = part * strip
        copies = [
            pltpu.make_async_copy(
                gd.at[slot], gd_out.at[pl.ds(2 * pair, 2), pl.ds(row0, strip)], gd_sem.at[slot]
            )
        ]
        for n in range(2):
            cols = pl.ds(pl.multiple_of((2 * pair + n) * D + row0, strip), strip)
            copies.append(
                pltpu.make_async_copy(
                    gu.at[slot, :, :, n * strip : (n + 1) * strip], gu_out.at[:, :, cols], gu_sem.at[slot, n]
                )
            )
        return copies

    root = math.sqrt(2.0 / math.pi)

    for part in range(THIRDS):
        arrived(1 + 2 * part)
        arrived(2 + 2 * part)

        def feed(pair, carry):
            at = pl.ds(pl.multiple_of(pair * 2 * strip, 2 * strip), 2 * strip)
            w_up = wug[:, part, :, at].reshape(D, 2 * strip)
            w_down = wdg[pl.ds(2 * pair, 2), part * strip : (part + 1) * strip, :].reshape(2 * strip, D)
            up = dot_nn(mlp_in[...], w_up)
            bend = jnp.tanh(root * (up + 0.044715 * (up * up * up)))
            act = (0.5 * up * (1.0 + bend)).astype(BF)
            slope = 0.5 * (1.0 + bend) + 0.5 * up * (1.0 - bend * bend) * (root * (1.0 + 0.134145 * (up * up)))
            macc[...] += dot_nn(act, w_down)
            d_up = (slope * dot_nt(d_out[...], w_down)).astype(BF)
            dacc[...] += dot_nt(d_up, w_up)
            if part:
                for copy in store_all(part - 1, pair, pair):
                    copy.wait()
            gd[pair] = dot_tn(act, d_out[...]).astype(BF).reshape(2, strip, D)
            gu[pair] = dot_tn(mlp_in[...], d_up).astype(BF).reshape(SPAN, D // SPAN, 2 * strip)
            for copy in store_all(part, pair, pair):
                copy.start()
            return carry

        lax.fori_loop(0, 2, feed, 0)
        run_steps(AFTER_THIRD[part])

    def finish_rows(r, total):
        at = pl.ds(pl.multiple_of(r * step_rows, step_rows), step_rows)
        middle = mid[at, :]
        norm, inverse = centred(middle)
        term = macc[at, :]
        final[at, :] = (middle + term).astype(BF)
        d_middle = d_out[at, :].astype(F32) + norm_back(dacc[at, :] * gain_two[...].reshape(1, D), norm, inverse)
        mid[at, :] = d_middle
        mlp_in[at, :] = d_middle.astype(BF)
        return total + fold_lanes(jnp.sum(term * term, axis=0, keepdims=True))

    last = lax.fori_loop(0, rows // step_rows, finish_rows, zero)
    ends = [
        pltpu.make_async_copy(src, dst, out_sem.at[8 + n])
        for n, (src, dst) in enumerate(((mid, mid_out), (final, output)))
    ]
    for copy in ends:
        copy.start()
    corner = (lax.broadcasted_iota(jnp.int32, (64, D), 0) == 0) & (
        lax.broadcasted_iota(jnp.int32, (64, D), 1) == 0
    )
    for n in range(SPAN):
        dah[n] = dot_nt(mlp_in[...], wog[n]).astype(BF)
        go[n, : D // SPAN, :] = dot_tn(ohome[n], mlp_in[...]).astype(BF)
        value = jnp.sum((sums + (last,))[n], axis=1, keepdims=True)
        go[n, D // SPAN :, :] = jnp.where(corner, value, 0.0).astype(BF)
    ends += [
        pltpu.make_async_copy(src, dst, out_sem.at[10 + n])
        for n, (src, dst) in enumerate(((dah, dah_out), (go, go_out)))
    ]
    for copy in ends[2:]:
        copy.start()
    for pair in range(2):
        for copy in store_all(THIRDS - 1, pair, pair):
            copy.wait()
    for copy in saves + ends:
        copy.wait()
    for copy in out_x + out_q:
        copy.wait_send()
    weights_sent()
    for i in range(3):
        for t in range(2):
            _, onward, beside = chunk_copies(i, t)
            beside.wait_send()
            if i:

                @pl.when(depth == 1)
                def _(onward=onward):
                    onward.wait_send()

    @pl.when(at_home)
    def _():
        for copy in near_copies():
            copy.wait_send()

    @pl.when(home_u == 0)
    def _():
        for copy in start_copies():
            copy.wait_send()

    for b in range(SPAN):
        mine = (core == side) & (ka == b)

        @pl.when(jnp.logical_not(mine))
        def _(b=b):
            home_copy(b).wait_send()


def forward_call(x_in, second, gain_one, w_qkv, gain_two, d_out, wo, wu, wd):
    rows = x_in.shape[0]
    group = rows * SPAN
    anyspace = pl.BlockSpec(memory_space=pl.ANY)
    vmem = pl.BlockSpec(memory_space=pltpu.VMEM)
    shape = jax.ShapeDtypeStruct
    dma = pltpu.SemaphoreType.DMA
    vm = pltpu.VMEM
    count = PIECES
    tokens = (SPAN, 4, rows // 4, D)
    columns = (SPAN, D // SPAN, 3 * WIDE)
    heads = (LOCAL, group, HEAD)
    outs = (
        shape((rows, D), BF),
        shape((rows, D), F32),
        shape((SPAN, rows, WIDE), BF),
        shape((SPAN, D, D), BF),
        shape((SPAN, D // SPAN, SPAN * D), BF),
        shape((SPAN, D // SPAN + 64, D), BF),
        shape(tokens, BF),
        shape(columns, BF),
        shape(heads, BF),
        shape(heads, BF),
        shape(heads, BF),
        shape(heads, F32),
        shape((LOCAL, group, 128), F32),
        shape((8, 128), F32),
    )
    scratch = [
        vm((rows, D), BF),
        vm(columns, BF),
        vm((8, 128), F32),
        vm(tokens, BF),
        vm(columns, BF),
        vm(heads, BF),
        vm(heads, BF),
        vm(heads, BF),
        vm(heads, F32),
        vm((LOCAL, group, 128), F32),
        vm((SPAN, rows, WIDE), BF),
        vm((8, 128), F32),
        vm((SPAN, rows, WIDE), BF),
        vm((SPAN,) + wo.shape, BF),
        vm((SPAN, THIRDS, D // SPAN, SPAN * D // THIRDS), BF),
        vm((SPAN,) + wd.shape, BF),
        vm((rows, D), F32),
        vm((rows, D), BF),
        vm((rows, D), F32),
        vm((rows, D), F32),
        vm((2, 2, D // THIRDS, D), BF),
        vm((2, SPAN, D // SPAN, 2 * D // THIRDS), BF),
        vm((SPAN, D // SPAN + 64, D), BF),
        vm((SPAN, rows, WIDE), BF),
        vm((rows, D), BF),
        dma((18,)), dma((SPAN, 4)), dma((3,)), dma((3,)), dma((3, 3)), dma((3, 3)), dma((3,)), dma,
        dma((SPAN,)), dma((SPAN,)),
        dma((count, 3)), dma((count, 3)), dma((count, 3, 3)), dma((count, 3, 3)), dma((count, 3)), dma((count, 3)),
        dma((3 + SPAN * THIRDS,)), dma((12,)), dma((2,)), dma((2, 2)),
    ]
    return pl.pallas_call(
        forward_kernel,
        out_shape=outs,
        in_specs=[vmem, pl.BlockSpec(memory_space=pltpu.SMEM), vmem, vmem, vmem, vmem] + [anyspace] * 3,
        out_specs=(anyspace,) * len(outs),
        scratch_shapes=scratch,
        compiler_params=pltpu.CompilerParams(
            collective_id=0, has_side_effects=True, vmem_limit_bytes=60 << 20
        ),
        name="forward_layer",
    )(x_in, second, gain_one, w_qkv, gain_two, d_out, wo, wu, wd)


CHUNKS = (
    (0, 0, 384, 0, 384),
    (0, 384, 384, 0, 384),
    (1, 0, 192, 0, 768),
    (1, 0, 192, 768, 768),
    (2, 0, 256, 0, 384),
)


def backward_kernel(
    outer, dah, xg_in, wq_in, q_in, k_in, v_in, ah_in, tot_in, starts, gd, gu, go, x_in, gain_one, mid_in,
    d_input, fd, fu, fo, qkv_out,
    da, xg, wqs, qs, ks, vs, dms, deltas, dqs, dks, dvs, joint, own, mate, back, grad_q, gq,
    x_own, mid, dxh, through, fq, qkv,
    *refs,
):
    count = len(CHUNKS)
    halves, mates, firsts, seconds, relays, zs, fins, slots = (refs[i * count : (i + 1) * count] for i in range(8))
    refs = refs[8 * count :]
    fours_q, sum_q, zq, fin_q, slots_q = refs[:5]
    (
        send_a, recv_a, send_m, recv_m, send_h, recv_h, recv_t, in_sem, out_sem,
        own_sem, send_n, recv_n, send_p, recv_p, send_z, recv_z, send_o, recv_o,
        send_g, recv_g, send_c, recv_c, keep_sem,
    ) = refs[5:]
    pb = lax.axis_index("pb")
    ka = lax.axis_index("ka")
    core = pb % 2
    base = pb - core
    side = ka // 2
    depth = mirror(ka, side)
    sibling = sibling_of(pb)
    plane = neighbours(pb)
    rank = (pb // 2) % 4
    where = pb // 8
    beyond = [(pb + 8 * o) % (8 * outer) for o in range(1, outer)]
    rows = dah.shape[1]
    half = rows // 2

    barrier = greet(
        [(pb, (ka + i) % SPAN) for i in range(1, SPAN)]
        + [(sibling, (ka + i) % SPAN) for i in range(SPAN)]
        + [(p, ka) for p in plane]
        + [(p, ka) for p in beyond]
    )

    loads = [
        pltpu.make_async_copy(src, dst, in_sem.at[n])
        for n, (src, dst) in enumerate(
            (
                (ah_in, dks), (tot_in, dvs), (q_in, qs), (k_in, ks), (v_in, vs), (xg_in, xg), (wq_in, wqs),
                (x_in, x_own), (mid_in, mid),
            )
        )
    ]
    for copy in loads:
        copy.start()
    pl.semaphore_wait(barrier, 2 * SPAN - 1 + 3 + len(beyond))

    def outgoing(n):
        worker_depth, worker_core = n // 2, n % 2
        target, spot = base + worker_core, mirror(worker_depth, core)
        mine = (target == pb) & (spot == ka)
        return mine, far(dah.at[n], da.at[ka], send_a.at[n], recv_a.at[ka], target, spot)

    for n in range(SPAN):
        mine, remote = outgoing(n)

        @pl.when(jnp.logical_not(mine))
        def _():
            remote.start()

        @pl.when(mine)
        def _():
            pltpu.make_async_copy(dah.at[n], da.at[ka], recv_a.at[ka]).start()

    sources = (gd, gu, go)
    results = (fd, fu, fo)

    def block_of(ref, n, k, row0, height):
        _, _, _, col0, width = CHUNKS[n]
        at = pl.multiple_of(k * (ref.shape[-1] // 2) + col0, 128)
        return pl.ds(row0, height), pl.ds(at, width)

    def source(n, k):
        a, row0, height, _, _ = CHUNKS[n]
        r, c = block_of(sources[a], n, k, row0, height)
        return sources[a].at[:, r, c]

    def quarter(n, r):
        height = CHUNKS[n][2] // 4
        return pl.ds(pl.multiple_of(r * height, 16), height)

    def landing(n, r):
        a, row0, height, _, _ = CHUNKS[n]
        rr, c = block_of(results[a], n, core, pl.multiple_of(row0 + r * (height // 4), 16), height // 4)
        return results[a].at[rr, c]

    def strip(n, k):
        a, row0, height, _, _ = CHUNKS[n]
        r, c = block_of(results[a], n, k, row0, height)
        return results[a].at[r, c]

    def local_half(n):
        return pltpu.make_async_copy(source(n, core), halves[n], own_sem.at[n])

    def to_sibling(n):
        return far(source(n, 1 - core), mates[n], send_n.at[n], recv_n.at[n], sibling, ka)

    def rank_of(m):
        return (plane[m] // 2) % 4

    def to_first(n, m):
        first = n % 2
        r = rank_of((first, 2)[m])
        return far(
            halves[n].at[:, quarter(n, r), :], firsts[n].at[m], send_p.at[n, m], recv_p.at[n, m], plane[first], ka
        )

    def to_second(n):
        other = 1 - n % 2
        return far(
            halves[n].at[:, quarter(n, rank_of(other)), :], seconds[n], send_p.at[n, 2], recv_p.at[n, 2],
            plane[other], ka,
        )

    inner = (ka + ka // 2) % 2
    partner = ka + 1 - 2 * (ka % 2)
    far_side = 2 - 2 * (ka // 2)

    def to_partner(n):
        return far(
            halves[n].at[partner, quarter(n, rank), :], zs[n].at[0], send_z.at[n, 0], recv_z.at[n, 0], pb, partner
        )

    def to_relay(n):
        return far(
            halves[n].at[pl.ds(far_side, 2), quarter(n, rank), :], relays[n], send_z.at[n, 1], recv_z.at[n, 2],
            pb, partner,
        )

    def to_far(n, i):
        return far(
            halves[n].at[far_side + i, quarter(n, rank), :], zs[n].at[1], send_z.at[n, 1 + i], recv_z.at[n, 1],
            pb, far_side + i,
        )

    def keep(n):
        return pltpu.make_async_copy(fins[n], landing(n, rank), keep_sem.at[n])

    def to_all(n, m):
        return far(fins[n], landing(n, rank), send_g.at[n, m], recv_g.at[n, m], plane[m], ka)

    def to_twin(n):
        return far(strip(n, core), strip(n, core), send_c.at[n], recv_c.at[n], sibling, ka)

    def merge_sibling(n):
        local_half(n).wait()
        to_sibling(n).wait_recv()

        def add(z, carry):
            halves[n][z] = (halves[n][z].astype(F32) + mates[n][z].astype(F32)).astype(BF)
            return carry

        lax.fori_loop(0, SPAN, add, 0)
        if n < 2:
            begin_first(n)

    def begin_first(n):
        for m in (1, 0):
            to_first(n, m).start()

    def merge_first(n):
        for m in (1, 0):
            to_first(n, m).wait_recv()
            held = quarter(n, (rank, rank_of(1 - n % 2))[m])

            def add(z, carry):
                halves[n][z, held, :] = (halves[n][z, held, :].astype(F32) + firsts[n][m, z].astype(F32)).astype(BF)
                return carry

            lax.fori_loop(0, SPAN, add, 0)
            if m:
                to_second(n).start()

    def merge_second(n):
        to_second(n).wait_recv()
        held = quarter(n, rank)

        def add(z, carry):
            halves[n][z, held, :] = (halves[n][z, held, :].astype(F32) + seconds[n][z].astype(F32)).astype(BF)
            return carry

        lax.fori_loop(0, SPAN, add, 0)
        @pl.when(inner == 0)
        def _():
            to_relay(n).start()

        to_partner(n).start()

    def merge_relay(n):
        @pl.when(inner == 1)
        def _():
            to_relay(n).wait_recv()
            held = quarter(n, rank)
            for i in range(2):
                z = far_side + i
                halves[n][z, held, :] = (halves[n][z, held, :].astype(F32) + relays[n][i].astype(F32)).astype(BF)
                to_far(n, i).start()

    def merge_beyond(fin, slot, n):
        for o, p in enumerate(beyond):
            far(fin, slot.at[where], send_o.at[n, o], recv_o.at[n, o], p, ka).start()
        slot[where] = fin[...]
        for o in range(outer - 1):
            far(slot.at[0], slot.at[0], send_o.at[n, o], recv_o.at[n, o], pb, ka).wait()
        total = slot[0].astype(F32)
        for o in range(1, outer):
            total = total + slot[o].astype(F32)
        fin[...] = total.astype(BF)

    def merge_z(n):
        to_partner(n).wait_recv()
        to_far(n, 0).wait_recv()
        total = halves[n][ka, quarter(n, rank), :].astype(F32) + zs[n][0].astype(F32) + zs[n][1].astype(F32)
        fins[n][...] = total.astype(BF)
        if outer > 1:
            merge_beyond(fins[n], slots[n], n)
        keep(n).start()
        for m in range(3):
            to_all(n, m).start()

    def pass_twin(n):
        keep(n).wait()
        for m in range(3):
            got = landing(n, (plane[m] // 2) % 4)
            far(got, got, send_g.at[n, m], recv_g.at[n, m], pb, ka).wait_recv()
        to_twin(n).start()

    def finish(n):
        got = strip(n, 1 - core)
        far(got, got, send_c.at[n], recv_c.at[n], sibling, ka).wait_recv()
        to_sibling(n).wait_send()
        for m in range(3):
            to_all(n, m).wait_send()
        for m in range(2):
            to_first(n, m).wait_send()
        to_second(n).wait_send()
        to_partner(n).wait_send()

        @pl.when(inner == 0)
        def _():
            to_relay(n).wait_send()

        @pl.when(inner == 1)
        def _():
            for i in range(2):
                to_far(n, i).wait_send()

        to_twin(n).wait_send()

    for n in range(count):
        local_half(n).start()
        to_sibling(n).start()

    dqs[...] = jnp.zeros_like(dqs)

    for n in range(count):
        merge_sibling(n)

    for copy in loads[:5]:
        copy.wait()

    scale = LOG2E / math.sqrt(HEAD)
    unit = 1.0 / math.sqrt(HEAD)
    one = jnp.where(starts[0:1, 0:1] > (SPAN // 2) * rows + 0.5, 1.0, 0.0)
    sub = 256

    def prepare(u):
        b = mirror(u, side)
        far(dah.at[0], da.at[b], send_a.at[0], recv_a.at[b], pb, ka).wait_recv()
        block = da[b].astype(F32)
        rows_b = pl.ds(pl.multiple_of(b * rows, rows), rows)
        for h in range(LOCAL):
            scaled = block[:, h * HEAD : (h + 1) * HEAD] / dvs[h, rows_b, :HEAD]
            dms[h, rows_b, :] = scaled.astype(BF)
            deltas[h, :, rows_b] = lax.dot_general(
                jnp.ones((8, HEAD), F32), scaled * dks[h, rows_b, :],
                (((1,), (1,)), ((), ())), precision=lax.Precision.HIGHEST, preferred_element_type=F32,
            )
            dvs[h, rows_b, :] = jnp.zeros((rows, 128), F32)
            dks[h, rows_b, :] = jnp.zeros((rows, HEAD), F32)

    for u in (depth, 1 - depth, 2, 3):
        prepare(u)

    def tile(h, row0, height, at, width, seen=None, keep_it=None):
        q = qs[h, pl.ds(row0, height), :]
        dm = dms[h, pl.ds(row0, height), :]
        keys = ks[h, pl.ds(at, width), :]
        s = dot_nt(keys, q) * scale
        up, down = jnp.exp2(s - 1.0), jnp.exp2(-s - 1.0)
        if seen is not None:
            up = jnp.where(seen, up, 0.0)
            down = jnp.where(seen, down, 0.0)
        expo, sine = up + down, up - down
        dsig = dot_nt(vs[h, pl.ds(at, width), :], dm)
        delta = deltas[h, 0:1, pl.ds(row0, height)]
        ds = (expo * dsig - sine * delta).astype(BF)
        dk, dv, dq = dot_nn(ds, q), dot_nn(sine.astype(BF), dm), dot_tn(ds, keys)
        if keep_it is not None:
            dk, dv, dq = (jnp.where(keep_it, t, 0.0) for t in (dk, dv, dq))
        dks[h, pl.ds(at, width), :] += dk
        dvs[h, pl.ds(at, width), :HEAD] += dv
        dqs[h, pl.ds(row0, height), :] += dq

    def attend_own(u):
        b = mirror(u, side)

        def head(h, carry):
            for part in range(rows // sub):
                height = rows - part * sub
                at = pl.multiple_of(b * rows + part * sub, sub)
                seen = lax.broadcasted_iota(jnp.int32, (sub, height), 0) <= lax.broadcasted_iota(
                    jnp.int32, (sub, height), 1
                )
                tile(h, at, height, at, sub, seen=seen)
            return carry

        lax.fori_loop(0, LOCAL, head, 0)

    def attend_pair(high, low):
        qb = high + side * (SPAN - 1 - low - high)
        kb = low + side * (SPAN - 1 - low - high)
        same = jnp.where(qb // 2 == kb // 2, 1.0, 0.0)
        keep_it = jnp.maximum(one, same) > 0.5

        def head(h, carry):
            for part in range(rows // sub):
                tile(
                    h, pl.multiple_of(qb * rows, rows), rows,
                    pl.multiple_of(kb * rows + part * sub, sub), sub, keep_it=keep_it,
                )
            return carry

        lax.fori_loop(0, LOCAL, head, 0)

    def home_copy(b):
        return far(back.at[b], dxh.at[depth, core], send_h.at[b], recv_h.at[depth, core], base + side, b)

    def swap(u):
        return far(own.at[u % 2, 1 - core], mate.at[u], send_m.at[u], recv_m.at[u], sibling, ka)

    half = rows // 2

    def block_done(u):
        b = mirror(u, side)
        at = pl.ds(pl.multiple_of(b * rows, rows), rows)
        joint[...] = jnp.concatenate(
            [(dqs[h, at, :] * unit).astype(BF) for h in range(LOCAL)]
            + [(dks[h, at, :] * unit).astype(BF) for h in range(LOCAL)]
            + [dvs[h, at, :HEAD].astype(BF) for h in range(LOCAL)],
            axis=1,
        )
        if u < 2:
            swap(u + 2).wait_send()
        own[u % 2] = dot_nt(joint[...], wqs[...].reshape(D, 3 * WIDE)).astype(BF).reshape(2, half, D)
        swap(u).start()
        part = dot_tn(xg[b].reshape(rows, D), joint[...])
        if u == SPAN - 1:
            grad_q[...] = part
        else:
            grad_q[...] += part

    def send_home(u):
        b = mirror(u, side)
        swap(u).wait_recv()
        back[b] = (own[u % 2, core].astype(F32) + mate[u].astype(F32)).astype(BF)
        if u >= 2:

            @pl.when(depth == 0)
            def _():
                to_inner(u).start()

            return
        mine = (core == side) & (ka == b)

        @pl.when(jnp.logical_not(mine))
        def _():
            home_copy(b).start()

        @pl.when(mine)
        def _():
            pltpu.make_async_copy(back.at[b], dxh.at[depth, core], recv_h.at[depth, core]).start()

    def to_inner(u):
        b = mirror(u, side)
        return far(back.at[b], through.at[u - 2], send_h.at[b], recv_t.at[u - 2], pb, mirror(1, side))

    def join_home(u):
        b = mirror(u, side)

        @pl.when(depth == 1)
        def _():
            to_inner(u).wait_recv()
            back[b] = (back[b].astype(F32) + through[u - 2].astype(F32)).astype(BF)
            home_copy(b).start()

    steps = {
        "first": merge_first, "second": merge_second, "z": merge_z, "twin": pass_twin, "home": send_home,
        "relay": merge_relay, "join": join_home, "go": begin_first,
    }
    todo = [list(row) for row in BACKWARD_STEPS]

    def run_next():
        for step, n in todo.pop(0):
            steps[step](n)

    run_next()
    loads[5].wait()
    loads[6].wait()
    for high in range(SPAN - 1, -1, -1):
        attend_own(high)
        run_next()
        for low in range(high - 1, -1, -1):
            attend_pair(high, low)
            run_next()
        block_done(high)
    gq[...] = grad_q[...].astype(BF).reshape(gq.shape)
    height_q = gq.shape[1] // 4

    def lines(r):
        return pl.ds(pl.multiple_of(r * height_q, 16), height_q)

    def q_plane(m):
        return far(
            gq.at[:, lines(rank_of(m)), :], fours_q.at[m], send_p.at[count, m], recv_p.at[count, m], plane[m], ka
        )

    def q_owner(i):
        z = (ka + i) % SPAN
        return far(sum_q.at[z], zq.at[ka], send_z.at[count, i - 1], recv_z.at[count, i - 1], pb, z)

    def q_landing(d, r):
        return fq.at[2 * d + core, lines(r)]

    def q_all(d, m):
        return far(fin_q.at[d], q_landing(d, rank), send_g.at[count + d, m], recv_g.at[count + d, m], plane[m], ka)

    def q_twin(d):
        ref = fq.at[2 * d + core]
        return far(ref, ref, send_c.at[count + d], recv_c.at[count + d], sibling, ka)

    for m in range(3):
        q_plane(m).start()
    send_home(0)
    run_next()

    for m in range(3):
        q_plane(m).wait_recv()
    mine_q = lines(rank)
    sum_q[...] = (
        gq[:, mine_q, :].astype(F32) + fours_q[0].astype(F32) + fours_q[1].astype(F32) + fours_q[2].astype(F32)
    ).astype(BF)
    for i in (2, 1, 3):
        q_owner(i).start()
    zq[ka] = sum_q[ka]
    run_next()
    def from_chip(d):
        for k in range(2):
            far(back.at[0], dxh.at[d, k], send_h.at[0], recv_h.at[d, k], pb, ka).wait_recv()

    @pl.when(mirror(ka, core) < 2)
    def _():
        from_chip(0)

    @pl.when(mirror(ka, core) >= 2)
    def _():
        dxh[0] = jnp.zeros(dxh.shape[1:], BF)

    from_chip(1)
    loads[7].wait()
    loads[8].wait()
    step_rows = 128

    def input_rows(r, carry):
        at = pl.ds(pl.multiple_of(r * step_rows, step_rows), step_rows)
        inner = pl.ds(pl.multiple_of((r % 2) * step_rows, step_rows), step_rows)
        cot = dxh[0, r // 2, inner, :].astype(F32) + dxh[1, r // 2, inner, :].astype(F32)
        norm, inverse = centred(x_own[at, :].astype(F32))
        mid[at, :] = mid[at, :] + norm_back(cot * gain_one[...].reshape(1, D), norm, inverse)
        return carry

    lax.fori_loop(0, rows // step_rows, input_rows, 0)
    out_copy = pltpu.make_async_copy(mid, d_input, out_sem.at[0])
    out_copy.start()
    for i in range(1, SPAN):
        z = (ka - i) % SPAN
        far(zq.at[z], zq.at[z], send_z.at[count, i - 1], recv_z.at[count, i - 1], pb, z).wait_recv()
    for d in range(2):
        fin_q[d] = (zq[d].astype(F32) + zq[SPAN - 1 - d].astype(F32)).astype(BF)
    if outer > 1:
        merge_beyond(fin_q, slots_q, count)
    for d in range(2):
        fq[2 * d + core, lines(rank), :] = fin_q[d]
        for m in range(3):
            q_all(d, m).start()
    run_next()
    for d in range(2):
        for m in range(3):
            got = q_landing(d, rank_of(m))
            far(got, got, send_g.at[count + d, m], recv_g.at[count + d, m], pb, ka).wait_recv()
        q_twin(d).start()
    for d in range(2):
        got = fq.at[2 * d + 1 - core]
        far(got, got, send_c.at[count + d], recv_c.at[count + d], sibling, ka).wait_recv()
    for n in range(SPAN):
        for part in range(3):
            col = part * D + n * WIDE
            qkv[:, col : col + WIDE] = fq[n, :, part * WIDE : (part + 1) * WIDE].astype(F32)
    qkv_copy = pltpu.make_async_copy(qkv, qkv_out, out_sem.at[1])
    qkv_copy.start()
    for n in range(count):
        finish(n)
    for m in range(3):
        q_plane(m).wait_send()
        for d in range(2):
            q_all(d, m).wait_send()
    for i in range(1, SPAN):
        q_owner(i).wait_send()
    for d in range(2):
        q_twin(d).wait_send()
        swap(d).wait_send()
    for n in range(SPAN):
        mine, remote = outgoing(n)

        @pl.when(jnp.logical_not(mine))
        def _():
            remote.wait_send()

        mine_b = (core == side) & (ka == n)

        @pl.when(jnp.logical_not(mine_b))
        def _():
            home_copy(n).wait_send()

    out_copy.wait()
    qkv_copy.wait()


BACKWARD_STEPS = ((('first', 1), ('first', 0), ('go', 3), ('go', 2), ('go', 4)), (), (), (('second', 0), ('second', 1)), (('relay', 0), ('relay', 1)), (('home', 3), ('first', 2), ('first', 3)), (('join', 3),), (('first', 4), ('second', 2), ('z', 0), ('z', 1)), (('home', 2), ('second', 3), ('relay', 2)), (('join', 2), ('second', 4), ('relay', 3), ('z', 2)), (('home', 1), ('relay', 4), ('twin', 0), ('twin', 1)), (('z', 3), ('z', 4), ('twin', 2)), (('twin', 3),), (('twin', 4),))


def backward_call(dah, xg, wq, q, k, v, ah, tot, starts, gd, gu, go, x_in, gain_one, mid):
    outer = lax.axis_size("pb") // 8
    rows = dah.shape[1]
    group = rows * SPAN
    count = len(CHUNKS)
    anyspace = pl.BlockSpec(memory_space=pl.ANY)
    vmem = pl.BlockSpec(memory_space=pltpu.VMEM)
    shape = jax.ShapeDtypeStruct
    dma = pltpu.SemaphoreType.DMA
    vm = pltpu.VMEM
    big = [(h, w) for _, _, h, _, w in CHUNKS]
    small = [(h // 4, w) for h, w in big]
    sq = (wq.shape[1] // 4, wq.shape[2])
    beyond = max(outer - 1, 1)
    held = max(outer, 1)
    spare = (16, 128)
    half = rows // 2
    scratch = (
        [
            vm((SPAN, rows, WIDE), BF),
            vm(xg.shape, BF),
            vm(wq.shape, BF),
            vm(q.shape, BF),
            vm(q.shape, BF),
            vm(q.shape, BF),
            vm(q.shape, BF),
            vm((LOCAL, 8, group), F32),
            vm(q.shape, F32),
            vm(q.shape, F32),
            vm(tot.shape, F32),
            vm((rows, 3 * WIDE), BF),
            vm((2, 2, half, D), BF),
            vm((SPAN, half, D), BF),
            vm((SPAN, half, D), BF),
            vm((D, 3 * WIDE), F32),
            vm(wq.shape, BF),
            vm(x_in.shape, BF),
            vm(mid.shape, F32),
            vm((2, 2, half, D), BF),
            vm((2, half, D), BF),
            vm(wq.shape, BF),
            vm((D // SPAN, 3 * D), F32),
        ]
        + [vm((SPAN,) + s, BF) for s in big]
        + [vm((SPAN,) + s, BF) for s in big]
        + [vm((2, SPAN) + s, BF) for s in small]
        + [vm((SPAN,) + s, BF) for s in small]
        + [vm((2,) + s, BF) for s in small]
        + [vm((2,) + s, BF) for s in small]
        + [vm(s, BF) for s in small]
        + [vm((held,) + (s if outer > 1 else spare), BF) for s in small]
        + [
            vm((3, SPAN) + sq, BF),
            vm((SPAN,) + sq, BF),
            vm((SPAN,) + sq, BF),
            vm((2,) + sq, BF),
            vm((held, 2) + (sq if outer > 1 else spare), BF),
        ]
        + [
            dma((SPAN,)), dma((SPAN,)), dma((SPAN,)), dma((SPAN,)), dma((SPAN,)), dma((2, 2)), dma((2,)), dma((9,)), dma((2,)),
            dma((count,)), dma((count,)), dma((count,)), dma((count + 1, 3)), dma((count + 1, 3)),
            dma((count + 1, 3)), dma((count + 1, 3)), dma((count + 1, beyond)), dma((count + 1, beyond)),
            dma((count + 2, 3)), dma((count + 2, 3)), dma((count + 2,)), dma((count + 2,)), dma((count + 2,)),
        ]
    )
    return pl.pallas_call(
        functools.partial(backward_kernel, outer),
        out_shape=(
            shape((rows, D), F32),
            shape(gd.shape[1:], BF),
            shape(gu.shape[1:], BF),
            shape(go.shape[1:], BF),
            shape((D // SPAN, 3 * D), F32),
        ),
        in_specs=[anyspace] * 8 + [vmem] + [anyspace] * 4 + [vmem, anyspace],
        out_specs=(anyspace,) * 5,
        scratch_shapes=scratch,
        compiler_params=pltpu.CompilerParams(
            collective_id=1, has_side_effects=True, vmem_limit_bytes=60 << 20
        ),
        name="backward_attention",
    )(dah, xg, wq, q, k, v, ah, tot, starts, gd, gu, go, x_in, gain_one, mid)


def body(layer_input, second_start, gain_attn, w_qkv, w_out, gain_mlp, w_up, w_down, d_output):
    rows = layer_input.shape[0]
    kv_index = lax.axis_index("ka")
    (output, d_middle, dah, gd, gu, go, xg, wq, q, k, v, ah, tot, starts) = forward_call(
        layer_input, second_start, gain_attn, w_qkv, gain_mlp, d_output, w_out, w_up, w_down
    )
    d_input, fd, fu, fo, total_qkv = backward_call(
        dah, xg, wq, q, k, v, ah, tot, starts, gd, gu, go, layer_input, gain_attn, d_middle
    )
    total_down = fd.astype(F32)
    total_up = fu.astype(F32)
    total_out = fo[: D // SPAN].astype(F32)
    def gain_grad(weight, grad, gain):
        own = lax.dynamic_slice_in_dim(gain, kv_index * (D // SPAN), D // SPAN)
        return jnp.sum(weight.astype(F32) * grad, axis=1) / own

    total_gain_attn = gain_grad(w_qkv, total_qkv, gain_attn)
    total_gain_mlp = gain_grad(w_up, total_up, gain_mlp)
    entry_count = rows * SPAN * lax.axis_size("pb") * D
    rms = jnp.sqrt(fo[D // SPAN, 0:1].astype(F32) / entry_count)
    return (
        output, d_input, total_gain_attn, total_qkv, total_out, total_gain_mlp, total_up, total_down, rms,
    )


def solution(mesh):
    if mesh.shape["ka"] != SPAN or mesh.shape["pb"] % 8:
        raise ValueError("unsupported mesh")
    placed = (
        P(("pb", "ka"), None), P("pb"), P(), P("ka", None), P("ka", None), P(), P("ka", None), P("ka", None),
        P(("pb", "ka"), None),
    )
    return jax.shard_map(
        body,
        mesh=mesh,
        in_specs=placed,
        out_specs=(
            P(("pb", "ka"), None), P(("pb", "ka"), None), P("ka"), P("ka", None), P("ka", None), P("ka"),
            P("ka", None), P("ka", None), P("ka"),
        ),
        check_vma=False,
    )
```

```python
import functools
import math

import jax
import jax.numpy as jnp
from jax import lax
from jax.experimental import pallas as pl
from jax.experimental.pallas import tpu as pltpu
from jax.sharding import PartitionSpec as P

D = 768
HEADS = 12
HEAD = 64
SPAN = 4
LOCAL = HEADS // SPAN
WIDE = LOCAL * HEAD
LOG2E = 1.4426950408889634
MESH = pl.DeviceIdType.MESH
BF = jnp.bfloat16
F32 = jnp.float32


def mirror(depth, side):
    return depth + side * (SPAN - 1 - 2 * depth)


def neighbours(pb):
    across_x = pb + 2 - 4 * ((pb // 2) % 2)
    across_y = pb + 4 - 8 * ((pb // 4) % 2)
    across_both = across_x + 4 - 8 * ((across_x // 4) % 2)
    return across_x, across_y, across_both


def sibling_of(pb):
    return pb + 1 - 2 * (pb % 2)


def centred(values):
    center = values - jnp.mean(values, axis=1, keepdims=True)
    inverse = lax.rsqrt(jnp.mean(center * center, axis=1, keepdims=True) + 1e-05)
    return center * inverse, inverse


def norm_back(cot, norm, inverse):
    return inverse * (
        cot - jnp.mean(cot, axis=1, keepdims=True) - norm * jnp.mean(cot * norm, axis=1, keepdims=True)
    )


def far(src, dst, send_sem, recv_sem, pb, ka):
    return pltpu.make_async_remote_copy(
        src, dst, send_sem, recv_sem, device_id=(pb, ka), device_id_type=MESH
    )


def greet(peers):
    barrier = pltpu.get_barrier_semaphore()
    for peer in peers:
        pl.semaphore_signal(barrier, 1, device_id=peer, device_id_type=MESH)
    return barrier


def dot_nt(left, right):
    return lax.dot_general(left, right, (((1,), (1,)), ((), ())), preferred_element_type=F32)


def dot_tn(left, right):
    return lax.dot_general(left, right, (((0,), (0,)), ((), ())), preferred_element_type=F32)


def dot_nn(left, right):
    return jnp.dot(left, right, preferred_element_type=F32)


def fold_lanes(tile):
    out = tile[:, :128]
    for at in range(128, tile.shape[1], 128):
        out = out + tile[:, at : at + 128]
    return out


THIRDS = 3
EARLY = 5
PIECES = 1 + 2 * THIRDS
FORWARD_STEPS = ((), (), (('plane', 0),), (('plane', 1),), (('plane', 2), ('pass', 0)), (('plane', 3), ('pass', 1), ('across', 0)))
AFTER_HEADS = (('pass', 2), ('across', 1), ('plane', 4))
AFTER_BRANCH = (('across', 2), ('pass', 3))
AFTER_NORM = (('pass', 4), ('across', 3))
AFTER_THIRD = ((('across', 4), ('plane', 5), ('plane', 6)), (('pass', 5), ('pass', 6), ('across', 5), ('across', 6)), ())


def forward_kernel(
    x_in, second, gain_one, w_qkv, gain_two, d_out, wo, wu, wd,
    output, mid_out, dah_out, gd_out, gu_out, go_out,
    xg_out, wq_out, q_out, k_out, v_out, ah_out, tot_out, start_out,
    xa, wq4, start, xg, wqs, qs, ks, vs, ahs, tots, ob, starts, ohome, wog, wug, wdg,
    mid, mlp_in, macc, dacc, gd, gu, go, dah, final,
    send_x, recv_x, send_q, recv_q, send_w, recv_w, send_s, recv_s, send_o, recv_o,
    send_z, recv_z, send_p, recv_p, send_c, recv_c, own_sem, out_sem, gd_sem, gu_sem,
):
    pb = lax.axis_index("pb")
    ka = lax.axis_index("ka")
    core = pb % 2
    base = pb - core
    side = ka // 2
    depth = mirror(ka, side)
    home_u = mirror(ka, core)
    quarter = 2 * depth + core
    sibling = sibling_of(pb)
    plane = neighbours(pb)
    rows = x_in.shape[0]
    rank = (pb // 2) % 4

    barrier = greet(
        [(pb, (ka + i) % SPAN) for i in range(1, SPAN)]
        + [(sibling, (ka + i) % SPAN) for i in range(SPAN)]
        + [(p, ka) for p in plane]
    )

    start[...] = jnp.full(start.shape, second[0].astype(F32), F32)
    for n in range(SPAN):
        for part in range(3):
            col = part * D + n * WIDE
            wq4[n, :, part * WIDE : (part + 1) * WIDE] = w_qkv[:, col : col + WIDE]
    height = wq4.shape[1] // 4

    def lines(ref, r):
        return ref.at[pl.ds(pl.multiple_of(r * height, 16), height)]

    step_rows = 128

    def first_norm(r, carry):
        at = pl.ds(pl.multiple_of(r * step_rows, step_rows), step_rows)
        norm, _ = centred(x_in[at, :].astype(F32))
        xa[at, :] = (norm * gain_one[...].reshape(1, D)).astype(BF)
        return carry

    lax.fori_loop(0, rows // step_rows, first_norm, 0)

    pl.semaphore_wait(barrier, 2 * SPAN - 1 + 3)
    out_q = []
    for i in range(1, SPAN):
        z = (ka + i) % SPAN
        zd = mirror(z, z // 2)
        out_q.append(
            far(
                lines(wq4.at[2 * zd + core], rank), lines(wqs.at[ka], rank),
                send_q.at[i - 1], recv_q.at[i - 1], pb, z,
            )
        )
    for copy in out_q:
        copy.start()
    own_q = pltpu.make_async_copy(wq4.at[quarter], wqs.at[ka], own_sem.at[0])
    own_q.start()

    tick = rows // 4
    odd = (((home_u + 1) // 2) % 2) * (1 - home_u // 2)
    goal = mirror(1 - odd, core)
    out_x = [
        far(xa.at[pl.ds(t * tick, tick)], xg.at[ka, t], send_x.at[t], recv_x.at[ka, t], base + t // 2, goal)
        for t in (0, 2, 1, 3)
    ]
    for copy in out_x:
        copy.start()

    at_home = core == side

    def near_copies():
        return [
            far(xa.at[pl.ds(t * tick, tick)], xg.at[ka, t], send_x.at[4 + t], recv_x.at[ka, t], sibling, ka)
            for t in range(4)
        ]

    @pl.when(at_home)
    def _():
        for copy in near_copies():
            copy.start()
        for t in range(4):
            xg[ka, t] = xa[t * tick : (t + 1) * tick, :]

    def start_copies():
        out = []
        for n, (d, k) in enumerate(((0, 1), (1, 0), (1, 1))):
            target = base + (core + k) % 2
            out.append(far(start, starts, send_s.at[n], recv_s, target, mirror(d, core)))
        return out

    @pl.when(home_u == 0)
    def _():
        for copy in start_copies():
            copy.start()
        pltpu.make_async_copy(start, starts, recv_s).start()

    own_w = [
        pltpu.make_async_copy(wo, wog.at[ka], own_sem.at[1]),
        pltpu.make_async_copy(wd, wdg.at[ka], own_sem.at[2]),
    ]
    strip = D // THIRDS
    for part in range(THIRDS):
        for z in range(SPAN):
            own_w.append(
                pltpu.make_async_copy(
                    wu.at[:, z * D + part * strip : z * D + (part + 1) * strip],
                    wug.at[ka, part, :, z * strip : (z + 1) * strip],
                    own_sem.at[3 + part * SPAN + z],
                )
            )
    for copy in own_w:
        copy.start()

    def area(n, z, k, r=None):
        if n == 0:
            ref, row0, height, width = wog.at[z], 0, D // SPAN, D // 2
        elif n % 2:
            ref, row0, height, width = wug.at[z, n // 2], 0, D // SPAN, SPAN * strip // 2
        else:
            ref, row0, height, width = wdg.at[z], (n // 2 - 1) * strip, strip, D // 2
        at = pl.ds(pl.multiple_of(k * width, 128), width)
        if r is None:
            return ref.at[pl.ds(row0, height), at]
        return ref.at[pl.ds(pl.multiple_of(row0 + r * (height // 4), 16), height // 4), at]

    def z_copy(n, i):
        ref = area(n, ka, core, rank)
        return far(ref, ref, send_z.at[n, i - 1], recv_z.at[n, i - 1], pb, (ka + i) % SPAN)

    def z_arrival(n, i):
        ref = area(n, (ka - i) % SPAN, core, rank)
        return far(ref, ref, send_z.at[n, i - 1], recv_z.at[n, i - 1], pb, ka)

    def start_along_z():
        for copy in own_w:
            copy.wait()
        for n in range(EARLY):
            for i in (2, 1, 3):
                z_copy(n, i).start()

    @pl.when(depth == 0)
    def _():
        start_along_z()

    def chunk_copies(i, t):
        u = (1 - depth) if i == 0 else i + 1
        b = mirror(u, side)
        n = 2 * i + t
        t = 2 * core + t
        got = xg.at[b, t]
        here = far(got, got, send_x.at[8 + n], recv_x.at[b, t], pb, ka)
        onward = far(got, got, send_x.at[14 + n - 2], recv_x.at[b, t], pb, mirror(0, side)) if i else None
        return here, onward, far(got, got, send_x.at[8 + n], recv_x.at[b, t], sibling, ka)

    def pass_chunk(i, t, inner):
        here, onward, beside = chunk_copies(i, t)
        here.wait_recv()
        if inner and i:
            onward.start()
        beside.start()

    def beside_arrived(i):
        u = (1 - depth) if i == 0 else i + 1
        b = mirror(u, side)
        for t in range(2):
            got = xg.at[b, 2 * (1 - core) + t]
            far(got, got, send_x.at[8], recv_x.at[b, 2 * (1 - core) + t], pb, ka).wait_recv()

    for n in range(1, SPAN):
        mine_q = lines(wqs.at[(ka - n) % SPAN], rank)
        far(mine_q, mine_q, send_q.at[0], recv_q.at[n - 1], pb, ka).wait_recv()
        for m, p in enumerate(plane):
            copy = far(mine_q, mine_q, send_w.at[n - 1, m], recv_w.at[n - 1, m], p, ka)
            copy.start()
            out_q.append(copy)

    @pl.when(depth == 1)
    def _():
        pass_chunk(1, 0, True)
        pass_chunk(1, 1, True)

    pass_chunk(0, 0, False)
    pass_chunk(0, 1, False)
    for i in range(1, SPAN):
        for m, p in enumerate(plane):
            theirs = lines(wqs.at[(ka - i) % SPAN], (p // 2) % 4)
            far(theirs, theirs, send_w.at[i - 1, m], recv_w.at[i - 1, m], p, ka).wait_recv()
    own_q.wait()
    pltpu.make_async_copy(start, starts, recv_s).wait()

    def project(u):
        b = mirror(u, side)
        xb = xg[b].reshape(rows, D)
        at = pl.multiple_of(b * rows, rows)
        for dst, col in ((qs, 0), (ks, WIDE), (vs, 2 * WIDE)):
            w = wqs[:, :, col : col + WIDE].reshape(D, WIDE)
            out = dot_nn(xb, w).astype(BF)
            for h in range(LOCAL):
                dst[h, pl.ds(at, rows), :] = out[:, h * HEAD : (h + 1) * HEAD]

    def plane_copy(n, i, m, r, p):
        ref = area(n, (ka - i) % SPAN, core, r)
        return far(ref, ref, send_p.at[n, i - 1, m], recv_p.at[n, i - 1, m], p, ka)

    def rank_of(m):
        return (plane[m] // 2) % 4

    def begin_plane(n):
        for i in range(1, SPAN):
            z_arrival(n, i).wait_recv()
            for m in range(2):
                plane_copy(n, i, m, rank, plane[m]).start()

    def pass_on(n):
        first = n % 2
        for i in range(1, SPAN):
            plane_copy(n, i, first, rank_of(first), pb).wait_recv()
            plane_copy(n, i, 2, rank_of(first), plane[1 - first]).start()

    def across_copy(n, i):
        ref = area(n, (ka - i) % SPAN, core)
        return far(ref, ref, send_c.at[n, i - 1], recv_c.at[n, i - 1], sibling, ka)

    def begin_across(n):
        other = 1 - n % 2
        for i in range(1, SPAN):
            plane_copy(n, i, other, rank_of(other), pb).wait_recv()
            plane_copy(n, i, 2, rank_of(2), pb).wait_recv()
            across_copy(n, i).start()

    def arrived(n):
        for i in range(1, SPAN):
            ref = area(n, (ka - i) % SPAN, 1 - core)
            far(ref, ref, send_c.at[n, i - 1], recv_c.at[n, i - 1], pb, ka).wait_recv()

    def weights_sent():
        for n in range(PIECES):
            for i in range(1, SPAN):
                z_copy(n, i).wait_send()
                for m in range(3):
                    plane_copy(n, i, m, rank, pb).wait_send()
                across_copy(n, i).wait_send()

    scale = LOG2E / math.sqrt(HEAD)
    one = jnp.where(starts[0:1, 0:1] > (SPAN // 2) * rows + 0.5, 1.0, 0.0)
    sub = 256

    def attend_own(u):
        b = mirror(u, side)

        def head(h, carry):
            for part in range(rows // sub):
                width = (part + 1) * sub
                at = pl.multiple_of(b * rows, rows)
                row0 = pl.multiple_of(b * rows + part * sub, sub)
                s = dot_nt(qs[h, pl.ds(row0, sub), :], ks[h, pl.ds(at, width), :]) * scale
                seen = (
                    lax.broadcasted_iota(jnp.int32, (sub, width), 0) + part * sub
                    >= lax.broadcasted_iota(jnp.int32, (sub, width), 1)
                )
                up = jnp.where(seen, jnp.exp2(s - 1.0), 0.0)
                down = jnp.where(seen, jnp.exp2(-s - 1.0), 0.0)
                tots[h, pl.ds(row0, sub), :] = fold_lanes(up + down)
                ahs[h, pl.ds(row0, sub), :] = dot_nn((up - down).astype(BF), vs[h, pl.ds(at, width), :])
            return carry

        lax.fori_loop(0, LOCAL, head, 0)

    def attend_pair(high, low):
        qb = high + side * (SPAN - 1 - low - high)
        kb = low + side * (SPAN - 1 - low - high)
        same = jnp.where(qb // 2 == kb // 2, 1.0, 0.0)
        keep = jnp.maximum(one, same) > 0.5

        def head(h, carry):
            at = pl.multiple_of(kb * rows, rows)
            for part in range(rows // sub):
                row0 = pl.multiple_of(qb * rows + part * sub, sub)
                s = dot_nt(qs[h, pl.ds(row0, sub), :], ks[h, pl.ds(at, rows), :]) * scale
                up, down = jnp.exp2(s - 1.0), jnp.exp2(-s - 1.0)
                tots[h, pl.ds(row0, sub), :] += jnp.where(keep, fold_lanes(up + down), 0.0)
                ahs[h, pl.ds(row0, sub), :] += jnp.where(
                    keep, dot_nn((up - down).astype(BF), vs[h, pl.ds(at, rows), :]), 0.0
                )
            return carry

        lax.fori_loop(0, LOCAL, head, 0)

    actions = {"plane": begin_plane, "pass": pass_on, "across": begin_across}

    def run_steps(todo):
        for step, n in todo:
            actions[step](n)

    def home_copy(b):
        return far(ob.at[b], ohome.at[quarter], send_o.at[b], recv_o.at[quarter], base + side, b)

    def send_home(u):
        b = mirror(u, side)
        at = pl.ds(pl.multiple_of(b * rows, rows), rows)
        done = []
        for h in range(LOCAL):
            total = jnp.sum(tots[h, at, :], axis=1, keepdims=True)
            heads = ahs[h, at, :] / total
            ahs[h, at, :] = heads
            tots[h, at, :] = jnp.broadcast_to(total, (rows, 128))
            done.append(heads)
        ob[b] = jnp.concatenate(done, axis=1).astype(BF)
        mine = (core == side) & (ka == b)

        @pl.when(jnp.logical_not(mine))
        def _():
            home_copy(b).start()

        @pl.when(mine)
        def _():
            pltpu.make_async_copy(ob.at[b], ohome.at[quarter], recv_o.at[quarter]).start()

    @pl.when(jnp.logical_not(at_home))
    def _():
        for t in range(4):
            far(xg.at[ka, t], xg.at[ka, t], send_x.at[8], recv_x.at[ka, t], pb, ka).wait_recv()

    project(depth)
    attend_own(depth)

    @pl.when(depth == 1)
    def _():
        pass_chunk(2, 0, True)
        pass_chunk(2, 1, True)
        start_along_z()

    run_steps(FORWARD_STEPS[0])
    beside_arrived(0)
    project(1 - depth)
    attend_own(1 - depth)
    attend_pair(1, 0)

    @pl.when(side == 0)
    def _():
        send_home(0)
        send_home(1)

    run_steps(FORWARD_STEPS[1])

    @pl.when(depth == 0)
    def _():
        pass_chunk(1, 0, False)
        pass_chunk(1, 1, False)

    beside_arrived(1)
    project(2)
    attend_own(2)
    attend_pair(2, 1)
    attend_pair(2, 0)

    @pl.when(side == 0)
    def _():
        send_home(2)

    run_steps(FORWARD_STEPS[2])

    @pl.when(depth == 0)
    def _():
        pass_chunk(2, 0, False)
        pass_chunk(2, 1, False)

    beside_arrived(2)
    project(3)
    attend_own(3)

    @pl.when(side == 1)
    def _():
        send_home(3)

    for low in (2, 1, 0):
        attend_pair(3, low)

        @pl.when(side == 1)
        def _(low=low):
            send_home(low)

        run_steps(FORWARD_STEPS[5 - low])

    @pl.when(side == 0)
    def _():
        send_home(3)

    for n in range(EARLY, PIECES):
        for i in (2, 1, 3):
            z_copy(n, i).start()
    saves = [
        pltpu.make_async_copy(src, dst, out_sem.at[n])
        for n, (src, dst) in enumerate(
            (
                (xg, xg_out), (wqs, wq_out), (qs, q_out), (ks, k_out), (vs, v_out),
                (ahs, ah_out), (tots, tot_out), (starts, start_out),
            )
        )
    ]
    for copy in saves:
        copy.start()

    run_steps(AFTER_HEADS)
    arrived(0)
    for n in range(SPAN):
        far(ob.at[0], ohome.at[n], send_o.at[0], recv_o.at[n], pb, ka).wait_recv()

    branch = dot_nn(ohome[0], wog[0])
    for n in range(1, SPAN):
        branch = branch + dot_nn(ohome[n], wog[n])
    mid[...] = branch
    run_steps(AFTER_BRANCH)

    def second_norm(r, sums):
        at = pl.ds(pl.multiple_of(r * step_rows, step_rows), step_rows)
        x32 = x_in[at, :].astype(F32)
        term = mid[at, :]
        middle = x32 + term
        norm, _ = centred(middle)
        mid[at, :] = middle
        mlp_in[at, :] = (norm * gain_two[...].reshape(1, D)).astype(BF)
        return tuple(
            s + fold_lanes(jnp.sum(t * t, axis=0, keepdims=True))
            for s, t in zip(sums, (x32, term, middle))
        )

    zero = jnp.zeros((1, 128), F32)
    sums = lax.fori_loop(0, rows // step_rows, second_norm, (zero, zero, zero))
    run_steps(AFTER_NORM)
    macc[...] = jnp.zeros_like(macc)
    dacc[...] = jnp.zeros_like(dacc)

    def store_all(part, pair, slot):
        row0 = part * strip
        copies = [
            pltpu.make_async_copy(
                gd.at[slot], gd_out.at[pl.ds(2 * pair, 2), pl.ds(row0, strip)], gd_sem.at[slot]
            )
        ]
        for n in range(2):
            cols = pl.ds(pl.multiple_of((2 * pair + n) * D + row0, strip), strip)
            copies.append(
                pltpu.make_async_copy(
                    gu.at[slot, :, :, n * strip : (n + 1) * strip], gu_out.at[:, :, cols], gu_sem.at[slot, n]
                )
            )
        return copies

    root = math.sqrt(2.0 / math.pi)

    for part in range(THIRDS):
        arrived(1 + 2 * part)
        arrived(2 + 2 * part)

        def feed(pair, carry):
            at = pl.ds(pl.multiple_of(pair * 2 * strip, 2 * strip), 2 * strip)
            w_up = wug[:, part, :, at].reshape(D, 2 * strip)
            w_down = wdg[pl.ds(2 * pair, 2), part * strip : (part + 1) * strip, :].reshape(2 * strip, D)
            up = dot_nn(mlp_in[...], w_up)
            bend = jnp.tanh(root * (up + 0.044715 * (up * up * up)))
            act = (0.5 * up * (1.0 + bend)).astype(BF)
            slope = 0.5 * (1.0 + bend) + 0.5 * up * (1.0 - bend * bend) * (root * (1.0 + 0.134145 * (up * up)))
            macc[...] += dot_nn(act, w_down)
            d_up = (slope * dot_nt(d_out[...], w_down)).astype(BF)
            dacc[...] += dot_nt(d_up, w_up)
            if part:
                for copy in store_all(part - 1, pair, pair):
                    copy.wait()
            gd[pair] = dot_tn(act, d_out[...]).astype(BF).reshape(2, strip, D)
            gu[pair] = dot_tn(mlp_in[...], d_up).astype(BF).reshape(SPAN, D // SPAN, 2 * strip)
            for copy in store_all(part, pair, pair):
                copy.start()
            return carry

        lax.fori_loop(0, 2, feed, 0)
        run_steps(AFTER_THIRD[part])

    def finish_rows(r, total):
        at = pl.ds(pl.multiple_of(r * step_rows, step_rows), step_rows)
        middle = mid[at, :]
        norm, inverse = centred(middle)
        term = macc[at, :]
        final[at, :] = (middle + term).astype(BF)
        d_middle = d_out[at, :].astype(F32) + norm_back(dacc[at, :] * gain_two[...].reshape(1, D), norm, inverse)
        mid[at, :] = d_middle
        mlp_in[at, :] = d_middle.astype(BF)
        return total + fold_lanes(jnp.sum(term * term, axis=0, keepdims=True))

    last = lax.fori_loop(0, rows // step_rows, finish_rows, zero)
    ends = [
        pltpu.make_async_copy(src, dst, out_sem.at[8 + n])
        for n, (src, dst) in enumerate(((mid, mid_out), (final, output)))
    ]
    for copy in ends:
        copy.start()
    corner = (lax.broadcasted_iota(jnp.int32, (64, D), 0) == 0) & (
        lax.broadcasted_iota(jnp.int32, (64, D), 1) == 0
    )
    for n in range(SPAN):
        dah[n] = dot_nt(mlp_in[...], wog[n]).astype(BF)
        go[n, : D // SPAN, :] = dot_tn(ohome[n], mlp_in[...]).astype(BF)
        value = jnp.sum((sums + (last,))[n], axis=1, keepdims=True)
        go[n, D // SPAN :, :] = jnp.where(corner, value, 0.0).astype(BF)
    ends += [
        pltpu.make_async_copy(src, dst, out_sem.at[10 + n])
        for n, (src, dst) in enumerate(((dah, dah_out), (go, go_out)))
    ]
    for copy in ends[2:]:
        copy.start()
    for pair in range(2):
        for copy in store_all(THIRDS - 1, pair, pair):
            copy.wait()
    for copy in saves + ends:
        copy.wait()
    for copy in out_x + out_q:
        copy.wait_send()
    weights_sent()
    for i in range(3):
        for t in range(2):
            _, onward, beside = chunk_copies(i, t)
            beside.wait_send()
            if i:

                @pl.when(depth == 1)
                def _(onward=onward):
                    onward.wait_send()

    @pl.when(at_home)
    def _():
        for copy in near_copies():
            copy.wait_send()

    @pl.when(home_u == 0)
    def _():
        for copy in start_copies():
            copy.wait_send()

    for b in range(SPAN):
        mine = (core == side) & (ka == b)

        @pl.when(jnp.logical_not(mine))
        def _(b=b):
            home_copy(b).wait_send()


def forward_call(x_in, second, gain_one, w_qkv, gain_two, d_out, wo, wu, wd):
    rows = x_in.shape[0]
    group = rows * SPAN
    anyspace = pl.BlockSpec(memory_space=pl.ANY)
    vmem = pl.BlockSpec(memory_space=pltpu.VMEM)
    shape = jax.ShapeDtypeStruct
    dma = pltpu.SemaphoreType.DMA
    vm = pltpu.VMEM
    count = PIECES
    tokens = (SPAN, 4, rows // 4, D)
    columns = (SPAN, D // SPAN, 3 * WIDE)
    heads = (LOCAL, group, HEAD)
    outs = (
        shape((rows, D), BF),
        shape((rows, D), F32),
        shape((SPAN, rows, WIDE), BF),
        shape((SPAN, D, D), BF),
        shape((SPAN, D // SPAN, SPAN * D), BF),
        shape((SPAN, D // SPAN + 64, D), BF),
        shape(tokens, BF),
        shape(columns, BF),
        shape(heads, BF),
        shape(heads, BF),
        shape(heads, BF),
        shape(heads, F32),
        shape((LOCAL, group, 128), F32),
        shape((8, 128), F32),
    )
    scratch = [
        vm((rows, D), BF),
        vm(columns, BF),
        vm((8, 128), F32),
        vm(tokens, BF),
        vm(columns, BF),
        vm(heads, BF),
        vm(heads, BF),
        vm(heads, BF),
        vm(heads, F32),
        vm((LOCAL, group, 128), F32),
        vm((SPAN, rows, WIDE), BF),
        vm((8, 128), F32),
        vm((SPAN, rows, WIDE), BF),
        vm((SPAN,) + wo.shape, BF),
        vm((SPAN, THIRDS, D // SPAN, SPAN * D // THIRDS), BF),
        vm((SPAN,) + wd.shape, BF),
        vm((rows, D), F32),
        vm((rows, D), BF),
        vm((rows, D), F32),
        vm((rows, D), F32),
        vm((2, 2, D // THIRDS, D), BF),
        vm((2, SPAN, D // SPAN, 2 * D // THIRDS), BF),
        vm((SPAN, D // SPAN + 64, D), BF),
        vm((SPAN, rows, WIDE), BF),
        vm((rows, D), BF),
        dma((18,)), dma((SPAN, 4)), dma((3,)), dma((3,)), dma((3, 3)), dma((3, 3)), dma((3,)), dma,
        dma((SPAN,)), dma((SPAN,)),
        dma((count, 3)), dma((count, 3)), dma((count, 3, 3)), dma((count, 3, 3)), dma((count, 3)), dma((count, 3)),
        dma((3 + SPAN * THIRDS,)), dma((12,)), dma((2,)), dma((2, 2)),
    ]
    return pl.pallas_call(
        forward_kernel,
        out_shape=outs,
        in_specs=[vmem, pl.BlockSpec(memory_space=pltpu.SMEM), vmem, vmem, vmem, vmem] + [anyspace] * 3,
        out_specs=(anyspace,) * len(outs),
        scratch_shapes=scratch,
        compiler_params=pltpu.CompilerParams(
            collective_id=0, has_side_effects=True, vmem_limit_bytes=60 << 20
        ),
        name="forward_layer",
    )(x_in, second, gain_one, w_qkv, gain_two, d_out, wo, wu, wd)


CHUNKS = (
    (0, 0, 384, 0, 384),
    (0, 384, 384, 0, 384),
    (1, 0, 192, 0, 768),
    (1, 0, 192, 768, 768),
    (2, 0, 256, 0, 384),
)


def backward_kernel(
    outer, dah, xg_in, wq_in, q_in, k_in, v_in, ah_in, tot_in, starts, gd, gu, go, x_in, gain_one, mid_in,
    d_input, fd, fu, fo, qkv_out,
    da, xg, wqs, qs, ks, vs, dms, deltas, dqs, dks, dvs, joint, own, mate, back, grad_q, gq,
    x_own, mid, dxh, through, fq, qkv,
    *refs,
):
    count = len(CHUNKS)
    halves, mates, firsts, seconds, relays, zs, fins, slots = (refs[i * count : (i + 1) * count] for i in range(8))
    refs = refs[8 * count :]
    fours_q, sum_q, zq, fin_q, slots_q = refs[:5]
    (
        send_a, recv_a, send_m, recv_m, send_h, recv_h, recv_t, in_sem, out_sem,
        own_sem, send_n, recv_n, send_p, recv_p, send_z, recv_z, send_o, recv_o,
        send_g, recv_g, send_c, recv_c, keep_sem,
    ) = refs[5:]
    pb = lax.axis_index("pb")
    ka = lax.axis_index("ka")
    core = pb % 2
    base = pb - core
    side = ka // 2
    depth = mirror(ka, side)
    sibling = sibling_of(pb)
    plane = neighbours(pb)
    rank = (pb // 2) % 4
    where = pb // 8
    beyond = [(pb + 8 * o) % (8 * outer) for o in range(1, outer)]
    rows = dah.shape[1]
    half = rows // 2

    barrier = greet(
        [(pb, (ka + i) % SPAN) for i in range(1, SPAN)]
        + [(sibling, (ka + i) % SPAN) for i in range(SPAN)]
        + [(p, ka) for p in plane]
        + [(p, ka) for p in beyond]
    )

    loads = [
        pltpu.make_async_copy(src, dst, in_sem.at[n])
        for n, (src, dst) in enumerate(
            (
                (ah_in, dks), (tot_in, dvs), (q_in, qs), (k_in, ks), (v_in, vs), (xg_in, xg), (wq_in, wqs),
                (x_in, x_own), (mid_in, mid),
            )
        )
    ]
    for copy in loads:
        copy.start()
    pl.semaphore_wait(barrier, 2 * SPAN - 1 + 3 + len(beyond))

    def outgoing(n):
        worker_depth, worker_core = n // 2, n % 2
        target, spot = base + worker_core, mirror(worker_depth, core)
        mine = (target == pb) & (spot == ka)
        return mine, far(dah.at[n], da.at[ka], send_a.at[n], recv_a.at[ka], target, spot)

    for n in range(SPAN):
        mine, remote = outgoing(n)

        @pl.when(jnp.logical_not(mine))
        def _():
            remote.start()

        @pl.when(mine)
        def _():
            pltpu.make_async_copy(dah.at[n], da.at[ka], recv_a.at[ka]).start()

    sources = (gd, gu, go)
    results = (fd, fu, fo)

    def block_of(ref, n, k, row0, height):
        _, _, _, col0, width = CHUNKS[n]
        at = pl.multiple_of(k * (ref.shape[-1] // 2) + col0, 128)
        return pl.ds(row0, height), pl.ds(at, width)

    def source(n, k):
        a, row0, height, _, _ = CHUNKS[n]
        r, c = block_of(sources[a], n, k, row0, height)
        return sources[a].at[:, r, c]

    def quarter(n, r):
        height = CHUNKS[n][2] // 4
        return pl.ds(pl.multiple_of(r * height, 16), height)

    def landing(n, r):
        a, row0, height, _, _ = CHUNKS[n]
        rr, c = block_of(results[a], n, core, pl.multiple_of(row0 + r * (height // 4), 16), height // 4)
        return results[a].at[rr, c]

    def strip(n, k):
        a, row0, height, _, _ = CHUNKS[n]
        r, c = block_of(results[a], n, k, row0, height)
        return results[a].at[r, c]

    def local_half(n):
        return pltpu.make_async_copy(source(n, core), halves[n], own_sem.at[n])

    def to_sibling(n):
        return far(source(n, 1 - core), mates[n], send_n.at[n], recv_n.at[n], sibling, ka)

    def rank_of(m):
        return (plane[m] // 2) % 4

    def to_first(n, m):
        first = n % 2
        r = rank_of((first, 2)[m])
        return far(
            halves[n].at[:, quarter(n, r), :], firsts[n].at[m], send_p.at[n, m], recv_p.at[n, m], plane[first], ka
        )

    def to_second(n):
        other = 1 - n % 2
        return far(
            halves[n].at[:, quarter(n, rank_of(other)), :], seconds[n], send_p.at[n, 2], recv_p.at[n, 2],
            plane[other], ka,
        )

    inner = (ka + ka // 2) % 2
    partner = ka + 1 - 2 * (ka % 2)
    far_side = 2 - 2 * (ka // 2)

    def to_partner(n):
        return far(
            halves[n].at[partner, quarter(n, rank), :], zs[n].at[0], send_z.at[n, 0], recv_z.at[n, 0], pb, partner
        )

    def to_relay(n):
        return far(
            halves[n].at[pl.ds(far_side, 2), quarter(n, rank), :], relays[n], send_z.at[n, 1], recv_z.at[n, 2],
            pb, partner,
        )

    def to_far(n, i):
        return far(
            halves[n].at[far_side + i, quarter(n, rank), :], zs[n].at[1], send_z.at[n, 1 + i], recv_z.at[n, 1],
            pb, far_side + i,
        )

    def keep(n):
        return pltpu.make_async_copy(fins[n], landing(n, rank), keep_sem.at[n])

    def to_all(n, m):
        return far(fins[n], landing(n, rank), send_g.at[n, m], recv_g.at[n, m], plane[m], ka)

    def to_twin(n):
        return far(strip(n, core), strip(n, core), send_c.at[n], recv_c.at[n], sibling, ka)

    def merge_sibling(n):
        local_half(n).wait()
        to_sibling(n).wait_recv()

        def add(z, carry):
            halves[n][z] = (halves[n][z].astype(F32) + mates[n][z].astype(F32)).astype(BF)
            return carry

        lax.fori_loop(0, SPAN, add, 0)
        if n < 2:
            begin_first(n)

    def begin_first(n):
        for m in (1, 0):
            to_first(n, m).start()

    def merge_first(n):
        for m in (1, 0):
            to_first(n, m).wait_recv()
            held = quarter(n, (rank, rank_of(1 - n % 2))[m])

            def add(z, carry):
                halves[n][z, held, :] = (halves[n][z, held, :].astype(F32) + firsts[n][m, z].astype(F32)).astype(BF)
                return carry

            lax.fori_loop(0, SPAN, add, 0)
            if m:
                to_second(n).start()

    def merge_second(n):
        to_second(n).wait_recv()
        held = quarter(n, rank)

        def add(z, carry):
            halves[n][z, held, :] = (halves[n][z, held, :].astype(F32) + seconds[n][z].astype(F32)).astype(BF)
            return carry

        lax.fori_loop(0, SPAN, add, 0)
        @pl.when(inner == 0)
        def _():
            to_relay(n).start()

        to_partner(n).start()

    def merge_relay(n):
        @pl.when(inner == 1)
        def _():
            to_relay(n).wait_recv()
            held = quarter(n, rank)
            for i in range(2):
                z = far_side + i
                halves[n][z, held, :] = (halves[n][z, held, :].astype(F32) + relays[n][i].astype(F32)).astype(BF)
                to_far(n, i).start()

    def merge_beyond(fin, slot, n):
        for o, p in enumerate(beyond):
            far(fin, slot.at[where], send_o.at[n, o], recv_o.at[n, o], p, ka).start()
        slot[where] = fin[...]
        for o in range(outer - 1):
            far(slot.at[0], slot.at[0], send_o.at[n, o], recv_o.at[n, o], pb, ka).wait()
        total = slot[0].astype(F32)
        for o in range(1, outer):
            total = total + slot[o].astype(F32)
        fin[...] = total.astype(BF)

    def merge_z(n):
        to_partner(n).wait_recv()
        to_far(n, 0).wait_recv()
        total = halves[n][ka, quarter(n, rank), :].astype(F32) + zs[n][0].astype(F32) + zs[n][1].astype(F32)
        fins[n][...] = total.astype(BF)
        if outer > 1:
            merge_beyond(fins[n], slots[n], n)
        keep(n).start()
        for m in range(3):
            to_all(n, m).start()

    def pass_twin(n):
        keep(n).wait()
        for m in range(3):
            got = landing(n, (plane[m] // 2) % 4)
            far(got, got, send_g.at[n, m], recv_g.at[n, m], pb, ka).wait_recv()
        to_twin(n).start()

    def finish(n):
        got = strip(n, 1 - core)
        far(got, got, send_c.at[n], recv_c.at[n], sibling, ka).wait_recv()
        to_sibling(n).wait_send()
        for m in range(3):
            to_all(n, m).wait_send()
        for m in range(2):
            to_first(n, m).wait_send()
        to_second(n).wait_send()
        to_partner(n).wait_send()

        @pl.when(inner == 0)
        def _():
            to_relay(n).wait_send()

        @pl.when(inner == 1)
        def _():
            for i in range(2):
                to_far(n, i).wait_send()

        to_twin(n).wait_send()

    for n in range(count):
        local_half(n).start()
        to_sibling(n).start()

    dqs[...] = jnp.zeros_like(dqs)

    for n in range(count):
        merge_sibling(n)

    for copy in loads[:5]:
        copy.wait()

    scale = LOG2E / math.sqrt(HEAD)
    unit = 1.0 / math.sqrt(HEAD)
    one = jnp.where(starts[0:1, 0:1] > (SPAN // 2) * rows + 0.5, 1.0, 0.0)
    sub = 256

    def prepare(u):
        b = mirror(u, side)
        far(dah.at[0], da.at[b], send_a.at[0], recv_a.at[b], pb, ka).wait_recv()
        block = da[b].astype(F32)
        rows_b = pl.ds(pl.multiple_of(b * rows, rows), rows)
        for h in range(LOCAL):
            scaled = block[:, h * HEAD : (h + 1) * HEAD] / dvs[h, rows_b, :HEAD]
            dms[h, rows_b, :] = scaled.astype(BF)
            deltas[h, :, rows_b] = lax.dot_general(
                jnp.ones((8, HEAD), F32), scaled * dks[h, rows_b, :],
                (((1,), (1,)), ((), ())), precision=lax.Precision.HIGHEST, preferred_element_type=F32,
            )
            dvs[h, rows_b, :] = jnp.zeros((rows, 128), F32)
            dks[h, rows_b, :] = jnp.zeros((rows, HEAD), F32)

    for u in (depth, 1 - depth, 2, 3):
        prepare(u)

    def tile(h, row0, height, at, width, seen=None, keep_it=None):
        q = qs[h, pl.ds(row0, height), :]
        dm = dms[h, pl.ds(row0, height), :]
        keys = ks[h, pl.ds(at, width), :]
        s = dot_nt(keys, q) * scale
        up, down = jnp.exp2(s - 1.0), jnp.exp2(-s - 1.0)
        if seen is not None:
            up = jnp.where(seen, up, 0.0)
            down = jnp.where(seen, down, 0.0)
        expo, sine = up + down, up - down
        dsig = dot_nt(vs[h, pl.ds(at, width), :], dm)
        delta = deltas[h, 0:1, pl.ds(row0, height)]
        ds = (expo * dsig - sine * delta).astype(BF)
        dk, dv, dq = dot_nn(ds, q), dot_nn(sine.astype(BF), dm), dot_tn(ds, keys)
        if keep_it is not None:
            dk, dv, dq = (jnp.where(keep_it, t, 0.0) for t in (dk, dv, dq))
        dks[h, pl.ds(at, width), :] += dk
        dvs[h, pl.ds(at, width), :HEAD] += dv
        dqs[h, pl.ds(row0, height), :] += dq

    def attend_own(u):
        b = mirror(u, side)

        def head(h, carry):
            for part in range(rows // sub):
                height = rows - part * sub
                at = pl.multiple_of(b * rows + part * sub, sub)
                seen = lax.broadcasted_iota(jnp.int32, (sub, height), 0) <= lax.broadcasted_iota(
                    jnp.int32, (sub, height), 1
                )
                tile(h, at, height, at, sub, seen=seen)
            return carry

        lax.fori_loop(0, LOCAL, head, 0)

    def attend_pair(high, low):
        qb = high + side * (SPAN - 1 - low - high)
        kb = low + side * (SPAN - 1 - low - high)
        same = jnp.where(qb // 2 == kb // 2, 1.0, 0.0)
        keep_it = jnp.maximum(one, same) > 0.5

        def head(h, carry):
            for part in range(rows // sub):
                tile(
                    h, pl.multiple_of(qb * rows, rows), rows,
                    pl.multiple_of(kb * rows + part * sub, sub), sub, keep_it=keep_it,
                )
            return carry

        lax.fori_loop(0, LOCAL, head, 0)

    def home_copy(b):
        return far(back.at[b], dxh.at[depth, core], send_h.at[b], recv_h.at[depth, core], base + side, b)

    def swap(u):
        return far(own.at[u % 2, 1 - core], mate.at[u], send_m.at[u], recv_m.at[u], sibling, ka)

    half = rows // 2

    def block_done(u):
        b = mirror(u, side)
        at = pl.ds(pl.multiple_of(b * rows, rows), rows)
        joint[...] = jnp.concatenate(
            [(dqs[h, at, :] * unit).astype(BF) for h in range(LOCAL)]
            + [(dks[h, at, :] * unit).astype(BF) for h in range(LOCAL)]
            + [dvs[h, at, :HEAD].astype(BF) for h in range(LOCAL)],
            axis=1,
        )
        if u < 2:
            swap(u + 2).wait_send()
        own[u % 2] = dot_nt(joint[...], wqs[...].reshape(D, 3 * WIDE)).astype(BF).reshape(2, half, D)
        swap(u).start()
        part = dot_tn(xg[b].reshape(rows, D), joint[...])
        if u == SPAN - 1:
            grad_q[...] = part
        else:
            grad_q[...] += part

    def send_home(u):
        b = mirror(u, side)
        swap(u).wait_recv()
        back[b] = (own[u % 2, core].astype(F32) + mate[u].astype(F32)).astype(BF)
        if u >= 2:

            @pl.when(depth == 0)
            def _():
                to_inner(u).start()

            return
        mine = (core == side) & (ka == b)

        @pl.when(jnp.logical_not(mine))
        def _():
            home_copy(b).start()

        @pl.when(mine)
        def _():
            pltpu.make_async_copy(back.at[b], dxh.at[depth, core], recv_h.at[depth, core]).start()

    def to_inner(u):
        b = mirror(u, side)
        return far(back.at[b], through.at[u - 2], send_h.at[b], recv_t.at[u - 2], pb, mirror(1, side))

    def join_home(u):
        b = mirror(u, side)

        @pl.when(depth == 1)
        def _():
            to_inner(u).wait_recv()
            back[b] = (back[b].astype(F32) + through[u - 2].astype(F32)).astype(BF)
            home_copy(b).start()

    steps = {
        "first": merge_first, "second": merge_second, "z": merge_z, "twin": pass_twin, "home": send_home,
        "relay": merge_relay, "join": join_home, "go": begin_first,
    }
    todo = [list(row) for row in BACKWARD_STEPS]

    def run_next():
        for step, n in todo.pop(0):
            steps[step](n)

    run_next()
    loads[5].wait()
    loads[6].wait()
    for high in range(SPAN - 1, -1, -1):
        attend_own(high)
        run_next()
        for low in range(high - 1, -1, -1):
            attend_pair(high, low)
            run_next()
        block_done(high)
    gq[...] = grad_q[...].astype(BF).reshape(gq.shape)
    height_q = gq.shape[1] // 4

    def lines(r):
        return pl.ds(pl.multiple_of(r * height_q, 16), height_q)

    def q_plane(m):
        return far(
            gq.at[:, lines(rank_of(m)), :], fours_q.at[m], send_p.at[count, m], recv_p.at[count, m], plane[m], ka
        )

    def q_owner(i):
        z = (ka + i) % SPAN
        return far(sum_q.at[z], zq.at[ka], send_z.at[count, i - 1], recv_z.at[count, i - 1], pb, z)

    def q_landing(d, r):
        return fq.at[2 * d + core, lines(r)]

    def q_all(d, m):
        return far(fin_q.at[d], q_landing(d, rank), send_g.at[count + d, m], recv_g.at[count + d, m], plane[m], ka)

    def q_twin(d):
        ref = fq.at[2 * d + core]
        return far(ref, ref, send_c.at[count + d], recv_c.at[count + d], sibling, ka)

    for m in range(3):
        q_plane(m).start()
    send_home(0)
    run_next()

    for m in range(3):
        q_plane(m).wait_recv()
    mine_q = lines(rank)
    sum_q[...] = (
        gq[:, mine_q, :].astype(F32) + fours_q[0].astype(F32) + fours_q[1].astype(F32) + fours_q[2].astype(F32)
    ).astype(BF)
    for i in (2, 1, 3):
        q_owner(i).start()
    zq[ka] = sum_q[ka]
    run_next()
    def from_chip(d):
        for k in range(2):
            far(back.at[0], dxh.at[d, k], send_h.at[0], recv_h.at[d, k], pb, ka).wait_recv()

    @pl.when(mirror(ka, core) < 2)
    def _():
        from_chip(0)

    @pl.when(mirror(ka, core) >= 2)
    def _():
        dxh[0] = jnp.zeros(dxh.shape[1:], BF)

    from_chip(1)
    loads[7].wait()
    loads[8].wait()
    step_rows = 128

    def input_rows(r, carry):
        at = pl.ds(pl.multiple_of(r * step_rows, step_rows), step_rows)
        inner = pl.ds(pl.multiple_of((r % 2) * step_rows, step_rows), step_rows)
        cot = dxh[0, r // 2, inner, :].astype(F32) + dxh[1, r // 2, inner, :].astype(F32)
        norm, inverse = centred(x_own[at, :].astype(F32))
        mid[at, :] = mid[at, :] + norm_back(cot * gain_one[...].reshape(1, D), norm, inverse)
        return carry

    lax.fori_loop(0, rows // step_rows, input_rows, 0)
    out_copy = pltpu.make_async_copy(mid, d_input, out_sem.at[0])
    out_copy.start()
    for i in range(1, SPAN):
        z = (ka - i) % SPAN
        far(zq.at[z], zq.at[z], send_z.at[count, i - 1], recv_z.at[count, i - 1], pb, z).wait_recv()
    for d in range(2):
        fin_q[d] = (zq[d].astype(F32) + zq[SPAN - 1 - d].astype(F32)).astype(BF)
    if outer > 1:
        merge_beyond(fin_q, slots_q, count)
    for d in range(2):
        fq[2 * d + core, lines(rank), :] = fin_q[d]
        for m in range(3):
            q_all(d, m).start()
    run_next()
    for d in range(2):
        for m in range(3):
            got = q_landing(d, rank_of(m))
            far(got, got, send_g.at[count + d, m], recv_g.at[count + d, m], pb, ka).wait_recv()
        q_twin(d).start()
    for d in range(2):
        got = fq.at[2 * d + 1 - core]
        far(got, got, send_c.at[count + d], recv_c.at[count + d], sibling, ka).wait_recv()
    for n in range(SPAN):
        for part in range(3):
            col = part * D + n * WIDE
            qkv[:, col : col + WIDE] = fq[n, :, part * WIDE : (part + 1) * WIDE]
    qkv_copy = pltpu.make_async_copy(qkv, qkv_out, out_sem.at[1])
    qkv_copy.start()
    for n in range(count):
        finish(n)
    for m in range(3):
        q_plane(m).wait_send()
        for d in range(2):
            q_all(d, m).wait_send()
    for i in range(1, SPAN):
        q_owner(i).wait_send()
    for d in range(2):
        q_twin(d).wait_send()
        swap(d).wait_send()
    for n in range(SPAN):
        mine, remote = outgoing(n)

        @pl.when(jnp.logical_not(mine))
        def _():
            remote.wait_send()

        mine_b = (core == side) & (ka == n)

        @pl.when(jnp.logical_not(mine_b))
        def _():
            home_copy(n).wait_send()

    out_copy.wait()
    qkv_copy.wait()


BACKWARD_STEPS = ((('first', 1), ('first', 0), ('go', 3), ('go', 2), ('go', 4)), (), (), (('second', 0), ('second', 1)), (('relay', 0), ('relay', 1)), (('home', 3), ('first', 2), ('first', 3)), (('join', 3),), (('first', 4), ('second', 2), ('z', 0), ('z', 1)), (('home', 2), ('second', 3), ('relay', 2)), (('join', 2), ('second', 4), ('relay', 3), ('z', 2)), (('home', 1), ('relay', 4), ('twin', 0), ('twin', 1)), (('z', 3), ('z', 4), ('twin', 2)), (('twin', 3),), (('twin', 4),))


def backward_call(dah, xg, wq, q, k, v, ah, tot, starts, gd, gu, go, x_in, gain_one, mid):
    outer = lax.axis_size("pb") // 8
    rows = dah.shape[1]
    group = rows * SPAN
    count = len(CHUNKS)
    anyspace = pl.BlockSpec(memory_space=pl.ANY)
    vmem = pl.BlockSpec(memory_space=pltpu.VMEM)
    shape = jax.ShapeDtypeStruct
    dma = pltpu.SemaphoreType.DMA
    vm = pltpu.VMEM
    big = [(h, w) for _, _, h, _, w in CHUNKS]
    small = [(h // 4, w) for h, w in big]
    sq = (wq.shape[1] // 4, wq.shape[2])
    beyond = max(outer - 1, 1)
    held = max(outer, 1)
    spare = (16, 128)
    half = rows // 2
    scratch = (
        [
            vm((SPAN, rows, WIDE), BF),
            vm(xg.shape, BF),
            vm(wq.shape, BF),
            vm(q.shape, BF),
            vm(q.shape, BF),
            vm(q.shape, BF),
            vm(q.shape, BF),
            vm((LOCAL, 8, group), F32),
            vm(q.shape, F32),
            vm(q.shape, F32),
            vm(tot.shape, F32),
            vm((rows, 3 * WIDE), BF),
            vm((2, 2, half, D), BF),
            vm((SPAN, half, D), BF),
            vm((SPAN, half, D), BF),
            vm((D, 3 * WIDE), F32),
            vm(wq.shape, BF),
            vm(x_in.shape, BF),
            vm(mid.shape, F32),
            vm((2, 2, half, D), BF),
            vm((2, half, D), BF),
            vm(wq.shape, BF),
            vm((D // SPAN, 3 * D), BF),
        ]
        + [vm((SPAN,) + s, BF) for s in big]
        + [vm((SPAN,) + s, BF) for s in big]
        + [vm((2, SPAN) + s, BF) for s in small]
        + [vm((SPAN,) + s, BF) for s in small]
        + [vm((2,) + s, BF) for s in small]
        + [vm((2,) + s, BF) for s in small]
        + [vm(s, BF) for s in small]
        + [vm((held,) + (s if outer > 1 else spare), BF) for s in small]
        + [
            vm((3, SPAN) + sq, BF),
            vm((SPAN,) + sq, BF),
            vm((SPAN,) + sq, BF),
            vm((2,) + sq, BF),
            vm((held, 2) + (sq if outer > 1 else spare), BF),
        ]
        + [
            dma((SPAN,)), dma((SPAN,)), dma((SPAN,)), dma((SPAN,)), dma((SPAN,)), dma((2, 2)), dma((2,)), dma((9,)), dma((2,)),
            dma((count,)), dma((count,)), dma((count,)), dma((count + 1, 3)), dma((count + 1, 3)),
            dma((count + 1, 3)), dma((count + 1, 3)), dma((count + 1, beyond)), dma((count + 1, beyond)),
            dma((count + 2, 3)), dma((count + 2, 3)), dma((count + 2,)), dma((count + 2,)), dma((count + 2,)),
        ]
    )
    return pl.pallas_call(
        functools.partial(backward_kernel, outer),
        out_shape=(
            shape((rows, D), F32),
            shape(gd.shape[1:], BF),
            shape(gu.shape[1:], BF),
            shape(go.shape[1:], BF),
            shape((D // SPAN, 3 * D), BF),
        ),
        in_specs=[anyspace] * 8 + [vmem] + [anyspace] * 4 + [vmem, anyspace],
        out_specs=(anyspace,) * 5,
        scratch_shapes=scratch,
        compiler_params=pltpu.CompilerParams(
            collective_id=1, has_side_effects=True, vmem_limit_bytes=60 << 20
        ),
        name="backward_attention",
    )(dah, xg, wq, q, k, v, ah, tot, starts, gd, gu, go, x_in, gain_one, mid)


def body(layer_input, second_start, gain_attn, w_qkv, w_out, gain_mlp, w_up, w_down, d_output):
    rows = layer_input.shape[0]
    kv_index = lax.axis_index("ka")
    (output, d_middle, dah, gd, gu, go, xg, wq, q, k, v, ah, tot, starts) = forward_call(
        layer_input, second_start, gain_attn, w_qkv, gain_mlp, d_output, w_out, w_up, w_down
    )
    d_input, fd, fu, fo, sum_qkv = backward_call(
        dah, xg, wq, q, k, v, ah, tot, starts, gd, gu, go, layer_input, gain_attn, d_middle
    )
    total_qkv = sum_qkv.astype(F32)
    total_down = fd.astype(F32)
    total_up = fu.astype(F32)
    total_out = fo[: D // SPAN].astype(F32)
    def gain_grad(weight, grad, gain):
        own = lax.dynamic_slice_in_dim(gain, kv_index * (D // SPAN), D // SPAN)
        return jnp.sum(weight.astype(F32) * grad, axis=1) / own

    total_gain_attn = gain_grad(w_qkv, total_qkv, gain_attn)
    total_gain_mlp = gain_grad(w_up, total_up, gain_mlp)
    entry_count = rows * SPAN * lax.axis_size("pb") * D
    rms = jnp.sqrt(fo[D // SPAN, 0:1].astype(F32) / entry_count)
    return (
        output, d_input, total_gain_attn, total_qkv, total_out, total_gain_mlp, total_up, total_down, rms,
    )


def solution(mesh):
    if mesh.shape["ka"] != SPAN or mesh.shape["pb"] % 8:
        raise ValueError("unsupported mesh")
    placed = (
        P(("pb", "ka"), None), P("pb"), P(), P("ka", None), P("ka", None), P(), P("ka", None), P("ka", None),
        P(("pb", "ka"), None),
    )
    return jax.shard_map(
        body,
        mesh=mesh,
        in_specs=placed,
        out_specs=(
            P(("pb", "ka"), None), P(("pb", "ka"), None), P("ka"), P("ka", None), P("ka", None), P("ka"),
            P("ka", None), P("ka", None), P("ka"),
        ),
        check_vma=False,
    )
```
